128 devices in a mesh: tok: 4 (over z), ep: 32 (over y, x, core).
Axes of the slice: x: 4, y: 4, z: 4, core: 2. Of those that a mesh axis runs over, the one named last changes fastest.
Arguments:
- resid: bfloat16 [16384, 2048], P(('tok', 'ep')), may hold values from -6 to 6
- qkv: bfloat16 [16384, 5120], P(('tok', 'ep')), may hold values from -8 to 8
- cache_kv: bfloat16 [128, 4, 64, 256], P('ep', 'tok'), may hold values from -6 to 6
- page_slot: int32 [128], P('ep'), may hold values from 0 to 127, each once
- seg_lengths: int32 [16], replicated, may hold values from 1 to 2048, 16384 in all
- cache_age: int32 [16], replicated, may hold values from 0 to 512, as said below
- w_out: bfloat16 [4096, 2048], P('tok'), may hold values from -0.09375 to 0.09375
- norm_gain: float32 [2048], replicated, may hold values from 0.1 to 1.9
- routes: int32 [16384, 8], P(('tok', 'ep')), may hold values from 0 to 127, all different within a row; in each aligned block of 128 rows (0 to 127, 128 to 255, ...) at most 16 rows name the same one
- route_probs: float32 [16384, 8], P(('tok', 'ep')), may hold values from 0.05 to 1
- w_gate_up: bfloat16 [128, 2048, 1536], P(('tok', 'ep')), may hold values from -0.125 to 0.125
- w_down: bfloat16 [128, 768, 2048], P(('tok', 'ep')), may hold values from -0.21875 to 0.21875
Outputs:
- layer_out: bfloat16 [16384, 2048], P(('tok', 'ep'))
The draws below stay inside these ranges and needn't reach their ends.
Inputs may be any that keep to these rules, and one draw needn't show every extreme that they name: `routes`: in each aligned block of 128 rows (the rows of one shard) no expert is named more than 16 times, a bound that some block reaches. `cache_age`: exactly 5 segments have no cache; some segment has 512 cached positions. `page_slot`: logical page l is page l % 8 of segment l // 8.
All inputs are finite; a program needn't handle non-finite values.
Results may differ from the reference program's by a relative error of at most 0.015.
Values may be sent and summed in bfloat16 or wider, within the bound.
A program may use at most 128 MiB of HBM per device.

```python
import math
import jax
import jax.numpy as jnp
import numpy as np
from jax import lax

D = 2048
FF = 768
HEAD = 128
KV_HEADS = 4
QPG = 8
TOP = 8
TOK_DEV = 128
PAGE = 64
SEG_PAGES = 8
EXPERTS = 128
TOKENS = 16384
CAP = 16
SEGS = 16
SEG_MOST = 2048
CACHE_PAGES = 128


def draw_qkv(key, part):
    key_base = jax.random.fold_in(key, 0)
    q_width = QPG * HEAD
    width = q_width + 2 * HEAD
    base = jax.random.normal(key_base, (TOKENS, KV_HEADS, width), jnp.float32)
    columns = jnp.arange(width)
    base = jnp.clip(base * jnp.where(columns < q_width, 1.5, 1.0)[None, None, :], -8.0, 8.0)
    return base.reshape(TOKENS, KV_HEADS * width).astype(jnp.bfloat16)


def draw_cache_age(key, part):
    key_order, key_age = jax.random.split(key)
    longest = SEG_PAGES * PAGE
    order = jax.random.permutation(key_order, SEGS)
    ages = jax.random.randint(key_age, (SEGS,), longest // 2, longest + 1)
    ages = jnp.where(order == SEGS - 1, longest, ages)
    return jnp.where(order < SEGS // 3, 0, ages).astype(jnp.int32)


def level_of(key, extent, pieces, smallest, largest):
    def one(dim, parts):
        draws = jax.random.uniform(jax.random.fold_in(jax.random.fold_in(key, 6), dim), (parts,), jnp.float32, smallest / len(pieces), largest / len(pieces))
        return jnp.repeat(jnp.exp(draws), extent[dim] // parts).reshape((-1,) + (1,) * (len(extent) - dim - 1))

    gain = one(*pieces[0])
    for cut in pieces[1:]:
        gain = gain * one(*cut)
    return gain


def length_profile(number_of, total, bound, lean):
    portions = [(1 << 20) // math.isqrt(grade ** lean) + 1 for grade in range(2, number_of + 1)]
    spare, holding = total - bound - (number_of - 1), [1] * (number_of - 1)
    while spare > 0:
        free = [i for i in range(number_of - 1) if holding[i] < bound]
        whole, budget = sum([portions[i] for i in free]), spare
        for i in free:
            more = min(bound - holding[i], max(1, budget * portions[i] // whole), spare)
            holding[i] = holding[i] + more
            spare = spare - more
    return np.array([bound] + holding)


def ragged_sizes(key, number_of, total, bound, skew):
    if number_of == 2:
        one = jax.random.randint(key, (), max(1, total - bound), min(bound, total - 1) + 1)
        return jnp.stack([one, total - one])
    lengths = jnp.asarray(length_profile(number_of, total, bound, skew), jnp.int32)
    pairs = (number_of - 1) // 2
    giver, sink = lengths[1:1 + 2 * pairs:2], lengths[2:2 + 2 * pairs:2]
    margin = jnp.minimum(giver - 1, bound - sink)
    shifted = jax.random.randint(jax.random.fold_in(key, 1), (pairs,), 0, 1 << 20) % (margin + 1)
    lengths = lengths.at[1:1 + 2 * pairs:2].set(giver - shifted).at[2:2 + 2 * pairs:2].set(sink + shifted)
    return lengths[jax.random.permutation(jax.random.fold_in(key, 2), number_of)]


def deal_out(stream_key, own, number, rows, amount, top, most, lean):
    order = jax.random.permutation(stream_key, amount)
    heavy_load, ordinary = load_shares(amount, rows * top, most, lean, True), load_shares(amount, rows * top, most, lean, False)
    places = jnp.arange(amount)

    def named(sizes, rotation):
        used = int((sizes > 0).sum())
        fixed = max(1, used // 4)
        moved = fixed + (places - fixed + rotation * (used - fixed)) % max(1, amount - fixed)
        return jnp.zeros((amount,), jnp.int32).at[order[jnp.where(places < fixed, places, moved)]].set(jnp.asarray(sizes, jnp.int32))

    sizes = jnp.where(number % 4 == 0, named(heavy_load, number // 4), named(ordinary, number - number // 4 - 1))
    mixed = jax.random.permutation(jax.random.fold_in(own, 3), amount)
    donor, receiver = mixed[0:amount // 2 * 2:2], mixed[1:amount // 2 * 2:2]
    slack = jnp.minimum(sizes[donor] - 1, most - sizes[receiver]) // 2
    slack = jnp.where((donor == order[0]) | (receiver == order[0]) | (sizes[receiver] == 0), 0, jnp.maximum(slack, 0))
    moved = jax.random.randint(jax.random.fold_in(own, 4), (amount // 2,), 0, 1 << 20) % (slack + 1)
    sizes = sizes.at[donor].add(-moved).at[receiver].add(moved)
    labels = jnp.searchsorted(jnp.cumsum(sizes), jnp.arange(rows * top), side="right").astype(jnp.int32)
    listing = labels.reshape(top, rows).T
    listing = listing[jax.random.permutation(jax.random.fold_in(own, 1), rows)]
    rotation = jax.random.randint(jax.random.fold_in(own, 2), (rows, 1), 0, top)
    return jnp.take_along_axis(listing, (jnp.arange(top)[None, :] + rotation) % top, axis=1)


def load_shares(count, total, most, slope, full):
    weights = [(1 << 20) // math.isqrt(standing ** slope) + 1 for standing in range(1, count + 1)]
    largest = most if full else min(most, max(-(-total // count), total * weights[0] // sum(weights)))
    least = 1 if total - largest >= count - 1 else 0
    counts, spare = [largest] + [least] * (count - 1), total - largest - least * (count - 1)
    while spare > 0:
        free = [i for i in range(1, count) if counts[i] < largest] or [i for i in range(1, count) if counts[i] < most]
        mass, budget = sum([weights[i] for i in free]), spare
        for i in free:
            more = min(most - counts[i], max(1, budget * weights[i] // mass), spare)
            counts[i] = counts[i] + more
            spare = spare - more
    return np.array(counts)


def scatter_about(own_key, extent, spread, limit, pieces=(), kind=jnp.bfloat16):
    gain = level_of(own_key, extent, pieces, -0.22, 0.18) if pieces else 1.0
    values = jax.random.normal(own_key, extent, jnp.float32) * spread * gain
    return jnp.minimum(jnp.maximum(values, -limit), limit).astype(kind)


def setup_inputs(seed: int = 0) -> dict:
    splits = jax.random.split(jax.random.key(seed), 13)
    resid = scatter_about(splits[0], (TOKENS, D), 1.0, 6.0, ((0, 128),))
    qkv = draw_qkv(jax.random.fold_in(splits[12], 71), 0)
    cache_kv = scatter_about(splits[2], (CACHE_PAGES, KV_HEADS, PAGE, 2 * HEAD), 1.0, 6.0, ((0, 32), (1, 4)))
    page_slot = jax.random.permutation(splits[3], CACHE_PAGES).astype(jnp.int32)
    seg_lengths = ragged_sizes(splits[4], SEGS, TOKENS, SEG_MOST, 2).astype(jnp.int32)
    cache_age = draw_cache_age(jax.random.fold_in(splits[12], 71), 0)
    w_out = scatter_about(splits[6], (KV_HEADS * QPG * HEAD, D), (KV_HEADS * QPG * HEAD) ** -0.5, 0.09375, ((0, 4),))
    norm_gain = jnp.clip(1.0 + 0.18 * jax.random.normal(splits[7], (D,), jnp.float32), 0.1, 1.9)
    routes_keys = jax.random.split(jax.random.fold_in(splits[8], 1), TOKENS // TOK_DEV)
    routes_turns = jax.random.permutation(jax.random.fold_in(splits[8], 3), TOKENS // TOK_DEV)
    routes = jax.vmap(lambda own, number: deal_out(jax.random.fold_in(splits[8], 2), own, number, TOK_DEV, EXPERTS, TOP, CAP, 2))(routes_keys, routes_turns).reshape((TOKENS, TOP))
    route_probs = jnp.clip(jnp.exp(math.log(1.0) - 2.9957323 * jax.random.uniform(splits[9], (TOKENS, TOP), jnp.float32) ** level_of(splits[9], (TOKENS, TOP), ((0, 128),), -0.2, 0.2)), 0.05, 1.0)
    w_gate_up = scatter_about(splits[10], (EXPERTS, D, 2 * FF), D ** -0.5, 0.125, ((0, 128),))
    w_down = scatter_about(splits[11], (EXPERTS, FF, D), FF ** -0.5, 0.21875, ((0, 128),))
    return {"resid": resid, "qkv": qkv, "cache_kv": cache_kv, "page_slot": page_slot, "seg_lengths": seg_lengths, "cache_age": cache_age, "w_out": w_out, "norm_gain": norm_gain, "routes": routes, "route_probs": route_probs, "w_gate_up": w_gate_up, "w_down": w_down}


NEG_FILL = -1e+30
NORM_EPS = 1e-06

def segment_meta(tok_rows, seg_lengths, cache_age):
    seg_ends = jnp.cumsum(seg_lengths).astype(jnp.int32)
    seg_starts = (seg_ends - seg_lengths).astype(jnp.int32)
    segment = lax.optimization_barrier(jnp.sum((tok_rows[:, None] >= seg_ends[None, :]).astype(jnp.int32), axis=1)).astype(jnp.int32)
    matched = segment[:, None] == jnp.arange(seg_lengths.shape[0], dtype=jnp.int32)[None, :]
    first_row = lax.optimization_barrier(jnp.sum(jnp.where(matched, seg_starts[None, :], 0), axis=1))
    seg_age = lax.optimization_barrier(jnp.sum(jnp.where(matched, cache_age[None, :], 0), axis=1))
    return (segment, (tok_rows - first_row + seg_age).astype(jnp.int32))

def online_update(states, scores, allowed, value_rows):
    running, denom, summed = states
    scores = jnp.where(allowed, scores, NEG_FILL)
    newest = jnp.maximum(running, lax.optimization_barrier(jnp.max(scores, axis=-1)))
    weights = jnp.where(allowed, jnp.exp(scores - newest[..., None]), 0.0)
    factor = jnp.exp(running - newest)
    denom = denom * factor + lax.optimization_barrier(jnp.sum(weights, axis=-1))
    rounded = lax.optimization_barrier(weights.astype(jnp.bfloat16)).astype(jnp.float32)
    summed = summed * factor[..., None] + jnp.einsum('gtqk,kgd->gtqd', rounded, value_rows.astype(jnp.float32))
    return (newest, denom, summed)

def attention(qkv, cache_kv, page_slot, seg_lengths, cache_age):
    tokens = qkv.shape[0]
    q_width = QPG * HEAD
    scale = 1.0 / math.sqrt(HEAD)
    grouped = qkv.reshape(tokens, KV_HEADS, q_width + 2 * HEAD)
    queries = grouped[:, :, :q_width].reshape(tokens, KV_HEADS, QPG, HEAD)
    key_rows = grouped[:, :, q_width:q_width + HEAD]
    value_rows = grouped[:, :, q_width + HEAD:]
    all_rows = jnp.arange(tokens, dtype=jnp.int32)
    segment, position = segment_meta(all_rows, seg_lengths, cache_age)
    seg_count = seg_lengths.shape[0]
    inverse = jnp.argsort(page_slot).astype(jnp.int32)
    logical = cache_kv[inverse].reshape(seg_count, SEG_PAGES, KV_HEADS, PAGE, 2 * HEAD)
    logical = jnp.transpose(logical, (0, 1, 3, 2, 4)).reshape(seg_count, SEG_PAGES * PAGE, KV_HEADS, 2 * HEAD)
    cache_pos = jnp.arange(SEG_PAGES * PAGE, dtype=jnp.int32)
    query_rows = 256
    window = SEG_MOST + query_rows

    def one_block(block_index):
        first = (block_index * query_rows).astype(jnp.int32)
        query_block = lax.dynamic_slice_in_dim(queries, first, query_rows, 0).astype(jnp.float32)
        q_segment = lax.dynamic_slice_in_dim(segment, first, query_rows, 0)
        q_position = lax.dynamic_slice_in_dim(position, first, query_rows, 0)
        key_first = jnp.clip(first + query_rows - window, 0, tokens - window).astype(jnp.int32)
        key_block = lax.dynamic_slice_in_dim(key_rows, key_first, window, 0).astype(jnp.float32)
        value_block = lax.dynamic_slice_in_dim(value_rows, key_first, window, 0)
        k_segment = lax.dynamic_slice_in_dim(segment, key_first, window, 0)
        k_position = lax.dynamic_slice_in_dim(position, key_first, window, 0)
        allowed = (q_segment[:, None] == k_segment[None, :]) & (k_position[None, :] <= q_position[:, None])
        scores = jnp.einsum('tgqd,kgd->gtqk', query_block, key_block) * scale
        start_state = (jnp.full((KV_HEADS, query_rows, QPG), NEG_FILL, jnp.float32), jnp.zeros((KV_HEADS, query_rows, QPG), jnp.float32), jnp.zeros((KV_HEADS, query_rows, QPG, HEAD), jnp.float32))
        state_now = online_update(start_state, scores, allowed[None, :, None, :], value_block)
        lowest = q_segment[0]
        highest = q_segment[query_rows - 1]

        def visit(current, seg_id):

            def attend(inner):
                cached = logical[seg_id]
                cached_keys = cached[:, :, :HEAD].astype(jnp.float32)
                cached_values = cached[:, :, HEAD:]
                cache_ok = (q_segment[:, None] == seg_id) & (cache_pos[None, :] < cache_age[seg_id])
                cache_scores = jnp.einsum('tgqd,kgd->gtqk', query_block, cached_keys) * scale
                return online_update(inner, cache_scores, cache_ok[None, :, None, :], cached_values)
            nested = lax.cond((seg_id >= lowest) & (seg_id <= highest), attend, lambda inner: inner, current)
            return (nested, None)
        state_now, ignored = lax.scan(visit, state_now, jnp.arange(seg_count, dtype=jnp.int32))
        running, denom, summed = state_now
        result = summed / denom[..., None]
        return jnp.transpose(result, (1, 0, 2, 3)).reshape(query_rows, KV_HEADS * q_width).astype(jnp.bfloat16)
    blocks_out = lax.map(one_block, jnp.arange(tokens // query_rows, dtype=jnp.int32))
    return blocks_out.reshape(tokens, KV_HEADS * q_width)

def experts_ref(normed, routes, shares, w_gate_up, w_down):
    tokens = normed.shape[0]
    flat_route = routes.reshape(-1)
    order = jnp.argsort(flat_route, stable=True).astype(jnp.int32)
    chosen = flat_route[order]
    source = (order // TOP).astype(jnp.int32)
    weights = shares.reshape(-1)[order]
    block_rows = 128
    block_count = flat_route.shape[0] // block_rows
    chosen = chosen.reshape(block_count, block_rows)
    source = source.reshape(block_count, block_rows)
    weights = weights.reshape(block_count, block_rows)

    def visit(totals, blocks):
        expert_ids, source_rows, row_weights = blocks
        inputs = normed[source_rows].astype(jnp.float32)

        def one_expert(expert, result):
            projected = jnp.dot(inputs, w_gate_up[expert].astype(jnp.float32))
            hidden = (jax.nn.silu(projected[:, :FF]) * projected[:, FF:]).astype(jnp.bfloat16)
            hidden = lax.optimization_barrier(hidden).astype(jnp.float32)
            produced = jnp.dot(hidden, w_down[expert].astype(jnp.float32)).astype(jnp.bfloat16)
            return jnp.where((expert_ids == expert)[:, None], produced, result)
        result = lax.fori_loop(expert_ids[0], expert_ids[block_rows - 1] + 1, one_expert, jnp.zeros((block_rows, normed.shape[1]), jnp.bfloat16))
        totals = totals.at[source_rows].add(row_weights[:, None] * result.astype(jnp.float32))
        return (totals, None)
    totals, ignored = lax.scan(visit, jnp.zeros((tokens, normed.shape[1]), jnp.float32), (chosen, source, weights))
    return totals

def reference(resid, qkv, cache_kv, page_slot, seg_lengths, cache_age, w_out, norm_gain, routes, route_probs, w_gate_up, w_down):
    attended = attention(qkv, cache_kv, page_slot, seg_lengths, cache_age)
    projected = jnp.dot(attended, w_out, preferred_element_type=jnp.float32)
    mixed = (resid.astype(jnp.float32) + projected).astype(jnp.bfloat16)
    widened = mixed.astype(jnp.float32)
    normed = (widened * lax.rsqrt(lax.optimization_barrier(jnp.mean(widened * widened, axis=-1, keepdims=True)) + NORM_EPS) * norm_gain[None, :]).astype(jnp.bfloat16)
    shares = route_probs / lax.optimization_barrier(jnp.sum(route_probs, axis=-1, keepdims=True))
    routed = experts_ref(normed, routes, shares, w_gate_up, w_down)
    return (widened + routed).astype(jnp.bfloat16)
```

```python
import functools
import math

import jax
import jax.numpy as jnp
from jax import lax
from jax.experimental import pallas as pl
from jax.experimental.pallas import tpu as pltpu
from jax.sharding import PartitionSpec as P

D = 2048
FF = 768
HEAD = 128
QPG = 8
TOP = 8
PAGE = 64
SEG_PAGES = 8
SEG_MOST = 2048
STEP = 256
META_ROWS = 16


NEG_FILL = -1e30
NORM_EPS = 1e-06


def attention_kernel(tok_dev, segs, most_steps, seg_ref, row_ref, q_ref, bank_ref, out_ref, score_ref, low_ref, top_ref, den_ref, acc_ref):
    rows = tok_dev * QPG
    pages = segs * SEG_PAGES
    rate = math.log2(math.e) / math.sqrt(HEAD)

    def tiled(mask):
        return jnp.concatenate([mask] * QPG, axis=0)

    def one_block(block, carry):
        first = seg_ref[3 * segs + block]
        last = first + tok_dev - 1
        token = first + lax.broadcasted_iota(jnp.int32, (tok_dev, STEP), 0)
        column = lax.broadcasted_iota(jnp.int32, (tok_dev, STEP), 1)
        low = jnp.zeros((tok_dev, STEP), jnp.int32)
        begin = jnp.int32(0)
        for s in range(segs):
            start = seg_ref[s]
            low = jnp.where(token >= start, start, low)
            begin = jnp.where(first >= start, start, begin)
        low_ref[...] = low
        query = jnp.concatenate([q_ref[block, :, h * HEAD:(h + 1) * HEAD] for h in range(QPG)], axis=0)
        den_ref[...] = jnp.zeros_like(den_ref)
        acc_ref[...] = jnp.zeros_like(acc_ref)

        def region(steps, bank_of, mask_of, opening):
            if opening:
                held = jnp.full((rows, HEAD), NEG_FILL, jnp.float32)
            else:
                held = top_ref[...]

            def score(step, running):
                keys = jnp.concatenate([bank_ref[pl.ds(at, size), :HEAD] for at, size in bank_of(step)], axis=0)
                scores = lax.dot_general(query, keys, (((1,), (1,)), ((), ())), preferred_element_type=jnp.float32) * rate
                scores = jnp.where(tiled(mask_of(step)), scores, NEG_FILL)
                score_ref[step] = scores
                return jnp.maximum(running, jnp.maximum(scores[:, :HEAD], scores[:, HEAD:]))

            newest = lax.fori_loop(0, steps, score, held)
            newest = jnp.broadcast_to(jnp.max(newest, axis=1, keepdims=True), (rows, HEAD))
            if not opening:
                factor = jnp.exp2(held - newest)
                den_ref[...] = den_ref[...] * factor
                acc_ref[...] = acc_ref[...] * factor
            top_ref[...] = newest

            def weigh(step, ignored):
                top = top_ref[...]
                weights = jnp.exp2(score_ref[step] - jnp.concatenate([top, top], axis=1))
                den_ref[...] += weights[:, :HEAD] + weights[:, HEAD:]
                values = jnp.concatenate([bank_ref[pl.ds(at, size), HEAD:] for at, size in bank_of(step)], axis=0)
                acc_ref[...] += jnp.dot(weights.astype(jnp.bfloat16), values, preferred_element_type=jnp.float32)
                return ignored

            lax.fori_loop(0, steps, weigh, 0)

        chunk_last = first // tok_dev
        chunk_first = begin // tok_dev
        steps = (chunk_last - chunk_first + 2) // 2

        def new_chunk(step, half):
            return chunk_last - 2 * step - 1 + half

        def new_bank(step):
            return [(pl.multiple_of(row_ref[pages + jnp.maximum(new_chunk(step, half), 0)], 16), tok_dev) for half in range(2)]

        def new_mask(step):
            key = new_chunk(step, 0) * tok_dev + column
            return (key >= low_ref[...]) & (key <= token)

        region(steps, new_bank, new_mask, True)

        def cached(s, ignored):
            start, end, age = seg_ref[s], seg_ref[segs + s], seg_ref[2 * segs + s]

            @pl.when((start <= last) & (end > first) & (age > 0))
            def _():
                def page_bank(step):
                    return [(pl.multiple_of(row_ref[s * SEG_PAGES + step * (STEP // PAGE) + part], 16), PAGE) for part in range(STEP // PAGE)]

                def page_mask(step):
                    return (token >= start) & (token < end) & (step * STEP + column < age)

                region((age + STEP - 1) // STEP, page_bank, page_mask, False)
            return ignored

        lax.fori_loop(0, segs, cached, 0)
        total = jnp.sum(den_ref[...], axis=1, keepdims=True)
        result = (acc_ref[...] / total).astype(jnp.bfloat16)
        for h in range(QPG):
            out_ref[block, :, h * HEAD:(h + 1) * HEAD] = result[h * tok_dev:(h + 1) * tok_dev]
        return carry

    lax.fori_loop(0, q_ref.shape[0], one_block, 0)


def attention(seg_table, row_table, queries, bank, segs, seg_most):
    blocks, tok_dev, width = queries.shape
    most_steps = max((seg_most + tok_dev) // tok_dev // 2 + 1, SEG_PAGES * PAGE // STEP)
    rows = tok_dev * QPG
    return pl.pallas_call(
        functools.partial(attention_kernel, tok_dev, segs, most_steps),
        out_shape=jax.ShapeDtypeStruct(queries.shape, jnp.bfloat16),
        in_specs=[pl.BlockSpec(memory_space=pltpu.SMEM)] * 2 + [pl.BlockSpec(memory_space=pltpu.VMEM)] * 2,
        out_specs=pl.BlockSpec(memory_space=pltpu.VMEM),
        scratch_shapes=[
            pltpu.VMEM((most_steps, rows, STEP), jnp.float32),
            pltpu.VMEM((tok_dev, STEP), jnp.int32),
            pltpu.VMEM((rows, HEAD), jnp.float32),
            pltpu.VMEM((rows, HEAD), jnp.float32),
            pltpu.VMEM((rows, HEAD), jnp.float32),
        ],
        compiler_params=pltpu.CompilerParams(vmem_limit_bytes=48 << 20),
        name="attend",
    )(seg_table, row_table, queries, bank)


def expert_rows(arrived, w_gate_up, w_down):
    shaped = arrived.shape
    flat_rows = arrived.reshape(-1, shaped[-1])
    projected = jnp.dot(flat_rows, w_gate_up[0], preferred_element_type=jnp.float32)
    hidden = (jax.nn.silu(projected[:, :FF]) * projected[:, FF:]).astype(jnp.bfloat16)
    produced = jnp.dot(hidden, w_down[0], preferred_element_type=jnp.float32).astype(jnp.bfloat16)
    return produced.reshape(shaped)


def on_device(
    resid,
    qkv,
    cache_kv,
    page_slot,
    seg_lengths,
    cache_age,
    w_out,
    norm_gain,
    routes,
    route_probs,
    w_gate_up,
    w_down,
):
    tok_groups = lax.axis_size("tok")
    ep_count = lax.axis_size("ep")
    member = lax.axis_index("ep")
    tok_dev = resid.shape[0]
    q_width = QPG * HEAD
    grouped = lax.all_to_all(qkv, "tok", split_axis=1, concat_axis=0, tiled=True)
    queries = grouped[:, :q_width]
    own_keys = grouped[:, q_width:]
    seg_count = seg_lengths.shape[0]
    page_count = cache_kv.shape[0]
    cached_rows = cache_kv.reshape(page_count * PAGE, 2 * HEAD)
    slots = jnp.broadcast_to(
        jnp.pad(page_slot, (0, 2 * HEAD - page_count))[None, :], (META_ROWS, 2 * HEAD)
    ).astype(jnp.bfloat16)
    own_bank = jnp.concatenate([own_keys, cached_rows, slots], axis=0)
    bank_rows = own_bank.shape[0]
    bank = lax.all_gather(own_bank, "ep", axis=0, tiled=True)
    held = bank.reshape(ep_count, bank_rows, 2 * HEAD)[:, bank_rows - 1, :page_count].astype(jnp.int32)
    first_cached = tok_groups * tok_dev
    slot_row = (
        jnp.arange(ep_count, dtype=jnp.int32)[:, None] * bank_rows
        + first_cached
        + jnp.arange(page_count, dtype=jnp.int32)[None, :] * PAGE
    )
    pages = seg_count * SEG_PAGES
    page_match = held.reshape(-1)[None, :] == jnp.arange(pages, dtype=jnp.int32)[:, None]
    page_row = jnp.sum(jnp.where(page_match, slot_row.reshape(-1)[None, :], 0), axis=1)
    chunk = jnp.arange(tok_groups * ep_count, dtype=jnp.int32)
    chunk_row = chunk % ep_count * bank_rows + chunk // ep_count * tok_dev
    row_table = jnp.concatenate([page_row, chunk_row]).astype(jnp.int32)
    seg_ends = jnp.cumsum(seg_lengths)
    first_tokens = (jnp.arange(tok_groups, dtype=jnp.int32) * ep_count + member) * tok_dev
    seg_table = jnp.concatenate([seg_ends - seg_lengths, seg_ends, cache_age, first_tokens]).astype(jnp.int32)
    attended = attention(
        seg_table, row_table, queries.reshape(tok_groups, tok_dev, q_width), bank, seg_count, SEG_MOST
    ).reshape(tok_groups * tok_dev, q_width)
    attn_sum = lax.psum_scatter(
        jnp.dot(attended, w_out, preferred_element_type=jnp.float32).astype(jnp.bfloat16),
        "tok",
        scatter_dimension=0,
        tiled=True,
    ).astype(jnp.float32)
    mixed = (resid.astype(jnp.float32) + attn_sum).astype(jnp.bfloat16)
    widened_mix = mixed.astype(jnp.float32)
    normed = (
        widened_mix
        * lax.rsqrt(jnp.mean(widened_mix * widened_mix, axis=-1, keepdims=True) + NORM_EPS)
        * norm_gain[None, :]
    ).astype(jnp.bfloat16)
    expert_count = tok_groups * ep_count
    capacity = max(2, 2 * tok_dev * TOP // expert_count)
    flat_route = routes.reshape(-1)
    one_hot = (flat_route[:, None] == jnp.arange(expert_count, dtype=jnp.int32)[None, :]).astype(
        jnp.int32
    )
    earlier = jnp.cumsum(one_hot, axis=0) - one_hot
    slot_rank = jnp.sum(earlier * one_hot, axis=1)
    slot_index = flat_route * capacity + slot_rank
    source_row = (
        jnp.full((expert_count * capacity,), tok_dev, jnp.int32)
        .at[slot_index]
        .set(jnp.arange(tok_dev * TOP, dtype=jnp.int32) // TOP)
    )
    padded = jnp.concatenate([normed, jnp.zeros((1, D), jnp.bfloat16)], axis=0)
    outgoing = padded[source_row].reshape(expert_count, capacity, D)
    returned = lax.all_to_all(
        expert_rows(
            lax.all_to_all(outgoing, ("tok", "ep"), split_axis=0, concat_axis=0, tiled=True),
            w_gate_up,
            w_down,
        ),
        ("tok", "ep"),
        split_axis=0,
        concat_axis=0,
        tiled=True,
    ).reshape(expert_count * capacity, D)
    picked = returned[slot_index].reshape(tok_dev, TOP, D)
    shares = route_probs / jnp.sum(route_probs, axis=1, keepdims=True)
    routed = jnp.einsum("tk,tkd->td", shares, picked, preferred_element_type=jnp.float32)
    return (widened_mix + routed).astype(jnp.bfloat16)


def solution(mesh):
    placed = (
        P(("tok", "ep"), None),
        P(("tok", "ep"), None),
        P("ep", "tok", None, None),
        P("ep"),
        P(),
        P(),
        P("tok", None),
        P(),
        P(("tok", "ep"), None),
        P(("tok", "ep"), None),
        P(("tok", "ep"), None, None),
        P(("tok", "ep"), None, None),
    )
    return jax.shard_map(
        on_device, mesh=mesh, in_specs=placed, out_specs=P(("tok", "ep"), None), check_vma=False
    )
```

```python
import functools
import math

import jax
import jax.numpy as jnp
from jax import lax
from jax.experimental import pallas as pl
from jax.experimental.pallas import tpu as pltpu
from jax.sharding import PartitionSpec as P

D = 2048
FF = 768
HEAD = 128
QPG = 8
TOP = 8
PAGE = 64
SEG_PAGES = 8
SEG_MOST = 2048
STEP = 256
META_ROWS = 16


NEG_FILL = -1e30
NORM_EPS = 1e-06


def attention_kernel(tok_dev, segs, most_steps, seg_ref, row_ref, q_ref, bank_ref, out_ref, score_ref, low_ref, top_ref, den_ref, acc_ref):
    rows = tok_dev * QPG
    pages = segs * SEG_PAGES
    rate = math.log2(math.e) / math.sqrt(HEAD)

    def tiled(mask):
        return jnp.concatenate([mask] * QPG, axis=0)

    def one_block(block, carry):
        first = seg_ref[3 * segs + block]
        last = first + tok_dev - 1
        token = first + lax.broadcasted_iota(jnp.int32, (tok_dev, STEP), 0)
        column = lax.broadcasted_iota(jnp.int32, (tok_dev, STEP), 1)
        low = jnp.zeros((tok_dev, STEP), jnp.int32)
        begin = jnp.int32(0)
        for s in range(segs):
            start = seg_ref[s]
            low = jnp.where(token >= start, start, low)
            begin = jnp.where(first >= start, start, begin)
        low_ref[...] = low
        query = jnp.concatenate([q_ref[block, :, h * HEAD:(h + 1) * HEAD] for h in range(QPG)], axis=0)
        den_ref[...] = jnp.zeros_like(den_ref)
        acc_ref[...] = jnp.zeros_like(acc_ref)

        def region(steps, bank_of, mask_of, opening):
            if opening:
                held = jnp.full((rows, HEAD), NEG_FILL, jnp.float32)
            else:
                held = top_ref[...]

            def score(step, running):
                keys = jnp.concatenate([bank_ref[pl.ds(at, size), :HEAD] for at, size in bank_of(step)], axis=0)
                scores = lax.dot_general(query, keys, (((1,), (1,)), ((), ())), preferred_element_type=jnp.float32) * rate
                scores = jnp.where(tiled(mask_of(step)), scores, NEG_FILL)
                score_ref[step] = scores
                return jnp.maximum(running, jnp.maximum(scores[:, :HEAD], scores[:, HEAD:]))

            newest = lax.fori_loop(0, steps, score, held)
            newest = jnp.broadcast_to(jnp.max(newest, axis=1, keepdims=True), (rows, HEAD))
            if not opening:
                factor = jnp.exp2(held - newest)
                den_ref[...] = den_ref[...] * factor
                acc_ref[...] = acc_ref[...] * factor
            top_ref[...] = newest

            def weigh(step, ignored):
                top = top_ref[...]
                weights = jnp.exp2(score_ref[step] - jnp.concatenate([top, top], axis=1))
                den_ref[...] += weights[:, :HEAD] + weights[:, HEAD:]
                values = jnp.concatenate([bank_ref[pl.ds(at, size), HEAD:] for at, size in bank_of(step)], axis=0)
                acc_ref[...] += jnp.dot(weights.astype(jnp.bfloat16), values, preferred_element_type=jnp.float32)
                return ignored

            lax.fori_loop(0, steps, weigh, 0)

        chunk_last = first // tok_dev
        chunk_first = begin // tok_dev
        steps = (chunk_last - chunk_first + 2) // 2

        def new_chunk(step, half):
            return chunk_last - 2 * step - 1 + half

        def new_bank(step):
            return [(pl.multiple_of(row_ref[pages + jnp.maximum(new_chunk(step, half), 0)], 16), tok_dev) for half in range(2)]

        def new_mask(step):
            key = new_chunk(step, 0) * tok_dev + column
            return (key >= low_ref[...]) & (key <= token)

        region(steps, new_bank, new_mask, True)

        def cached(s, ignored):
            start, end, age = seg_ref[s], seg_ref[segs + s], seg_ref[2 * segs + s]

            @pl.when((start <= last) & (end > first) & (age > 0))
            def _():
                def page_bank(step):
                    return [(pl.multiple_of(row_ref[s * SEG_PAGES + step * (STEP // PAGE) + part], 16), PAGE) for part in range(STEP // PAGE)]

                def page_mask(step):
                    return (token >= start) & (token < end) & (step * STEP + column < age)

                region((age + STEP - 1) // STEP, page_bank, page_mask, False)
            return ignored

        lax.fori_loop(0, segs, cached, 0)
        total = jnp.sum(den_ref[...], axis=1, keepdims=True)
        result = (acc_ref[...] / total).astype(jnp.bfloat16)
        for h in range(QPG):
            out_ref[block, :, h * HEAD:(h + 1) * HEAD] = result[h * tok_dev:(h + 1) * tok_dev]
        return carry

    lax.fori_loop(0, q_ref.shape[0], one_block, 0)


def attention(seg_table, row_table, queries, bank, segs, seg_most):
    blocks, tok_dev, width = queries.shape
    most_steps = max((seg_most + tok_dev) // tok_dev // 2 + 1, SEG_PAGES * PAGE // STEP)
    rows = tok_dev * QPG
    return pl.pallas_call(
        functools.partial(attention_kernel, tok_dev, segs, most_steps),
        out_shape=jax.ShapeDtypeStruct(queries.shape, jnp.bfloat16),
        in_specs=[pl.BlockSpec(memory_space=pltpu.SMEM)] * 2 + [pl.BlockSpec(memory_space=pltpu.VMEM)] * 2,
        out_specs=pl.BlockSpec(memory_space=pltpu.VMEM),
        scratch_shapes=[
            pltpu.VMEM((most_steps, rows, STEP), jnp.float32),
            pltpu.VMEM((tok_dev, STEP), jnp.int32),
            pltpu.VMEM((rows, HEAD), jnp.float32),
            pltpu.VMEM((rows, HEAD), jnp.float32),
            pltpu.VMEM((rows, HEAD), jnp.float32),
        ],
        compiler_params=pltpu.CompilerParams(vmem_limit_bytes=48 << 20),
        name="attend",
    )(seg_table, row_table, queries, bank)


MESH = pl.DeviceIdType.MESH
CAP = 16
GROUP = 16
MIX = 37

def hop(dims, step, way):
    deep, tall, wide, cores = dims
    total = deep * tall * wide * cores
    offset = lax.rem(step * MIX, total)
    tok, ep = lax.axis_index("tok"), lax.axis_index("ep")
    sizes = (deep, tall, wide, cores)
    mine = (tok, lax.div(ep, wide * cores), lax.rem(lax.div(ep, cores), wide), lax.rem(ep, cores))
    strides = (tall * wide * cores, wide * cores, cores, 1)
    at = [
        lax.rem(own + size + way * lax.rem(lax.div(offset, stride), size), size)
        for own, size, stride in zip(mine, sizes, strides)
    ]
    place = (at[1] * wide + at[2]) * cores + at[3]
    return (at[0], place), at[0] * (tall * wide * cores) + place


def routed_kernel(
    dims, normed_ref, mixed_ref, routes_ref, probs_ref, gate_up_hbm, down_hbm, out_ref,
    stage, arrived, back, gate_up, down, rank, share, pick, total,
    weight_sems, send_sems, recv_sems, back_send_sems, back_recv_sems,
):
    devices = dims[0] * dims[1] * dims[2] * dims[3]
    chunks = devices // GROUP
    rows = GROUP * CAP
    tokens = normed_ref.shape[0]
    hidden_width = down.shape[0]
    load_gate_up = pltpu.make_async_copy(gate_up_hbm.at[0], gate_up, weight_sems.at[0])
    load_down = pltpu.make_async_copy(down_hbm.at[0], down, weight_sems.at[1])
    load_gate_up.start()
    load_down.start()

    barrier = pltpu.get_barrier_semaphore()

    def greet(step, ignored):
        pl.semaphore_signal(barrier, inc=1, device_id=hop(dims, step, 1)[0], device_id_type=MESH)
        return ignored

    lax.fori_loop(1, devices, greet, 0)

    experts = lax.broadcasted_iota(jnp.int32, (devices, tokens), 0)
    probs = probs_ref[...]
    shares = probs / jnp.sum(probs, axis=0, keepdims=True)
    named = jnp.zeros((devices, tokens), jnp.float32)
    owed = jnp.zeros((devices, tokens), jnp.float32)
    for k in range(routes_ref.shape[0]):
        match = experts == routes_ref[k : k + 1, :]
        named = jnp.where(match, 1.0, named)
        owed = jnp.where(match, shares[k : k + 1, :], owed)
    before = (
        lax.broadcasted_iota(jnp.int32, (tokens, tokens), 0) < lax.broadcasted_iota(jnp.int32, (tokens, tokens), 1)
    ).astype(jnp.bfloat16)
    earlier = jnp.dot(named.astype(jnp.bfloat16), before, preferred_element_type=jnp.float32)
    rank[...] = jnp.where(named > 0.0, earlier, -1.0)
    share[...] = owed
    slot = lax.broadcasted_iota(jnp.int32, (CAP, tokens), 0).astype(jnp.float32)

    def slab(ref, step):
        return ref.at[pl.ds(pl.multiple_of(step * CAP, CAP), CAP)]

    def block(ref, chunk):
        return ref.at[pl.ds(pl.multiple_of(chunk * rows, rows), rows)]

    pl.semaphore_wait(barrier, devices - 1)

    def dispatch(chunk, ignored):
        def choose(j, inner):
            expert = hop(dims, chunk * GROUP + j, 1)[1]
            pick[pl.ds(pl.multiple_of(j * CAP, CAP), CAP), :] = jnp.where(
                rank[pl.ds(expert, 1), :] == slot, 1.0, 0.0
            ).astype(jnp.bfloat16)
            return inner

        lax.fori_loop(0, GROUP, choose, 0)
        block(stage, chunk)[...] = jnp.dot(
            pick[...], normed_ref[...], preferred_element_type=jnp.float32
        ).astype(jnp.bfloat16)

        def send(j, inner):
            step = chunk * GROUP + j

            @pl.when(step > 0)
            def _():
                pltpu.make_async_remote_copy(
                    src_ref=slab(stage, step), dst_ref=slab(arrived, step),
                    send_sem=send_sems.at[chunk], recv_sem=recv_sems.at[chunk],
                    device_id=hop(dims, step, 1)[0], device_id_type=MESH,
                ).start()

            @pl.when(step == 0)
            def _():
                pltpu.make_async_copy(slab(stage, step), slab(arrived, step), recv_sems.at[chunk]).start()

            return inner

        return lax.fori_loop(0, GROUP, send, ignored)

    lax.fori_loop(0, chunks, dispatch, 0)
    load_gate_up.wait()
    load_down.wait()

    def work(chunk, ignored):
        pltpu.make_async_copy(block(arrived, chunk), block(arrived, chunk), recv_sems.at[chunk]).wait()
        came = block(arrived, chunk)[...]
        gate = jnp.dot(came, gate_up[:, :hidden_width], preferred_element_type=jnp.float32)
        up = jnp.dot(came, gate_up[:, hidden_width:], preferred_element_type=jnp.float32)
        hidden = (gate * jax.nn.sigmoid(gate) * up).astype(jnp.bfloat16)
        block(arrived, chunk)[...] = jnp.dot(hidden, down[...], preferred_element_type=jnp.float32).astype(jnp.bfloat16)

        def give_back(j, inner):
            step = chunk * GROUP + j

            @pl.when(step > 0)
            def _():
                pltpu.make_async_remote_copy(
                    src_ref=slab(arrived, step), dst_ref=slab(back, step),
                    send_sem=back_send_sems.at[chunk], recv_sem=back_recv_sems.at[chunk],
                    device_id=hop(dims, step, -1)[0], device_id_type=MESH,
                ).start()

            @pl.when(step == 0)
            def _():
                pltpu.make_async_copy(slab(arrived, step), slab(back, step), back_recv_sems.at[chunk]).start()

            return inner

        return lax.fori_loop(0, GROUP, give_back, ignored)

    lax.fori_loop(0, chunks, work, 0)
    total[...] = mixed_ref[...].astype(jnp.float32)

    def combine(chunk, ignored):
        def owe(j, inner):
            expert = hop(dims, chunk * GROUP + j, 1)[1]
            pick[pl.ds(pl.multiple_of(j * CAP, CAP), CAP), :] = jnp.where(
                rank[pl.ds(expert, 1), :] == slot, share[pl.ds(expert, 1), :], 0.0
            ).astype(jnp.bfloat16)
            return inner

        lax.fori_loop(0, GROUP, owe, 0)
        pltpu.make_async_copy(block(back, chunk), block(back, chunk), back_recv_sems.at[chunk]).wait()
        total[...] += lax.dot_general(
            pick[...], block(back, chunk)[...], (((0,), (0,)), ((), ())), preferred_element_type=jnp.float32
        )
        return ignored

    lax.fori_loop(0, chunks, combine, 0)
    out_ref[...] = total[...].astype(jnp.bfloat16)

    own = CAP
    first = pl.ds(own, rows - own)
    pltpu.make_async_copy(stage.at[first], stage.at[first], send_sems.at[0]).wait()
    pltpu.make_async_copy(stage.at[first], stage.at[first], back_send_sems.at[0]).wait()

    def settle(chunk, ignored):
        pltpu.make_async_copy(block(stage, chunk), block(stage, chunk), send_sems.at[chunk]).wait()
        pltpu.make_async_copy(block(stage, chunk), block(stage, chunk), back_send_sems.at[chunk]).wait()
        return ignored

    lax.fori_loop(1, chunks, settle, 0)


def routed_experts(dims, normed, mixed, routes, probs, gate_up, down):
    devices = dims[0] * dims[1] * dims[2] * dims[3]
    chunks = devices // GROUP
    tokens, width = normed.shape
    slots = devices * CAP
    vmem = pl.BlockSpec(memory_space=pltpu.VMEM)
    kept = pl.BlockSpec(memory_space=pl.ANY)
    flops = 2 * slots * width * (down.shape[1] * 3 + 2 * tokens)
    return pl.pallas_call(
        functools.partial(routed_kernel, dims),
        out_shape=jax.ShapeDtypeStruct(mixed.shape, jnp.bfloat16),
        in_specs=[vmem] * 4 + [kept] * 2,
        out_specs=vmem,
        scratch_shapes=[
            pltpu.VMEM((slots, width), jnp.bfloat16),
            pltpu.VMEM((slots, width), jnp.bfloat16),
            pltpu.VMEM((slots, width), jnp.bfloat16),
            pltpu.VMEM(gate_up.shape[1:], jnp.bfloat16),
            pltpu.VMEM(down.shape[1:], jnp.bfloat16),
            pltpu.VMEM((devices, tokens), jnp.float32),
            pltpu.VMEM((devices, tokens), jnp.float32),
            pltpu.VMEM((GROUP * CAP, tokens), jnp.bfloat16),
            pltpu.VMEM((tokens, width), jnp.float32),
            pltpu.SemaphoreType.DMA((2,)),
            pltpu.SemaphoreType.DMA((chunks,)),
            pltpu.SemaphoreType.DMA((chunks,)),
            pltpu.SemaphoreType.DMA((chunks,)),
            pltpu.SemaphoreType.DMA((chunks,)),
        ],
        compiler_params=pltpu.CompilerParams(collective_id=0, has_side_effects=True, vmem_limit_bytes=56 << 20),
        cost_estimate=pl.CostEstimate(flops=flops, bytes_accessed=6 * slots * width * 2, transcendentals=0),
        name="routed_experts",
    )(normed, mixed, routes.T, probs.T, gate_up, down)


def on_device(
    resid,
    qkv,
    cache_kv,
    page_slot,
    seg_lengths,
    cache_age,
    w_out,
    norm_gain,
    routes,
    route_probs,
    w_gate_up,
    w_down,
):
    tok_groups = lax.axis_size("tok")
    ep_count = lax.axis_size("ep")
    member = lax.axis_index("ep")
    tok_dev = resid.shape[0]
    q_width = QPG * HEAD
    grouped = lax.all_to_all(qkv, "tok", split_axis=1, concat_axis=0, tiled=True)
    queries = grouped[:, :q_width]
    own_keys = grouped[:, q_width:]
    seg_count = seg_lengths.shape[0]
    page_count = cache_kv.shape[0]
    cached_rows = cache_kv.reshape(page_count * PAGE, 2 * HEAD)
    slots = jnp.broadcast_to(
        jnp.pad(page_slot, (0, 2 * HEAD - page_count))[None, :], (META_ROWS, 2 * HEAD)
    ).astype(jnp.bfloat16)
    own_bank = jnp.concatenate([own_keys, cached_rows, slots], axis=0)
    bank_rows = own_bank.shape[0]
    bank = lax.all_gather(own_bank, "ep", axis=0, tiled=True)
    held = bank.reshape(ep_count, bank_rows, 2 * HEAD)[:, bank_rows - 1, :page_count].astype(jnp.int32)
    first_cached = tok_groups * tok_dev
    slot_row = (
        jnp.arange(ep_count, dtype=jnp.int32)[:, None] * bank_rows
        + first_cached
        + jnp.arange(page_count, dtype=jnp.int32)[None, :] * PAGE
    )
    pages = seg_count * SEG_PAGES
    page_match = held.reshape(-1)[None, :] == jnp.arange(pages, dtype=jnp.int32)[:, None]
    page_row = jnp.sum(jnp.where(page_match, slot_row.reshape(-1)[None, :], 0), axis=1)
    chunk = jnp.arange(tok_groups * ep_count, dtype=jnp.int32)
    chunk_row = chunk % ep_count * bank_rows + chunk // ep_count * tok_dev
    row_table = jnp.concatenate([page_row, chunk_row]).astype(jnp.int32)
    seg_ends = jnp.cumsum(seg_lengths)
    first_tokens = (jnp.arange(tok_groups, dtype=jnp.int32) * ep_count + member) * tok_dev
    seg_table = jnp.concatenate([seg_ends - seg_lengths, seg_ends, cache_age, first_tokens]).astype(jnp.int32)
    attended = attention(
        seg_table, row_table, queries.reshape(tok_groups, tok_dev, q_width), bank, seg_count, SEG_MOST
    ).reshape(tok_groups * tok_dev, q_width)
    attn_sum = lax.psum_scatter(
        jnp.dot(attended, w_out, preferred_element_type=jnp.float32).astype(jnp.bfloat16),
        "tok",
        scatter_dimension=0,
        tiled=True,
    ).astype(jnp.float32)
    mixed = (resid.astype(jnp.float32) + attn_sum).astype(jnp.bfloat16)
    widened_mix = mixed.astype(jnp.float32)
    normed = (
        widened_mix
        * lax.rsqrt(jnp.mean(widened_mix * widened_mix, axis=-1, keepdims=True) + NORM_EPS)
        * norm_gain[None, :]
    ).astype(jnp.bfloat16)
    dims = (tok_groups, ep_count // 8, 4, 2)
    return routed_experts(dims, normed, mixed, routes, route_probs, w_gate_up, w_down)


def solution(mesh):
    placed = (
        P(("tok", "ep"), None),
        P(("tok", "ep"), None),
        P("ep", "tok", None, None),
        P("ep"),
        P(),
        P(),
        P("tok", None),
        P(),
        P(("tok", "ep"), None),
        P(("tok", "ep"), None),
        P(("tok", "ep"), None, None),
        P(("tok", "ep"), None, None),
    )
    return jax.shard_map(
        on_device, mesh=mesh, in_specs=placed, out_specs=P(("tok", "ep"), None), check_vma=False
    )
```

```python
import functools
import math

import jax
import jax.numpy as jnp
from jax import lax
from jax.experimental import pallas as pl
from jax.experimental.pallas import tpu as pltpu
from jax.sharding import PartitionSpec as P

D = 2048
FF = 768
HEAD = 128
QPG = 8
TOP = 8
PAGE = 64
SEG_PAGES = 8
SEG_MOST = 2048
STEP = 256
META_ROWS = 16


NEG_FILL = -1e30
NORM_EPS = 1e-06


def attention_kernel(tok_dev, segs, most_steps, seg_ref, row_ref, q_ref, window_ref, bank_ref, out_ref, score_ref, low_ref, top_ref, den_ref, acc_ref):
    rows = tok_dev * QPG
    held_chunks = window_ref.shape[0] // tok_dev
    opening_chunk = seg_ref[3 * segs] // tok_dev - (held_chunks - q_ref.shape[0])
    rate = math.log2(math.e) / math.sqrt(HEAD)

    def tiled(mask):
        return jnp.concatenate([mask] * QPG, axis=0)

    def one_block(block, carry):
        first = seg_ref[3 * segs + block]
        last = first + tok_dev - 1
        token = first + lax.broadcasted_iota(jnp.int32, (tok_dev, STEP), 0)
        column = lax.broadcasted_iota(jnp.int32, (tok_dev, STEP), 1)
        low = jnp.zeros((tok_dev, STEP), jnp.int32)
        begin = jnp.int32(0)
        for s in range(segs):
            start = seg_ref[s]
            low = jnp.where(token >= start, start, low)
            begin = jnp.where(first >= start, start, begin)
        low_ref[...] = low
        query = jnp.concatenate([q_ref[block, :, h * HEAD:(h + 1) * HEAD] for h in range(QPG)], axis=0)
        den_ref[...] = jnp.zeros_like(den_ref)
        acc_ref[...] = jnp.zeros_like(acc_ref)

        def region(bank, steps, bank_of, mask_of, opening):
            if opening:
                held = jnp.full((rows, HEAD), NEG_FILL, jnp.float32)
            else:
                held = top_ref[...]

            def score(step, running):
                keys = jnp.concatenate([bank[pl.ds(at, size), :HEAD] for at, size in bank_of(step)], axis=0)
                scores = lax.dot_general(query, keys, (((1,), (1,)), ((), ())), preferred_element_type=jnp.float32) * rate
                scores = jnp.where(tiled(mask_of(step)), scores, NEG_FILL)
                score_ref[step] = scores
                return jnp.maximum(running, jnp.maximum(scores[:, :HEAD], scores[:, HEAD:]))

            newest = lax.fori_loop(0, steps, score, held)
            newest = jnp.broadcast_to(jnp.max(newest, axis=1, keepdims=True), (rows, HEAD))
            if not opening:
                factor = jnp.exp2(held - newest)
                den_ref[...] = den_ref[...] * factor
                acc_ref[...] = acc_ref[...] * factor
            top_ref[...] = newest

            def weigh(step, ignored):
                top = top_ref[...]
                weights = jnp.exp2(score_ref[step] - jnp.concatenate([top, top], axis=1))
                den_ref[...] += weights[:, :HEAD] + weights[:, HEAD:]
                values = jnp.concatenate([bank[pl.ds(at, size), HEAD:] for at, size in bank_of(step)], axis=0)
                acc_ref[...] += jnp.dot(weights.astype(jnp.bfloat16), values, preferred_element_type=jnp.float32)
                return ignored

            lax.fori_loop(0, steps, weigh, 0)

        chunk_last = first // tok_dev
        chunk_first = begin // tok_dev
        steps = (chunk_last - chunk_first + 2) // 2

        def new_chunk(step, half):
            return chunk_last - 2 * step - 1 + half

        def new_bank(step):
            return [
                (pl.multiple_of(jnp.clip(new_chunk(step, half) - opening_chunk, 0, held_chunks - 1) * tok_dev, tok_dev), tok_dev)
                for half in range(2)
            ]

        def new_mask(step):
            key = new_chunk(step, 0) * tok_dev + column
            return (key >= low_ref[...]) & (key <= token)

        region(window_ref, steps, new_bank, new_mask, True)

        def cached(s, ignored):
            start, end, age = seg_ref[s], seg_ref[segs + s], seg_ref[2 * segs + s]

            @pl.when((start <= last) & (end > first) & (age > 0))
            def _():
                def page_bank(step):
                    return [(pl.multiple_of(row_ref[s * SEG_PAGES + step * (STEP // PAGE) + part], 16), PAGE) for part in range(STEP // PAGE)]

                def page_mask(step):
                    return (token >= start) & (token < end) & (step * STEP + column < age)

                region(bank_ref, (age + STEP - 1) // STEP, page_bank, page_mask, False)
            return ignored

        lax.fori_loop(0, segs, cached, 0)
        total = jnp.sum(den_ref[...], axis=1, keepdims=True)
        result = (acc_ref[...] / total).astype(jnp.bfloat16)
        for h in range(QPG):
            out_ref[block, :, h * HEAD:(h + 1) * HEAD] = result[h * tok_dev:(h + 1) * tok_dev]
        return carry

    lax.fori_loop(0, q_ref.shape[0], one_block, 0)


def attention(seg_table, row_table, queries, window, bank, segs, seg_most):
    blocks, tok_dev, width = queries.shape
    most_steps = max((seg_most + tok_dev) // tok_dev // 2 + 1, SEG_PAGES * PAGE // STEP)
    rows = tok_dev * QPG
    return pl.pallas_call(
        functools.partial(attention_kernel, tok_dev, segs, most_steps),
        out_shape=jax.ShapeDtypeStruct(queries.shape, jnp.bfloat16),
        in_specs=[pl.BlockSpec(memory_space=pltpu.SMEM)] * 2 + [pl.BlockSpec(memory_space=pltpu.VMEM)] * 3,
        out_specs=pl.BlockSpec(memory_space=pltpu.VMEM),
        scratch_shapes=[
            pltpu.VMEM((most_steps, rows, STEP), jnp.float32),
            pltpu.VMEM((tok_dev, STEP), jnp.int32),
            pltpu.VMEM((rows, HEAD), jnp.float32),
            pltpu.VMEM((rows, HEAD), jnp.float32),
            pltpu.VMEM((rows, HEAD), jnp.float32),
        ],
        compiler_params=pltpu.CompilerParams(vmem_limit_bytes=48 << 20),
        name="attend",
    )(seg_table, row_table, queries, window, bank)


MESH = pl.DeviceIdType.MESH


def place_of(group, head):
    tok, tall, core = lax.div(group, 8), lax.rem(lax.div(group, 2), 4), lax.rem(group, 2)
    return (tall * 4 + lax.rem(tok + head, 4)) * 2 + core


def group_at(ep, head):
    tall, wide, core = lax.div(ep, 8), lax.rem(lax.div(ep, 2), 4), lax.rem(ep, 2)
    return lax.rem(wide + 4 - head, 4) * 8 + 2 * tall + core


def owner_of(group, block):
    tok = lax.div(group, 8)
    return tok, lax.rem(group, 8) * 4 + block


def exchange_kernel(
    qkv_ref, cache_ref, slots_ref, query_ref, window_ref, bank_ref,
    stage_q, stage_kv, load_sems, key_send, key_recv, query_send, query_recv, pass_send, pass_recv, own_sem, line_send, line_recv,
    plane_send, plane_recv, pair_send, pair_recv,
):
    tok, ep = lax.axis_index("tok"), lax.axis_index("ep")
    tok_dev = qkv_ref.shape[0]
    q_width = QPG * HEAD
    number = tok * 32 + ep
    group, block = lax.div(number, 4), lax.rem(number, 4)
    mine = group_at(ep, tok)
    reach = SEG_MOST // (4 * tok_dev)
    span = 4 * tok_dev

    def column(head):
        return head * (q_width + 2 * HEAD)

    def remote(source, place, send_sem, recv_sem, device):
        return pltpu.make_async_remote_copy(
            src_ref=source, dst_ref=place, send_sem=send_sem, recv_sem=recv_sem, device_id=device, device_id_type=MESH
        )

    def load(turn, keys):
        head = lax.rem(tok + turn, 4)
        if keys:
            source = qkv_ref.at[:, pl.ds(pl.multiple_of(column(head) + q_width, HEAD), 2 * HEAD)]
            return pltpu.make_async_copy(source, stage_kv.at[turn], load_sems.at[turn])
        source = qkv_ref.at[:, pl.ds(pl.multiple_of(column(head), HEAD), q_width)]
        return pltpu.make_async_copy(source, stage_q.at[turn], load_sems.at[4 + turn])

    for keys in (True, False):
        for turn in range(4):
            load(turn, keys).start()

    def key_copy(turn):
        head = lax.rem(tok + turn, 4)
        place = window_ref.at[pl.ds(pl.multiple_of(reach * span + block * tok_dev, tok_dev), tok_dev)]
        return stage_kv.at[turn], place, key_send.at[turn], key_recv, (head, place_of(group, head))

    def query_copy(turn):
        head = lax.rem(tok + turn, 4)
        return stage_q.at[turn], query_ref.at[block], query_send.at[turn], query_recv, (head, place_of(group, head))

    def spans(index):
        return window_ref.at[pl.ds(pl.multiple_of(index * span, span), span)]

    def pass_copy(turn):
        device = (tok, place_of(lax.rem(mine + 2 * turn, 32), tok))
        return spans(reach), spans(reach - 2 * turn), pass_send.at[turn - 1], pass_recv.at[turn - 1], device

    def cross_copy(turn):
        device = (tok, at(tall, wide, 1 - core))
        return spans(6 - 2 * turn - 2 * core), spans(5 - 2 * turn), pass_send.at[turn + 1], pass_recv.at[turn + 1], device

    held, told = cache_ref.shape[0], slots_ref.shape[0]
    piece = held + told
    cut = piece // 32 * 16
    tall, wide, core = lax.div(ep, 8), lax.rem(lax.div(ep, 2), 4), lax.rem(ep, 2)

    def at(y, x, c):
        return (lax.rem(y, 4) * 4 + lax.rem(x, 4)) * 2 + c

    def part(y, x, c, start, size):
        return bank_ref.at[pl.ds(pl.multiple_of(at(y, x, c) * piece + start, 16), size)]

    own_cache = pltpu.make_async_copy(cache_ref, part(tall, wide, core, 0, held), own_sem.at[0])
    own_slots = pltpu.make_async_copy(slots_ref, part(tall, wide, core, held, told), own_sem.at[1])
    own_cache.start()
    own_slots.start()

    def line_copies():
        for turn in range(1, 4):
            first = part(tall, wide, core, 0, cut)
            yield remote(first, first, line_send, line_recv, (tok, at(tall, wide + turn, core)))
            rest = part(tall, wide, core, cut, piece - cut)
            yield remote(rest, rest, line_send, line_recv, (tok, at(tall + turn, wide, core)))

    def plane_copies():
        for turn in range(1, 4):
            for along in range(4):
                first = part(tall, wide + along, core, 0, cut)
                yield remote(first, first, plane_send, plane_recv, (tok, at(tall + turn, wide, core)))
                rest = part(tall + along, wide, core, cut, piece - cut)
                yield remote(rest, rest, plane_send, plane_recv, (tok, at(tall, wide + turn, core)))

    def pair_copies():
        for y in range(4):
            for x in range(4):
                whole = part(y, x, core, 0, piece)
                yield remote(whole, whole, pair_send, pair_recv, (tok, at(tall, wide, 1 - core)))

    def settle(rows, sem):
        pltpu.make_async_copy(bank_ref.at[pl.ds(0, rows)], bank_ref.at[pl.ds(0, rows)], sem).wait()

    barrier = pltpu.get_barrier_semaphore()
    at_home = place_of(group, tok) == ep
    for turn in range(1, 4):
        for partner in (at(tall, wide + turn, core), at(tall + turn, wide, core)):
            pl.semaphore_signal(barrier, inc=1, device_id=(tok, partner), device_id_type=MESH)
    pl.semaphore_signal(barrier, inc=1, device_id=(tok, at(tall, wide, 1 - core)), device_id_type=MESH)
    for turn in range(4):
        theirs = owner_of(mine, turn)

        @pl.when(jnp.logical_not((theirs[0] == tok) & (theirs[1] == ep)))
        def _():
            pl.semaphore_signal(barrier, inc=1, device_id=theirs, device_id_type=MESH)

    for turn in range(1, 3):
        pl.semaphore_signal(
            barrier, inc=1, device_id=(tok, place_of(lax.rem(mine + 32 - 2 * turn, 32), tok)), device_id_type=MESH
        )
    pl.semaphore_wait(barrier, 13 - jnp.where(at_home, 1, 0))

    own_cache.wait()
    own_slots.wait()
    for copy in (key_copy, query_copy):
        if copy is query_copy:
            for line_copy in line_copies():
                line_copy.start()
        for turn in range(4):
            source, place, send_sem, recv_sem, device = copy(turn)
            load(turn, copy is key_copy).wait()
            if turn == 0:

                @pl.when(at_home)
                def _():
                    pltpu.make_async_copy(source, place, recv_sem).start()

                @pl.when(jnp.logical_not(at_home))
                def _():
                    remote(source, place, send_sem, recv_sem, device).start()
            else:
                remote(source, place, send_sem, recv_sem, device).start()
    own = window_ref.at[pl.ds(reach * span, span)]
    pltpu.make_async_copy(own, own, key_recv).wait()
    for turn in range(1, 3):
        remote(*pass_copy(turn)).start()
    settle(3 * piece, line_recv)
    for plane_copy in plane_copies():
        plane_copy.start()
    settle(12 * piece, plane_recv)
    for pair_copy in pair_copies():
        pair_copy.start()
    for turn in range(1, 3):
        remote(*pass_copy(turn)).wait()
    for turn in range(1, 3):
        remote(*cross_copy(turn)).start()
    for turn in range(1, 3):
        remote(*cross_copy(turn)).wait()
    pltpu.make_async_copy(query_ref, query_ref, query_recv).wait()
    for copy in (key_copy, query_copy):
        for turn in range(4):
            if turn == 0:

                @pl.when(jnp.logical_not(at_home))
                def _():
                    remote(*copy(turn)).wait_send()
            else:
                remote(*copy(turn)).wait_send()
    settle(16 * piece, pair_recv)
    settle(3 * piece, line_send)
    settle(12 * piece, plane_send)
    settle(16 * piece, pair_send)


def exchange(qkv, cached, slots):
    tok_dev = qkv.shape[0]
    reach = SEG_MOST // (4 * tok_dev)
    kept = pl.BlockSpec(memory_space=pl.ANY)
    return pl.pallas_call(
        exchange_kernel,
        out_shape=(
            jax.ShapeDtypeStruct((4, tok_dev, QPG * HEAD), jnp.bfloat16),
            jax.ShapeDtypeStruct(((reach + 1) * 4 * tok_dev, 2 * HEAD), jnp.bfloat16),
            jax.ShapeDtypeStruct((32 * (cached.shape[0] + slots.shape[0]), 2 * HEAD), jnp.bfloat16),
        ),
        in_specs=[kept] * 3,
        out_specs=(kept,) * 3,
        scratch_shapes=[
            pltpu.VMEM((4, tok_dev, QPG * HEAD), jnp.bfloat16),
            pltpu.VMEM((4, tok_dev, 2 * HEAD), jnp.bfloat16),
            pltpu.SemaphoreType.DMA((8,)),
            pltpu.SemaphoreType.DMA((4,)),
            pltpu.SemaphoreType.DMA,
            pltpu.SemaphoreType.DMA((4,)),
            pltpu.SemaphoreType.DMA,
            pltpu.SemaphoreType.DMA((4,)),
            pltpu.SemaphoreType.DMA((4,)),
            pltpu.SemaphoreType.DMA((2,)),
        ]
        + [pltpu.SemaphoreType.DMA] * 6,
        compiler_params=pltpu.CompilerParams(collective_id=1, has_side_effects=True),
        cost_estimate=pl.CostEstimate(flops=0, bytes_accessed=80 << 20, transcendentals=0),
        name="exchange",
    )(qkv, cached, slots)


def project_kernel(
    attended_ref, weight_ref, resid_ref, gain_ref, mixed_ref, normed_ref, stage, inbox, send_sems, recv_sem
):
    tok, ep = lax.axis_index("tok"), lax.axis_index("ep")
    blocks, tok_dev, width = attended_ref.shape
    number = tok * 32 + ep
    group = lax.div(number, 4)
    mine = group_at(ep, tok)
    barrier = pltpu.get_barrier_semaphore()
    for turn in range(4):
        head = lax.rem(tok + turn, 4)
        target = place_of(group, head)

        @pl.when(jnp.logical_not((target == ep) & (head == tok)))
        def _():
            pl.semaphore_signal(barrier, inc=1, device_id=(head, target), device_id_type=MESH)

    home = [owner_of(mine, block) for block in range(blocks)]
    is_own = [(place[0] == tok) & (place[1] == ep) for place in home]
    others = 4 - sum([jnp.where(flag, 1, 0) for flag in is_own])
    pl.semaphore_wait(barrier, others)

    def copy(block):
        return pltpu.make_async_remote_copy(
            src_ref=stage.at[block], dst_ref=inbox.at[tok], send_sem=send_sems.at[block], recv_sem=recv_sem,
            device_id=home[block], device_id_type=MESH,
        )

    for block in range(blocks):
        stage[block] = jnp.dot(
            attended_ref[block], weight_ref[...], preferred_element_type=jnp.float32
        ).astype(jnp.bfloat16)

        @pl.when(is_own[block])
        def _():
            pltpu.make_async_copy(stage.at[block], inbox.at[tok], recv_sem).start()

        @pl.when(jnp.logical_not(is_own[block]))
        def _():
            copy(block).start()

    pltpu.make_async_copy(inbox, inbox, recv_sem).wait()
    added = resid_ref[...].astype(jnp.float32)
    for head in range(4):
        added = added + inbox[head].astype(jnp.float32)
    mixed = added.astype(jnp.bfloat16)
    mixed_ref[...] = mixed
    wide = mixed.astype(jnp.float32)
    level = lax.rsqrt(jnp.mean(wide * wide, axis=-1, keepdims=True) + NORM_EPS)
    normed_ref[...] = (wide * level * gain_ref[...]).astype(jnp.bfloat16)
    for block in range(blocks):

        @pl.when(jnp.logical_not(is_own[block]))
        def _():
            copy(block).wait_send()


def project(attended, weight, resid, gain):
    blocks, tok_dev, width = attended.shape
    out = weight.shape[1]
    vmem = pl.BlockSpec(memory_space=pltpu.VMEM)
    return pl.pallas_call(
        project_kernel,
        out_shape=(jax.ShapeDtypeStruct(resid.shape, jnp.bfloat16),) * 2,
        in_specs=[vmem] * 4,
        out_specs=(vmem, vmem),
        scratch_shapes=[
            pltpu.VMEM((blocks, tok_dev, out), jnp.bfloat16),
            pltpu.VMEM((4, tok_dev, out), jnp.bfloat16),
            pltpu.SemaphoreType.DMA((blocks,)),
            pltpu.SemaphoreType.DMA,
        ],
        compiler_params=pltpu.CompilerParams(collective_id=2, has_side_effects=True, vmem_limit_bytes=40 << 20),
        cost_estimate=pl.CostEstimate(flops=2 * blocks * tok_dev * width * out, bytes_accessed=40 << 20, transcendentals=0),
        name="project",
    )(attended, weight, resid, gain[None, :])


CAP = 16
GROUP = 16
MIX = 37

def hop(dims, step, way):
    deep, tall, wide, cores = dims
    total = deep * tall * wide * cores
    offset = lax.rem(step * MIX, total)
    tok, ep = lax.axis_index("tok"), lax.axis_index("ep")
    sizes = (deep, tall, wide, cores)
    mine = (tok, lax.div(ep, wide * cores), lax.rem(lax.div(ep, cores), wide), lax.rem(ep, cores))
    strides = (tall * wide * cores, wide * cores, cores, 1)
    at = [
        lax.rem(own + size + way * lax.rem(lax.div(offset, stride), size), size)
        for own, size, stride in zip(mine, sizes, strides)
    ]
    place = (at[1] * wide + at[2]) * cores + at[3]
    return (at[0], place), at[0] * (tall * wide * cores) + place


def routed_kernel(
    dims, normed_ref, mixed_ref, routes_ref, probs_ref, gate_up_hbm, down_hbm, out_ref,
    stage, arrived, back, gate_up, down, rank, share, pick, total,
    weight_sems, send_sems, recv_sems, back_send_sems, back_recv_sems,
):
    devices = dims[0] * dims[1] * dims[2] * dims[3]
    chunks = devices // GROUP
    rows = GROUP * CAP
    tokens = normed_ref.shape[0]
    hidden_width = down.shape[0]
    load_gate_up = pltpu.make_async_copy(gate_up_hbm.at[0], gate_up, weight_sems.at[0])
    load_down = pltpu.make_async_copy(down_hbm.at[0], down, weight_sems.at[1])
    load_gate_up.start()
    load_down.start()

    barrier = pltpu.get_barrier_semaphore()

    def greet(step, ignored):
        pl.semaphore_signal(barrier, inc=1, device_id=hop(dims, step, 1)[0], device_id_type=MESH)
        return ignored

    lax.fori_loop(1, devices, greet, 0)

    experts = lax.broadcasted_iota(jnp.int32, (devices, tokens), 0)
    probs = probs_ref[...]
    shares = probs / jnp.sum(probs, axis=0, keepdims=True)
    named = jnp.zeros((devices, tokens), jnp.float32)
    owed = jnp.zeros((devices, tokens), jnp.float32)
    for k in range(routes_ref.shape[0]):
        match = experts == routes_ref[k : k + 1, :]
        named = jnp.where(match, 1.0, named)
        owed = jnp.where(match, shares[k : k + 1, :], owed)
    before = (
        lax.broadcasted_iota(jnp.int32, (tokens, tokens), 0) < lax.broadcasted_iota(jnp.int32, (tokens, tokens), 1)
    ).astype(jnp.bfloat16)
    earlier = jnp.dot(named.astype(jnp.bfloat16), before, preferred_element_type=jnp.float32)
    rank[...] = jnp.where(named > 0.0, earlier, -1.0)
    share[...] = owed
    slot = lax.broadcasted_iota(jnp.int32, (CAP, tokens), 0).astype(jnp.float32)

    def slab(ref, step):
        return ref.at[pl.ds(pl.multiple_of(step * CAP, CAP), CAP)]

    def block(ref, chunk):
        return ref.at[pl.ds(pl.multiple_of(chunk * rows, rows), rows)]

    pl.semaphore_wait(barrier, devices - 1)

    def dispatch(chunk, ignored):
        def choose(j, inner):
            expert = hop(dims, chunk * GROUP + j, 1)[1]
            pick[pl.ds(pl.multiple_of(j * CAP, CAP), CAP), :] = jnp.where(
                rank[pl.ds(expert, 1), :] == slot, 1.0, 0.0
            ).astype(jnp.bfloat16)
            return inner

        lax.fori_loop(0, GROUP, choose, 0)
        block(stage, chunk)[...] = jnp.dot(
            pick[...], normed_ref[...], preferred_element_type=jnp.float32
        ).astype(jnp.bfloat16)

        def send(j, inner):
            step = chunk * GROUP + j

            @pl.when(step > 0)
            def _():
                pltpu.make_async_remote_copy(
                    src_ref=slab(stage, step), dst_ref=slab(arrived, step),
                    send_sem=send_sems.at[chunk], recv_sem=recv_sems.at[chunk],
                    device_id=hop(dims, step, 1)[0], device_id_type=MESH,
                ).start()

            @pl.when(step == 0)
            def _():
                pltpu.make_async_copy(slab(stage, step), slab(arrived, step), recv_sems.at[chunk]).start()

            return inner

        return lax.fori_loop(0, GROUP, send, ignored)

    lax.fori_loop(0, chunks, dispatch, 0)
    load_gate_up.wait()
    load_down.wait()

    def work(chunk, ignored):
        pltpu.make_async_copy(block(arrived, chunk), block(arrived, chunk), recv_sems.at[chunk]).wait()
        came = block(arrived, chunk)[...]
        gate = jnp.dot(came, gate_up[:, :hidden_width], preferred_element_type=jnp.float32)
        up = jnp.dot(came, gate_up[:, hidden_width:], preferred_element_type=jnp.float32)
        hidden = (gate * jax.nn.sigmoid(gate) * up).astype(jnp.bfloat16)
        block(arrived, chunk)[...] = jnp.dot(hidden, down[...], preferred_element_type=jnp.float32).astype(jnp.bfloat16)

        def give_back(j, inner):
            step = chunk * GROUP + j

            @pl.when(step > 0)
            def _():
                pltpu.make_async_remote_copy(
                    src_ref=slab(arrived, step), dst_ref=slab(back, step),
                    send_sem=back_send_sems.at[chunk], recv_sem=back_recv_sems.at[chunk],
                    device_id=hop(dims, step, -1)[0], device_id_type=MESH,
                ).start()

            @pl.when(step == 0)
            def _():
                pltpu.make_async_copy(slab(arrived, step), slab(back, step), back_recv_sems.at[chunk]).start()

            return inner

        return lax.fori_loop(0, GROUP, give_back, ignored)

    lax.fori_loop(0, chunks, work, 0)
    total[...] = mixed_ref[...].astype(jnp.float32)

    def combine(chunk, ignored):
        def owe(j, inner):
            expert = hop(dims, chunk * GROUP + j, 1)[1]
            pick[pl.ds(pl.multiple_of(j * CAP, CAP), CAP), :] = jnp.where(
                rank[pl.ds(expert, 1), :] == slot, share[pl.ds(expert, 1), :], 0.0
            ).astype(jnp.bfloat16)
            return inner

        lax.fori_loop(0, GROUP, owe, 0)
        pltpu.make_async_copy(block(back, chunk), block(back, chunk), back_recv_sems.at[chunk]).wait()
        total[...] += lax.dot_general(
            pick[...], block(back, chunk)[...], (((0,), (0,)), ((), ())), preferred_element_type=jnp.float32
        )
        return ignored

    lax.fori_loop(0, chunks, combine, 0)
    out_ref[...] = total[...].astype(jnp.bfloat16)

    own = CAP
    first = pl.ds(own, rows - own)
    pltpu.make_async_copy(stage.at[first], stage.at[first], send_sems.at[0]).wait()
    pltpu.make_async_copy(stage.at[first], stage.at[first], back_send_sems.at[0]).wait()

    def settle(chunk, ignored):
        pltpu.make_async_copy(block(stage, chunk), block(stage, chunk), send_sems.at[chunk]).wait()
        pltpu.make_async_copy(block(stage, chunk), block(stage, chunk), back_send_sems.at[chunk]).wait()
        return ignored

    lax.fori_loop(1, chunks, settle, 0)


def routed_experts(dims, normed, mixed, routes, probs, gate_up, down):
    devices = dims[0] * dims[1] * dims[2] * dims[3]
    chunks = devices // GROUP
    tokens, width = normed.shape
    slots = devices * CAP
    vmem = pl.BlockSpec(memory_space=pltpu.VMEM)
    kept = pl.BlockSpec(memory_space=pl.ANY)
    flops = 2 * slots * width * (down.shape[1] * 3 + 2 * tokens)
    return pl.pallas_call(
        functools.partial(routed_kernel, dims),
        out_shape=jax.ShapeDtypeStruct(mixed.shape, jnp.bfloat16),
        in_specs=[vmem] * 4 + [kept] * 2,
        out_specs=vmem,
        scratch_shapes=[
            pltpu.VMEM((slots, width), jnp.bfloat16),
            pltpu.VMEM((slots, width), jnp.bfloat16),
            pltpu.VMEM((slots, width), jnp.bfloat16),
            pltpu.VMEM(gate_up.shape[1:], jnp.bfloat16),
            pltpu.VMEM(down.shape[1:], jnp.bfloat16),
            pltpu.VMEM((devices, tokens), jnp.float32),
            pltpu.VMEM((devices, tokens), jnp.float32),
            pltpu.VMEM((GROUP * CAP, tokens), jnp.bfloat16),
            pltpu.VMEM((tokens, width), jnp.float32),
            pltpu.SemaphoreType.DMA((2,)),
            pltpu.SemaphoreType.DMA((chunks,)),
            pltpu.SemaphoreType.DMA((chunks,)),
            pltpu.SemaphoreType.DMA((chunks,)),
            pltpu.SemaphoreType.DMA((chunks,)),
        ],
        compiler_params=pltpu.CompilerParams(collective_id=0, has_side_effects=True, vmem_limit_bytes=56 << 20),
        cost_estimate=pl.CostEstimate(flops=flops, bytes_accessed=6 * slots * width * 2, transcendentals=0),
        name="routed_experts",
    )(normed, mixed, routes.T, probs.T, gate_up, down)


def on_device(
    resid,
    qkv,
    cache_kv,
    page_slot,
    seg_lengths,
    cache_age,
    w_out,
    norm_gain,
    routes,
    route_probs,
    w_gate_up,
    w_down,
):
    tok_groups = lax.axis_size("tok")
    ep_count = lax.axis_size("ep")
    tok_dev = resid.shape[0]
    seg_count = seg_lengths.shape[0]
    page_count = cache_kv.shape[0]
    slots = jnp.broadcast_to(
        jnp.pad(page_slot, (0, 2 * HEAD - page_count))[None, :], (META_ROWS, 2 * HEAD)
    ).astype(jnp.bfloat16)
    bank_rows = page_count * PAGE + META_ROWS
    queries, window, bank = exchange(qkv, cache_kv.reshape(page_count * PAGE, 2 * HEAD), slots)
    held = bank.reshape(ep_count, bank_rows, 2 * HEAD)[:, bank_rows - 1, :page_count].astype(jnp.int32)
    slot_row = (
        jnp.arange(ep_count, dtype=jnp.int32)[:, None] * bank_rows
        + jnp.arange(page_count, dtype=jnp.int32)[None, :] * PAGE
    )
    page_match = held.reshape(-1)[None, :] == jnp.arange(seg_count * SEG_PAGES, dtype=jnp.int32)[:, None]
    row_table = jnp.sum(jnp.where(page_match, slot_row.reshape(-1)[None, :], 0), axis=1).astype(jnp.int32)
    seg_ends = jnp.cumsum(seg_lengths)
    blocks = queries.shape[0]
    first_tokens = (group_at(lax.axis_index("ep"), lax.axis_index("tok")) * blocks + jnp.arange(blocks, dtype=jnp.int32)) * tok_dev
    seg_table = jnp.concatenate([seg_ends - seg_lengths, seg_ends, cache_age, first_tokens]).astype(jnp.int32)
    attended = attention(seg_table, row_table, queries, window, bank, seg_count, SEG_MOST)
    mixed, normed = project(attended, w_out, resid, norm_gain)
    dims = (tok_groups, ep_count // 8, 4, 2)
    return routed_experts(dims, normed, mixed, routes, route_probs, w_gate_up, w_down)


def solution(mesh):
    placed = (
        P(("tok", "ep"), None),
        P(("tok", "ep"), None),
        P("ep", "tok", None, None),
        P("ep"),
        P(),
        P(),
        P("tok", None),
        P(),
        P(("tok", "ep"), None),
        P(("tok", "ep"), None),
        P(("tok", "ep"), None, None),
        P(("tok", "ep"), None, None),
    )
    return jax.shard_map(
        on_device, mesh=mesh, in_specs=placed, out_specs=P(("tok", "ep"), None), check_vma=False
    )
```

```python
import functools
import math

import jax
import jax.numpy as jnp
from jax import lax
from jax.experimental import pallas as pl
from jax.experimental.pallas import tpu as pltpu
from jax.sharding import PartitionSpec as P

D = 2048
FF = 768
HEAD = 128
QPG = 8
TOP = 8
PAGE = 64
SEG_PAGES = 8
SEG_MOST = 2048
STEP = 256
META_ROWS = 16


NEG_FILL = -1e30
NORM_EPS = 1e-06


def attention_kernel(tok_dev, segs, most_steps, seg_ref, row_ref, q_ref, window_ref, bank_ref, out_ref, score_ref, low_ref, top_ref, den_ref, acc_ref):
    rows = tok_dev * QPG
    held_chunks = window_ref.shape[0] // tok_dev
    opening_chunk = seg_ref[3 * segs] // tok_dev - (held_chunks - q_ref.shape[0])
    rate = math.log2(math.e) / math.sqrt(HEAD)

    def tiled(mask):
        return jnp.concatenate([mask] * QPG, axis=0)

    def one_block(block, carry):
        first = seg_ref[3 * segs + block]
        last = first + tok_dev - 1
        token = first + lax.broadcasted_iota(jnp.int32, (tok_dev, STEP), 0)
        column = lax.broadcasted_iota(jnp.int32, (tok_dev, STEP), 1)
        low = jnp.zeros((tok_dev, STEP), jnp.int32)
        begin = jnp.int32(0)
        for s in range(segs):
            start = seg_ref[s]
            low = jnp.where(token >= start, start, low)
            begin = jnp.where(first >= start, start, begin)
        low_ref[...] = low
        query = jnp.concatenate([q_ref[block, :, h * HEAD:(h + 1) * HEAD] for h in range(QPG)], axis=0)
        den_ref[...] = jnp.zeros_like(den_ref)
        acc_ref[...] = jnp.zeros_like(acc_ref)

        def region(bank, steps, bank_of, mask_of, opening):
            if opening:
                held = jnp.full((rows, HEAD), NEG_FILL, jnp.float32)
            else:
                held = top_ref[...]

            def score(step, running):
                keys = jnp.concatenate([bank[pl.ds(at, size), :HEAD] for at, size in bank_of(step)], axis=0)
                scores = lax.dot_general(query, keys, (((1,), (1,)), ((), ())), preferred_element_type=jnp.float32) * rate
                scores = jnp.where(tiled(mask_of(step)), scores, NEG_FILL)
                score_ref[step] = scores
                return jnp.maximum(running, jnp.maximum(scores[:, :HEAD], scores[:, HEAD:]))

            newest = lax.fori_loop(0, steps, score, held)
            newest = jnp.broadcast_to(jnp.max(newest, axis=1, keepdims=True), (rows, HEAD))
            if not opening:
                factor = jnp.exp2(held - newest)
                den_ref[...] = den_ref[...] * factor
                acc_ref[...] = acc_ref[...] * factor
            top_ref[...] = newest

            def weigh(step, ignored):
                top = top_ref[...]
                weights = jnp.exp2(score_ref[step] - jnp.concatenate([top, top], axis=1))
                den_ref[...] += weights[:, :HEAD] + weights[:, HEAD:]
                values = jnp.concatenate([bank[pl.ds(at, size), HEAD:] for at, size in bank_of(step)], axis=0)
                acc_ref[...] += jnp.dot(weights.astype(jnp.bfloat16), values, preferred_element_type=jnp.float32)
                return ignored

            lax.fori_loop(0, steps, weigh, 0)

        chunk_last = first // tok_dev
        chunk_first = begin // tok_dev
        steps = (chunk_last - chunk_first + 2) // 2

        def new_chunk(step, half):
            return chunk_last - 2 * step - 1 + half

        def new_bank(step):
            return [
                (pl.multiple_of(jnp.clip(new_chunk(step, half) - opening_chunk, 0, held_chunks - 1) * tok_dev, tok_dev), tok_dev)
                for half in range(2)
            ]

        def new_mask(step):
            key = new_chunk(step, 0) * tok_dev + column
            return (key >= low_ref[...]) & (key <= token)

        region(window_ref, steps, new_bank, new_mask, True)

        def cached(s, ignored):
            start, end, age = seg_ref[s], seg_ref[segs + s], seg_ref[2 * segs + s]

            @pl.when((start <= last) & (end > first) & (age > 0))
            def _():
                def page_bank(step):
                    return [(pl.multiple_of(row_ref[s * SEG_PAGES + step * (STEP // PAGE) + part], 16), PAGE) for part in range(STEP // PAGE)]

                def page_mask(step):
                    return (token >= start) & (token < end) & (step * STEP + column < age)

                region(bank_ref, (age + STEP - 1) // STEP, page_bank, page_mask, False)
            return ignored

        lax.fori_loop(0, segs, cached, 0)
        total = jnp.sum(den_ref[...], axis=1, keepdims=True)
        result = (acc_ref[...] / total).astype(jnp.bfloat16)
        for h in range(QPG):
            out_ref[block, :, h * HEAD:(h + 1) * HEAD] = result[h * tok_dev:(h + 1) * tok_dev]
        return carry

    lax.fori_loop(0, q_ref.shape[0], one_block, 0)


def attention(seg_table, row_table, queries, window, bank, segs, seg_most):
    blocks, tok_dev, width = queries.shape
    most_steps = max((seg_most + tok_dev) // tok_dev // 2 + 1, SEG_PAGES * PAGE // STEP)
    rows = tok_dev * QPG
    return pl.pallas_call(
        functools.partial(attention_kernel, tok_dev, segs, most_steps),
        out_shape=jax.ShapeDtypeStruct(queries.shape, jnp.bfloat16),
        in_specs=[pl.BlockSpec(memory_space=pltpu.SMEM)] * 2 + [pl.BlockSpec(memory_space=pltpu.VMEM)] * 3,
        out_specs=pl.BlockSpec(memory_space=pltpu.VMEM),
        scratch_shapes=[
            pltpu.VMEM((most_steps, rows, STEP), jnp.float32),
            pltpu.VMEM((tok_dev, STEP), jnp.int32),
            pltpu.VMEM((rows, HEAD), jnp.float32),
            pltpu.VMEM((rows, HEAD), jnp.float32),
            pltpu.VMEM((rows, HEAD), jnp.float32),
        ],
        compiler_params=pltpu.CompilerParams(vmem_limit_bytes=48 << 20),
        name="attend",
    )(seg_table, row_table, queries, window, bank)


MESH = pl.DeviceIdType.MESH


def place_of(group, head):
    tok, tall, core = lax.div(group, 8), lax.rem(lax.div(group, 2), 4), lax.rem(group, 2)
    return (tall * 4 + lax.rem(tok + head, 4)) * 2 + core


def group_at(ep, head):
    tall, wide, core = lax.div(ep, 8), lax.rem(lax.div(ep, 2), 4), lax.rem(ep, 2)
    return lax.rem(wide + 4 - head, 4) * 8 + 2 * tall + core


def owner_of(group, block):
    tok = lax.div(group, 8)
    return tok, lax.rem(group, 8) * 4 + block


def exchange_kernel(
    qkv_ref, cache_ref, slots_ref, query_ref, window_ref, bank_ref,
    stage_q, stage_kv, load_sems, key_send, key_recv, query_send, query_recv, pass_send, pass_recv, own_sem, line_send, line_recv,
    plane_send, plane_recv, pair_send, pair_recv,
):
    tok, ep = lax.axis_index("tok"), lax.axis_index("ep")
    tok_dev = qkv_ref.shape[0]
    q_width = QPG * HEAD
    number = tok * 32 + ep
    group, block = lax.div(number, 4), lax.rem(number, 4)
    mine = group_at(ep, tok)
    reach = SEG_MOST // (4 * tok_dev)
    span = 4 * tok_dev

    def column(head):
        return head * (q_width + 2 * HEAD)

    def remote(source, place, send_sem, recv_sem, device):
        return pltpu.make_async_remote_copy(
            src_ref=source, dst_ref=place, send_sem=send_sem, recv_sem=recv_sem, device_id=device, device_id_type=MESH
        )

    def load(turn, keys):
        head = lax.rem(tok + turn, 4)
        if keys:
            source = qkv_ref.at[:, pl.ds(pl.multiple_of(column(head) + q_width, HEAD), 2 * HEAD)]
            return pltpu.make_async_copy(source, stage_kv.at[turn], load_sems.at[turn])
        source = qkv_ref.at[:, pl.ds(pl.multiple_of(column(head), HEAD), q_width)]
        return pltpu.make_async_copy(source, stage_q.at[turn], load_sems.at[4 + turn])

    for keys in (True, False):
        for turn in range(4):
            load(turn, keys).start()

    def key_copy(turn):
        head = lax.rem(tok + turn, 4)
        place = window_ref.at[pl.ds(pl.multiple_of(reach * span + block * tok_dev, tok_dev), tok_dev)]
        return stage_kv.at[turn], place, key_send.at[turn], key_recv, (head, place_of(group, head))

    def query_copy(turn):
        head = lax.rem(tok + turn, 4)
        return stage_q.at[turn], query_ref.at[block], query_send.at[turn], query_recv, (head, place_of(group, head))

    def spans(index):
        return window_ref.at[pl.ds(pl.multiple_of(index * span, span), span)]

    def pass_copy(turn):
        device = (tok, place_of(lax.rem(mine + 2 * turn, 32), tok))
        return spans(reach), spans(reach - 2 * turn), pass_send.at[turn - 1], pass_recv.at[turn - 1], device

    def cross_copy(turn):
        device = (tok, at(tall, wide, 1 - core))
        return spans(6 - 2 * turn - 2 * core), spans(5 - 2 * turn), pass_send.at[turn + 1], pass_recv.at[turn + 1], device

    held, told = cache_ref.shape[0], slots_ref.shape[0]
    piece = held + told
    cut = piece // 32 * 16
    tall, wide, core = lax.div(ep, 8), lax.rem(lax.div(ep, 2), 4), lax.rem(ep, 2)

    def at(y, x, c):
        return (lax.rem(y, 4) * 4 + lax.rem(x, 4)) * 2 + c

    def part(y, x, c, start, size):
        return bank_ref.at[pl.ds(pl.multiple_of(at(y, x, c) * piece + start, 16), size)]

    own_cache = pltpu.make_async_copy(cache_ref, part(tall, wide, core, 0, held), own_sem.at[0])
    own_slots = pltpu.make_async_copy(slots_ref, part(tall, wide, core, held, told), own_sem.at[1])
    own_cache.start()
    own_slots.start()

    def line_copies():
        for turn in range(1, 4):
            first = part(tall, wide, core, 0, cut)
            yield remote(first, first, line_send, line_recv, (tok, at(tall, wide + turn, core)))
            rest = part(tall, wide, core, cut, piece - cut)
            yield remote(rest, rest, line_send, line_recv, (tok, at(tall + turn, wide, core)))

    def plane_copies():
        for turn in range(1, 4):
            for along in range(4):
                first = part(tall, wide + along, core, 0, cut)
                yield remote(first, first, plane_send, plane_recv, (tok, at(tall + turn, wide, core)))
                rest = part(tall + along, wide, core, cut, piece - cut)
                yield remote(rest, rest, plane_send, plane_recv, (tok, at(tall, wide + turn, core)))

    def pair_copies():
        for y in range(4):
            for x in range(4):
                whole = part(y, x, core, 0, piece)
                yield remote(whole, whole, pair_send, pair_recv, (tok, at(tall, wide, 1 - core)))

    def settle(rows, sem):
        pltpu.make_async_copy(bank_ref.at[pl.ds(0, rows)], bank_ref.at[pl.ds(0, rows)], sem).wait()

    barrier = pltpu.get_barrier_semaphore()
    at_home = place_of(group, tok) == ep
    for turn in range(1, 4):
        for partner in (at(tall, wide + turn, core), at(tall + turn, wide, core)):
            pl.semaphore_signal(barrier, inc=1, device_id=(tok, partner), device_id_type=MESH)
    pl.semaphore_signal(barrier, inc=1, device_id=(tok, at(tall, wide, 1 - core)), device_id_type=MESH)
    for turn in range(4):
        theirs = owner_of(mine, turn)

        @pl.when(jnp.logical_not((theirs[0] == tok) & (theirs[1] == ep)))
        def _():
            pl.semaphore_signal(barrier, inc=1, device_id=theirs, device_id_type=MESH)

    for turn in range(1, 3):
        pl.semaphore_signal(
            barrier, inc=1, device_id=(tok, place_of(lax.rem(mine + 32 - 2 * turn, 32), tok)), device_id_type=MESH
        )
    pl.semaphore_wait(barrier, 13 - jnp.where(at_home, 1, 0))

    own_cache.wait()
    own_slots.wait()
    for copy in (key_copy, query_copy):
        if copy is query_copy:
            for line_copy in line_copies():
                line_copy.start()
        for turn in range(4):
            source, place, send_sem, recv_sem, device = copy(turn)
            load(turn, copy is key_copy).wait()
            if turn == 0:

                @pl.when(at_home)
                def _():
                    pltpu.make_async_copy(source, place, recv_sem).start()

                @pl.when(jnp.logical_not(at_home))
                def _():
                    remote(source, place, send_sem, recv_sem, device).start()
            else:
                remote(source, place, send_sem, recv_sem, device).start()
    own = window_ref.at[pl.ds(reach * span, span)]
    pltpu.make_async_copy(own, own, key_recv).wait()
    for turn in range(1, 3):
        remote(*pass_copy(turn)).start()
    settle(3 * piece, line_recv)
    for plane_copy in plane_copies():
        plane_copy.start()
    settle(12 * piece, plane_recv)
    for pair_copy in pair_copies():
        pair_copy.start()
    for turn in range(1, 3):
        remote(*pass_copy(turn)).wait()
    for turn in range(1, 3):
        remote(*cross_copy(turn)).start()
    for turn in range(1, 3):
        remote(*cross_copy(turn)).wait()
    pltpu.make_async_copy(query_ref, query_ref, query_recv).wait()
    for copy in (key_copy, query_copy):
        for turn in range(4):
            if turn == 0:

                @pl.when(jnp.logical_not(at_home))
                def _():
                    remote(*copy(turn)).wait_send()
            else:
                remote(*copy(turn)).wait_send()
    settle(16 * piece, pair_recv)
    settle(3 * piece, line_send)
    settle(12 * piece, plane_send)
    settle(16 * piece, pair_send)


def exchange(qkv, cached, slots):
    tok_dev = qkv.shape[0]
    reach = SEG_MOST // (4 * tok_dev)
    kept = pl.BlockSpec(memory_space=pl.ANY)
    return pl.pallas_call(
        exchange_kernel,
        out_shape=(
            jax.ShapeDtypeStruct((4, tok_dev, QPG * HEAD), jnp.bfloat16),
            jax.ShapeDtypeStruct(((reach + 1) * 4 * tok_dev, 2 * HEAD), jnp.bfloat16),
            jax.ShapeDtypeStruct((32 * (cached.shape[0] + slots.shape[0]), 2 * HEAD), jnp.bfloat16),
        ),
        in_specs=[kept] * 3,
        out_specs=(kept,) * 3,
        scratch_shapes=[
            pltpu.VMEM((4, tok_dev, QPG * HEAD), jnp.bfloat16),
            pltpu.VMEM((4, tok_dev, 2 * HEAD), jnp.bfloat16),
            pltpu.SemaphoreType.DMA((8,)),
            pltpu.SemaphoreType.DMA((4,)),
            pltpu.SemaphoreType.DMA,
            pltpu.SemaphoreType.DMA((4,)),
            pltpu.SemaphoreType.DMA,
            pltpu.SemaphoreType.DMA((4,)),
            pltpu.SemaphoreType.DMA((4,)),
            pltpu.SemaphoreType.DMA((2,)),
        ]
        + [pltpu.SemaphoreType.DMA] * 6,
        compiler_params=pltpu.CompilerParams(collective_id=1, has_side_effects=True),
        cost_estimate=pl.CostEstimate(flops=0, bytes_accessed=80 << 20, transcendentals=0),
        name="exchange",
    )(qkv, cached, slots)


def project_kernel(
    attended_ref, weight_ref, resid_ref, gain_ref, mixed_ref, normed_ref, stage, inbox, send_sems, recv_sem
):
    tok, ep = lax.axis_index("tok"), lax.axis_index("ep")
    blocks, tok_dev, width = attended_ref.shape
    number = tok * 32 + ep
    group = lax.div(number, 4)
    mine = group_at(ep, tok)
    barrier = pltpu.get_barrier_semaphore()
    for turn in range(4):
        head = lax.rem(tok + turn, 4)
        target = place_of(group, head)

        @pl.when(jnp.logical_not((target == ep) & (head == tok)))
        def _():
            pl.semaphore_signal(barrier, inc=1, device_id=(head, target), device_id_type=MESH)

    home = [owner_of(mine, block) for block in range(blocks)]
    is_own = [(place[0] == tok) & (place[1] == ep) for place in home]
    others = 4 - sum([jnp.where(flag, 1, 0) for flag in is_own])
    pl.semaphore_wait(barrier, others)

    def copy(block):
        return pltpu.make_async_remote_copy(
            src_ref=stage.at[block], dst_ref=inbox.at[tok], send_sem=send_sems.at[block], recv_sem=recv_sem,
            device_id=home[block], device_id_type=MESH,
        )

    for block in range(blocks):
        stage[block] = jnp.dot(
            attended_ref[block], weight_ref[...], preferred_element_type=jnp.float32
        ).astype(jnp.bfloat16)

        @pl.when(is_own[block])
        def _():
            pltpu.make_async_copy(stage.at[block], inbox.at[tok], recv_sem).start()

        @pl.when(jnp.logical_not(is_own[block]))
        def _():
            copy(block).start()

    pltpu.make_async_copy(inbox, inbox, recv_sem).wait()
    added = resid_ref[...].astype(jnp.float32)
    for head in range(4):
        added = added + inbox[head].astype(jnp.float32)
    mixed = added.astype(jnp.bfloat16)
    mixed_ref[...] = mixed
    wide = mixed.astype(jnp.float32)
    level = lax.rsqrt(jnp.mean(wide * wide, axis=-1, keepdims=True) + NORM_EPS)
    normed_ref[...] = (wide * level * gain_ref[...]).astype(jnp.bfloat16)
    for block in range(blocks):

        @pl.when(jnp.logical_not(is_own[block]))
        def _():
            copy(block).wait_send()


def project(attended, weight, resid, gain):
    blocks, tok_dev, width = attended.shape
    out = weight.shape[1]
    vmem = pl.BlockSpec(memory_space=pltpu.VMEM)
    return pl.pallas_call(
        project_kernel,
        out_shape=(jax.ShapeDtypeStruct(resid.shape, jnp.bfloat16),) * 2,
        in_specs=[vmem] * 4,
        out_specs=(vmem, vmem),
        scratch_shapes=[
            pltpu.VMEM((blocks, tok_dev, out), jnp.bfloat16),
            pltpu.VMEM((4, tok_dev, out), jnp.bfloat16),
            pltpu.SemaphoreType.DMA((blocks,)),
            pltpu.SemaphoreType.DMA,
        ],
        compiler_params=pltpu.CompilerParams(collective_id=2, has_side_effects=True, vmem_limit_bytes=40 << 20),
        cost_estimate=pl.CostEstimate(flops=2 * blocks * tok_dev * width * out, bytes_accessed=40 << 20, transcendentals=0),
        name="project",
    )(attended, weight, resid, gain[None, :])


CAP = 16
SIDE = 4
PLANE = 32
CUTS = ((0, 768), (768, 640), (1408, 640))


def position():
    tok, ep = lax.axis_index("tok"), lax.axis_index("ep")
    return tok, lax.div(ep, 8), lax.rem(lax.div(ep, 2), 4), lax.rem(ep, 2)


def moved(offsets, way):
    at = [lax.rem(own + size + way * off, size) for own, off, size in zip(position(), offsets, (4, 4, 4, 2))]
    return at[0], (at[1] * 4 + at[2]) * 2 + at[3]


def plane_offsets(cut, index, div, rem):
    core, outer, inner = div(index, 16), rem(div(index, 4), 4), rem(index, 4)
    return ((0, inner, outer, core), (inner, 0, outer, core), (outer, inner, 0, core))[cut]


def line_offsets(cut, turn):
    return tuple(turn if axis == cut else 0 for axis in range(3)) + (0,)


def routed_kernel(
    normed_ref, mixed_ref, table_ref, gate_up_hbm, down_hbm, out_ref,
    line0, line1, line2, stage0, stage1, stage2, came0, came1, came2, back0, back1, back2,
    part0, part1, part2, inbox0, inbox1, inbox2, sum0, sum1, sum2,
    gate_up, down, tables, rank, share, pick, rows_in,
    weight_sems, table_sems, line_send, line_recv, out_send, near_recv, far_recv, home_send, home_recv,
    part_send, part_recv,
):
    lines, stages, cames, backs = (line0, line1, line2), (stage0, stage1, stage2), (came0, came1, came2), (back0, back1, back2)
    parts, inboxes, sums = (part0, part1, part2), (inbox0, inbox1, inbox2), (sum0, sum1, sum2)
    tokens = normed_ref.shape[0]
    width = down.shape[0]
    devices = SIDE * PLANE
    message = SIDE * CAP
    load_gate_up = pltpu.make_async_copy(gate_up_hbm.at[0], gate_up, weight_sems.at[0])
    load_down = pltpu.make_async_copy(down_hbm.at[0], down, weight_sems.at[1])
    load_gate_up.start()
    load_down.start()
    barrier = pltpu.get_barrier_semaphore()

    def greet(step, ignored):
        offsets = (lax.div(step, 32), lax.rem(lax.div(step, 8), 4), lax.rem(lax.div(step, 2), 4), lax.rem(step, 2))
        pl.semaphore_signal(barrier, inc=1, device_id=moved(offsets, 1), device_id_type=MESH)
        return ignored

    lax.fori_loop(1, devices, greet, 0)
    for cut, (start, size) in enumerate(CUTS):
        lines[cut][:tokens] = normed_ref[:, start : start + size]
        tables[cut, 0] = table_ref[...]
    pl.semaphore_wait(barrier, devices - 1)

    def remote(source, place, send_sem, recv_sem, device):
        return pltpu.make_async_remote_copy(
            src_ref=source, dst_ref=place, send_sem=send_sem, recv_sem=recv_sem, device_id=device, device_id_type=MESH
        )

    def rows_of(ref, start, size):
        return ref.at[pl.ds(pl.multiple_of(start, CAP), size)]

    def settle(ref, size, sem):
        pltpu.make_async_copy(ref.at[pl.ds(0, size)], ref.at[pl.ds(0, size)], sem).wait()

    for cut in range(3):
        for turn in range(1, SIDE):
            remote(
                table_ref, tables.at[cut, turn], table_sems.at[0], table_sems.at[1], moved(line_offsets(cut, turn), 1)
            ).start()
    for cut in range(3):
        for turn in range(1, SIDE):
            remote(
                rows_of(lines[cut], 0, tokens), rows_of(lines[cut], turn * tokens, tokens),
                line_send.at[cut], line_recv.at[cut], moved(line_offsets(cut, turn), 1),
            ).start()

    pltpu.make_async_copy(tables.at[:, pl.ds(0, 3)], tables.at[:, pl.ds(0, 3)], table_sems.at[1]).wait()
    before = (
        lax.broadcasted_iota(jnp.int32, (tokens, tokens), 0) < lax.broadcasted_iota(jnp.int32, (tokens, tokens), 1)
    ).astype(jnp.bfloat16)
    index = lax.broadcasted_iota(jnp.int32, (PLANE, tokens), 0)
    shift = {16: 4, 4: 2}
    top = table_ref.shape[0] // 2
    for cut in range(3):
        offsets = plane_offsets(cut, index, lambda v, d: v >> shift[d], lambda v, d: v & (d - 1))
        z, y, x, c = [(own + off) & (size - 1) for own, off, size in zip(position(), offsets, (4, 4, 4, 2))]
        expert = (z * 32 + y * 8 + x * 2 + c).astype(jnp.float32)
        for turn in range(SIDE):
            probs = tables[cut, turn, top:, :]
            shares = probs / jnp.sum(probs, axis=0, keepdims=True)
            named = jnp.zeros((PLANE, tokens), jnp.float32)
            owed = jnp.zeros((PLANE, tokens), jnp.float32)
            for k in range(top):
                match = expert == tables[cut, turn, k : k + 1, :]
                named = jnp.where(match, 1.0, named)
                owed = jnp.where(match, shares[k : k + 1, :], owed)
            earlier = jnp.dot(named.astype(jnp.bfloat16), before, preferred_element_type=jnp.float32)
            at = (cut * SIDE + turn) * PLANE
            rank[at : at + PLANE, :] = jnp.where(named > 0.0, earlier, -1.0)
            share[at : at + PLANE, :] = owed

    slot = lax.broadcasted_iota(jnp.int32, (CAP, tokens), 0).astype(jnp.float32)

    def choose(cut, core, turn, weighted):
        for j in range(16):
            at = (cut * SIDE + turn) * PLANE + core * 16 + j
            chosen = share[pl.ds(at, 1), :] if weighted else 1.0
            pick[j * CAP : (j + 1) * CAP, :] = jnp.where(rank[pl.ds(at, 1), :] == slot, chosen, 0.0).astype(jnp.bfloat16)

    def send(cut, i, recv_sem):
        source, place = rows_of(stages[cut], i * message, message), rows_of(cames[cut], i * message, message)
        offsets = plane_offsets(cut, i, lax.div, lax.rem)

        @pl.when(i == 0)
        def _():
            pltpu.make_async_copy(source, place, recv_sem).start()

        @pl.when(i > 0)
        def _():
            remote(source, place, out_send.at[cut], recv_sem, moved(offsets, 1)).start()

    def fill(cut, core):
        def one_shard(turn, ignored):
            choose(cut, core, turn, False)
            found = jnp.dot(
                pick[...], rows_of(lines[cut], turn * tokens, tokens)[...], preferred_element_type=jnp.float32
            ).astype(jnp.bfloat16)
            for j in range(16):
                rows_of(stages[cut], (core * 16 + j) * message + turn * CAP, CAP)[...] = found[j * CAP : (j + 1) * CAP]
            return ignored

        lax.fori_loop(0, SIDE, one_shard, 0)

    def dispatch(core, ignored):
        fill(2, core)

        def send_far(j, inner):
            send(2, core * 16 + j, far_recv.at[core])
            return inner

        lax.fori_loop(0, 16, send_far, 0)
        fill(0, core)
        fill(1, core)

        def send_near(j, inner):
            chunk = core * 4 + lax.div(j, 4)
            send(0, core * 16 + j, near_recv.at[0, chunk])
            send(1, core * 16 + j, near_recv.at[1, chunk])
            return inner

        return lax.fori_loop(0, 16, send_near, ignored)

    for cut in range(3):
        settle(lines[cut], 3 * tokens, line_recv.at[cut])
    lax.fori_loop(0, 2, dispatch, 0)
    load_gate_up.wait()
    load_down.wait()
    block = SIDE * message

    def slab1(chunk, j):
        return rows_of(came1, chunk * block + (j % 4) * message + (j // 4) * CAP, CAP)

    def slab2(chunk, j):
        core, wide = lax.div(chunk, 4), lax.rem(chunk, 4)
        return rows_of(came2, (core * 16 + (j % 4) * 4 + j // 4) * message + wide * CAP, CAP)

    def give(cut, i):
        source, place = rows_of(cames[cut], i * message, message), rows_of(backs[cut], i * message, message)
        offsets = plane_offsets(cut, i, lax.div, lax.rem)
        recv_sem = home_recv.at[cut, lax.div(i, 16)]

        @pl.when(i == 0)
        def _():
            pltpu.make_async_copy(source, place, recv_sem).start()

        @pl.when(i > 0)
        def _():
            remote(source, place, home_send.at[cut], recv_sem, moved(offsets, -1)).start()

    def work(chunk, ignored):
        @pl.when(lax.rem(chunk, 4) == 0)
        def _():
            settle(came2, 16 * message, far_recv.at[lax.div(chunk, 4)])

        settle(came0, block, near_recv.at[0, chunk])
        settle(came1, block, near_recv.at[1, chunk])
        rows_in[:, 0:768] = rows_of(came0, chunk * block, block)[...]
        for j in range(16):
            rows_in[j * CAP : (j + 1) * CAP, 768:1408] = slab1(chunk, j)[...]
            rows_in[j * CAP : (j + 1) * CAP, 1408:2048] = slab2(chunk, j)[...]
        gate = jnp.dot(rows_in[...], gate_up[:, :width], preferred_element_type=jnp.float32)
        up = jnp.dot(rows_in[...], gate_up[:, width:], preferred_element_type=jnp.float32)
        hidden = (gate * jax.nn.sigmoid(gate) * up).astype(jnp.bfloat16)
        made = jnp.dot(hidden, down[...], preferred_element_type=jnp.float32).astype(jnp.bfloat16)
        rows_of(came0, chunk * block, block)[...] = made[:, 0:768]
        for j in range(16):
            slab1(chunk, j)[...] = made[j * CAP : (j + 1) * CAP, 768:1408]
            slab2(chunk, j)[...] = made[j * CAP : (j + 1) * CAP, 1408:2048]

        def give_near(j, inner):
            give(0, chunk * 4 + j)
            give(1, chunk * 4 + j)
            return inner

        lax.fori_loop(0, 4, give_near, 0)

        @pl.when(lax.rem(chunk, 4) == 3)
        def _():
            def give_far(j, inner):
                give(2, lax.div(chunk, 4) * 16 + j)
                return inner

            lax.fori_loop(0, 16, give_far, 0)

        return ignored

    lax.fori_loop(0, 8, work, 0)

    for cut in range(3):
        sums[cut][...] = jnp.zeros_like(sums[cut])

    def combine(core, ignored):
        for cut in range(3):
            settle(backs[cut], 16 * message, home_recv.at[cut, core])

            def one_shard(turn, inner):
                choose(cut, core, turn, True)
                found = jnp.concatenate(
                    [rows_of(backs[cut], (core * 16 + j) * message + turn * CAP, CAP)[...] for j in range(16)], axis=0
                )
                total = rows_of(sums[cut], turn * tokens, tokens)
                total[...] += lax.dot_general(
                    pick[...], found, (((0,), (0,)), ((), ())), preferred_element_type=jnp.float32
                )
                return inner

            lax.fori_loop(0, SIDE, one_shard, 0)

            @pl.when(core == 1)
            def _():
                parts[cut][...] = sums[cut][...].astype(jnp.bfloat16)
                for turn in range(1, SIDE):
                    remote(
                        rows_of(parts[cut], turn * tokens, tokens), rows_of(inboxes[cut], turn * tokens, tokens),
                        part_send.at[cut], part_recv.at[cut], moved(line_offsets(cut, turn), -1),
                    ).start()

        return ignored

    lax.fori_loop(0, 2, combine, 0)
    for cut, (start, size) in enumerate(CUTS):
        settle(inboxes[cut], 3 * tokens, part_recv.at[cut])
        total = mixed_ref[:, start : start + size].astype(jnp.float32) + sums[cut][:tokens]
        for turn in range(1, SIDE):
            total = total + inboxes[cut][turn * tokens : (turn + 1) * tokens].astype(jnp.float32)
        out_ref[:, start : start + size] = total.astype(jnp.bfloat16)
    pltpu.make_async_copy(tables.at[:, pl.ds(0, 3)], tables.at[:, pl.ds(0, 3)], table_sems.at[0]).wait()
    for cut in range(3):
        settle(lines[cut], 3 * tokens, line_send.at[cut])
        settle(stages[cut], (PLANE - 1) * message, out_send.at[cut])
        settle(stages[cut], (PLANE - 1) * message, home_send.at[cut])
        settle(lines[cut], 3 * tokens, part_send.at[cut])


def routed_experts(normed, mixed, routes, probs, gate_up, down):
    tokens, width = normed.shape
    vmem = pl.BlockSpec(memory_space=pltpu.VMEM)
    kept = pl.BlockSpec(memory_space=pl.ANY)
    slots = SIDE * PLANE * CAP
    flops = 2 * slots * width * (down.shape[1] * 3 + 2 * tokens)
    table = jnp.concatenate([routes.T.astype(jnp.float32), probs.T], axis=0)

    def each(rows, kind):
        return [pltpu.VMEM((rows, size), kind) for start, size in CUTS]

    return pl.pallas_call(
        routed_kernel,
        out_shape=jax.ShapeDtypeStruct(mixed.shape, jnp.bfloat16),
        in_specs=[vmem] * 3 + [kept] * 2,
        out_specs=vmem,
        scratch_shapes=each(SIDE * tokens, jnp.bfloat16)
        + each(slots, jnp.bfloat16)
        + each(slots, jnp.bfloat16)
        + each(slots, jnp.bfloat16)
        + each(SIDE * tokens, jnp.bfloat16)
        + each(SIDE * tokens, jnp.bfloat16)
        + each(SIDE * tokens, jnp.float32)
        + [
            pltpu.VMEM(gate_up.shape[1:], jnp.bfloat16),
            pltpu.VMEM(down.shape[1:], jnp.bfloat16),
            pltpu.VMEM((3, SIDE, 2 * routes.shape[1], tokens), jnp.float32),
            pltpu.VMEM((3 * SIDE * PLANE, tokens), jnp.float32),
            pltpu.VMEM((3 * SIDE * PLANE, tokens), jnp.float32),
            pltpu.VMEM((16 * CAP, tokens), jnp.bfloat16),
            pltpu.VMEM((16 * CAP, width), jnp.bfloat16),
            pltpu.SemaphoreType.DMA((2,)),
            pltpu.SemaphoreType.DMA((2,)),
            pltpu.SemaphoreType.DMA((3,)),
            pltpu.SemaphoreType.DMA((3,)),
            pltpu.SemaphoreType.DMA((3,)),
            pltpu.SemaphoreType.DMA((2, 8)),
            pltpu.SemaphoreType.DMA((2,)),
            pltpu.SemaphoreType.DMA((3,)),
            pltpu.SemaphoreType.DMA((3, 2)),
            pltpu.SemaphoreType.DMA((3,)),
            pltpu.SemaphoreType.DMA((3,)),
        ],
        compiler_params=pltpu.CompilerParams(collective_id=0, has_side_effects=True, vmem_limit_bytes=58 << 20),
        cost_estimate=pl.CostEstimate(flops=flops, bytes_accessed=6 * slots * width * 2, transcendentals=0),
        name="routed_experts",
    )(normed, mixed, table, gate_up, down)


def on_device(
    resid,
    qkv,
    cache_kv,
    page_slot,
    seg_lengths,
    cache_age,
    w_out,
    norm_gain,
    routes,
    route_probs,
    w_gate_up,
    w_down,
):
    ep_count = lax.axis_size("ep")
    tok_dev = resid.shape[0]
    seg_count = seg_lengths.shape[0]
    page_count = cache_kv.shape[0]
    slots = jnp.broadcast_to(
        jnp.pad(page_slot, (0, 2 * HEAD - page_count))[None, :], (META_ROWS, 2 * HEAD)
    ).astype(jnp.bfloat16)
    bank_rows = page_count * PAGE + META_ROWS
    queries, window, bank = exchange(qkv, cache_kv.reshape(page_count * PAGE, 2 * HEAD), slots)
    held = bank.reshape(ep_count, bank_rows, 2 * HEAD)[:, bank_rows - 1, :page_count].astype(jnp.int32)
    slot_row = (
        jnp.arange(ep_count, dtype=jnp.int32)[:, None] * bank_rows
        + jnp.arange(page_count, dtype=jnp.int32)[None, :] * PAGE
    )
    page_match = held.reshape(-1)[None, :] == jnp.arange(seg_count * SEG_PAGES, dtype=jnp.int32)[:, None]
    row_table = jnp.sum(jnp.where(page_match, slot_row.reshape(-1)[None, :], 0), axis=1).astype(jnp.int32)
    seg_ends = jnp.cumsum(seg_lengths)
    blocks = queries.shape[0]
    first_tokens = (group_at(lax.axis_index("ep"), lax.axis_index("tok")) * blocks + jnp.arange(blocks, dtype=jnp.int32)) * tok_dev
    seg_table = jnp.concatenate([seg_ends - seg_lengths, seg_ends, cache_age, first_tokens]).astype(jnp.int32)
    attended = attention(seg_table, row_table, queries, window, bank, seg_count, SEG_MOST)
    mixed, normed = project(attended, w_out, resid, norm_gain)
    return routed_experts(normed, mixed, routes, route_probs, w_gate_up, w_down)


def solution(mesh):
    placed = (
        P(("tok", "ep"), None),
        P(("tok", "ep"), None),
        P("ep", "tok", None, None),
        P("ep"),
        P(),
        P(),
        P("tok", None),
        P(),
        P(("tok", "ep"), None),
        P(("tok", "ep"), None),
        P(("tok", "ep"), None, None),
        P(("tok", "ep"), None, None),
    )
    return jax.shard_map(
        on_device, mesh=mesh, in_specs=placed, out_specs=P(("tok", "ep"), None), check_vma=False
    )
```

```python
import functools
import math

import jax
import jax.numpy as jnp
from jax import lax
from jax.experimental import pallas as pl
from jax.experimental.pallas import tpu as pltpu
from jax.sharding import PartitionSpec as P

D = 2048
FF = 768
HEAD = 128
QPG = 8
TOP = 8
PAGE = 64
SEG_PAGES = 8
SEG_MOST = 2048
STEP = 512
META_ROWS = 16


NEG_FILL = -1e30
NORM_EPS = 1e-06


def attention_kernel(tok_dev, segs, most_steps, seg_ref, row_ref, q_ref, window_ref, bank_ref, out_ref, score_ref, low_ref, top_ref, den_ref, acc_ref):
    rows = tok_dev * QPG
    held_chunks = window_ref.shape[0] // tok_dev
    opening_chunk = seg_ref[3 * segs] // tok_dev - (held_chunks - q_ref.shape[0])
    rate = math.log2(math.e) / math.sqrt(HEAD)

    def tiled(mask):
        return jnp.concatenate([mask] * QPG, axis=0)

    def one_block(block, carry):
        first = seg_ref[3 * segs + block]
        last = first + tok_dev - 1
        token = first + lax.broadcasted_iota(jnp.int32, (tok_dev, STEP), 0)
        column = lax.broadcasted_iota(jnp.int32, (tok_dev, STEP), 1)
        narrow = token[:, :HEAD]
        low = jnp.zeros((tok_dev, HEAD), jnp.int32)
        begin = jnp.int32(0)
        for s in range(segs):
            start = seg_ref[s]
            low = jnp.where(narrow >= start, start, low)
            begin = jnp.where(first >= start, start, begin)
        low_ref[...] = jnp.concatenate([low] * (STEP // HEAD), axis=1)
        query = jnp.concatenate([q_ref[block, :, h * HEAD:(h + 1) * HEAD] for h in range(QPG)], axis=0)
        den_ref[...] = jnp.zeros_like(den_ref)
        acc_ref[...] = jnp.zeros_like(acc_ref)

        def region(bank, steps, bank_of, mask_of, opening):
            if opening:
                held = jnp.full((rows, HEAD), NEG_FILL, jnp.float32)
            else:
                held = top_ref[...]

            def score(step, running):
                keys = jnp.concatenate([bank[pl.ds(at, size), :HEAD] for at, size in bank_of(step)], axis=0)
                scores = lax.dot_general(query, keys, (((1,), (1,)), ((), ())), preferred_element_type=jnp.float32) * rate
                scores = jnp.where(tiled(mask_of(step)), scores, NEG_FILL)
                score_ref[step] = scores
                for part in range(STEP // HEAD):
                    running = jnp.maximum(running, scores[:, part * HEAD : (part + 1) * HEAD])
                return running

            newest = lax.fori_loop(0, steps, score, held)
            newest = jnp.broadcast_to(jnp.max(newest, axis=1, keepdims=True), (rows, HEAD))
            if not opening:
                factor = jnp.exp2(held - newest)
                den_ref[...] = den_ref[...] * factor
                acc_ref[...] = acc_ref[...] * factor
            top_ref[...] = newest

            def weigh(step, ignored):
                top = top_ref[...]
                weights = jnp.exp2(score_ref[step] - jnp.concatenate([top] * (STEP // HEAD), axis=1))
                den_ref[...] += sum([weights[:, part * HEAD : (part + 1) * HEAD] for part in range(STEP // HEAD)])
                values = jnp.concatenate([bank[pl.ds(at, size), HEAD:] for at, size in bank_of(step)], axis=0)
                acc_ref[...] += jnp.dot(weights.astype(jnp.bfloat16), values, preferred_element_type=jnp.float32)
                return ignored

            lax.fori_loop(0, steps, weigh, 0)

        chunk_last = first // tok_dev
        chunk_first = begin // tok_dev
        per = STEP // tok_dev
        steps = (chunk_last - chunk_first + per) // per

        def new_chunk(step, half):
            return chunk_last - per * (step + 1) + 1 + half

        def new_bank(step):
            return [
                (pl.multiple_of(jnp.clip(new_chunk(step, half) - opening_chunk, 0, held_chunks - 1) * tok_dev, tok_dev), tok_dev)
                for half in range(per)
            ]

        def new_mask(step):
            key = new_chunk(step, 0) * tok_dev + column
            return (key >= low_ref[...]) & (key <= token)

        region(window_ref, steps, new_bank, new_mask, True)

        def cached(s, ignored):
            start, end, age = seg_ref[s], seg_ref[segs + s], seg_ref[2 * segs + s]

            @pl.when((start <= last) & (end > first) & (age > 0))
            def _():
                def page_bank(step):
                    return [(pl.multiple_of(row_ref[s * SEG_PAGES + step * (STEP // PAGE) + part], 16), PAGE) for part in range(STEP // PAGE)]

                def page_mask(step):
                    return (token >= start) & (token < end) & (step * STEP + column < age)

                region(bank_ref, (age + STEP - 1) // STEP, page_bank, page_mask, False)
            return ignored

        lax.fori_loop(0, segs, cached, 0)
        total = jnp.sum(den_ref[...], axis=1, keepdims=True)
        result = (acc_ref[...] / total).astype(jnp.bfloat16)
        for h in range(QPG):
            out_ref[block, :, h * HEAD:(h + 1) * HEAD] = result[h * tok_dev:(h + 1) * tok_dev]
        return carry

    lax.fori_loop(0, q_ref.shape[0], one_block, 0)


def attention(seg_table, row_table, queries, window, bank, segs, seg_most):
    blocks, tok_dev, width = queries.shape
    most_steps = max(((seg_most + tok_dev) // tok_dev + STEP // tok_dev - 1) // (STEP // tok_dev), 1)
    rows = tok_dev * QPG
    return pl.pallas_call(
        functools.partial(attention_kernel, tok_dev, segs, most_steps),
        out_shape=jax.ShapeDtypeStruct(queries.shape, jnp.bfloat16),
        in_specs=[pl.BlockSpec(memory_space=pltpu.SMEM)] * 2 + [pl.BlockSpec(memory_space=pltpu.VMEM)] * 3,
        out_specs=pl.BlockSpec(memory_space=pltpu.VMEM),
        scratch_shapes=[
            pltpu.VMEM((most_steps, rows, STEP), jnp.float32),
            pltpu.VMEM((tok_dev, STEP), jnp.int32),
            pltpu.VMEM((rows, HEAD), jnp.float32),
            pltpu.VMEM((rows, HEAD), jnp.float32),
            pltpu.VMEM((rows, HEAD), jnp.float32),
        ],
        compiler_params=pltpu.CompilerParams(vmem_limit_bytes=48 << 20),
        name="attend",
    )(seg_table, row_table, queries, window, bank)


MESH = pl.DeviceIdType.MESH


def place_of(group, head):
    tok, tall, core = lax.div(group, 8), lax.rem(lax.div(group, 2), 4), lax.rem(group, 2)
    return (tall * 4 + lax.rem(tok + head, 4)) * 2 + core


def group_at(ep, head):
    tall, wide, core = lax.div(ep, 8), lax.rem(lax.div(ep, 2), 4), lax.rem(ep, 2)
    return lax.rem(wide + 4 - head, 4) * 8 + 2 * tall + core


def owner_of(group, block):
    tok = lax.div(group, 8)
    return tok, lax.rem(group, 8) * 4 + block


def exchange_kernel(
    qkv_ref, cache_ref, slots_ref, query_ref, window_ref, bank_ref,
    stage_q, stage_kv, load_sems, key_send, key_recv, query_send, query_recv, pass_send, pass_recv, own_sem, line_send, line_recv,
    plane_send, plane_recv, pair_send, pair_recv,
):
    tok, ep = lax.axis_index("tok"), lax.axis_index("ep")
    tok_dev = qkv_ref.shape[0]
    q_width = QPG * HEAD
    number = tok * 32 + ep
    group, block = lax.div(number, 4), lax.rem(number, 4)
    mine = group_at(ep, tok)
    reach = SEG_MOST // (4 * tok_dev)
    span = 4 * tok_dev

    def column(head):
        return head * (q_width + 2 * HEAD)

    def remote(source, place, send_sem, recv_sem, device):
        return pltpu.make_async_remote_copy(
            src_ref=source, dst_ref=place, send_sem=send_sem, recv_sem=recv_sem, device_id=device, device_id_type=MESH
        )

    def load(turn, keys):
        head = lax.rem(tok + turn, 4)
        if keys:
            source = qkv_ref.at[:, pl.ds(pl.multiple_of(column(head) + q_width, HEAD), 2 * HEAD)]
            return pltpu.make_async_copy(source, stage_kv.at[turn], load_sems.at[turn])
        source = qkv_ref.at[:, pl.ds(pl.multiple_of(column(head), HEAD), q_width)]
        return pltpu.make_async_copy(source, stage_q.at[turn], load_sems.at[4 + turn])

    for keys in (True, False):
        for turn in range(4):
            load(turn, keys).start()

    def key_copy(turn):
        head = lax.rem(tok + turn, 4)
        place = window_ref.at[pl.ds(pl.multiple_of(reach * span + block * tok_dev, tok_dev), tok_dev)]
        return stage_kv.at[turn], place, key_send.at[turn], key_recv, (head, place_of(group, head))

    def query_copy(turn):
        head = lax.rem(tok + turn, 4)
        return stage_q.at[turn], query_ref.at[block], query_send.at[turn], query_recv, (head, place_of(group, head))

    def spans(index):
        return window_ref.at[pl.ds(pl.multiple_of(index * span, span), span)]

    def pass_copy(turn):
        device = (tok, place_of(lax.rem(mine + 2 * turn, 32), tok))
        return spans(reach), spans(reach - 2 * turn), pass_send.at[turn - 1], pass_recv.at[turn - 1], device

    def cross_copy(turn):
        device = (tok, at(tall, wide, 1 - core))
        return spans(6 - 2 * turn - 2 * core), spans(5 - 2 * turn), pass_send.at[turn + 1], pass_recv.at[turn + 1], device

    held, told = cache_ref.shape[0], slots_ref.shape[0]
    piece = held + told
    cut = piece // 32 * 16
    tall, wide, core = lax.div(ep, 8), lax.rem(lax.div(ep, 2), 4), lax.rem(ep, 2)

    def at(y, x, c):
        return (lax.rem(y, 4) * 4 + lax.rem(x, 4)) * 2 + c

    def part(y, x, c, start, size):
        return bank_ref.at[pl.ds(pl.multiple_of(at(y, x, c) * piece + start, 16), size)]

    own_cache = pltpu.make_async_copy(cache_ref, part(tall, wide, core, 0, held), own_sem.at[0])
    own_slots = pltpu.make_async_copy(slots_ref, part(tall, wide, core, held, told), own_sem.at[1])
    own_cache.start()
    own_slots.start()

    def line_copies():
        for turn in range(1, 4):
            first = part(tall, wide, core, 0, cut)
            yield remote(first, first, line_send, line_recv, (tok, at(tall, wide + turn, core)))
            rest = part(tall, wide, core, cut, piece - cut)
            yield remote(rest, rest, line_send, line_recv, (tok, at(tall + turn, wide, core)))

    def plane_copies():
        for turn in range(1, 4):
            for along in range(4):
                first = part(tall, wide + along, core, 0, cut)
                yield remote(first, first, plane_send, plane_recv, (tok, at(tall + turn, wide, core)))
                rest = part(tall + along, wide, core, cut, piece - cut)
                yield remote(rest, rest, plane_send, plane_recv, (tok, at(tall, wide + turn, core)))

    def pair_copies():
        for y in range(4):
            for x in range(4):
                whole = part(y, x, core, 0, piece)
                yield remote(whole, whole, pair_send, pair_recv, (tok, at(tall, wide, 1 - core)))

    def settle(rows, sem):
        pltpu.make_async_copy(bank_ref.at[pl.ds(0, rows)], bank_ref.at[pl.ds(0, rows)], sem).wait()

    barrier = pltpu.get_barrier_semaphore()
    at_home = place_of(group, tok) == ep
    for turn in range(1, 4):
        for partner in (at(tall, wide + turn, core), at(tall + turn, wide, core)):
            pl.semaphore_signal(barrier, inc=1, device_id=(tok, partner), device_id_type=MESH)
    pl.semaphore_signal(barrier, inc=1, device_id=(tok, at(tall, wide, 1 - core)), device_id_type=MESH)
    for turn in range(4):
        theirs = owner_of(mine, turn)

        @pl.when(jnp.logical_not((theirs[0] == tok) & (theirs[1] == ep)))
        def _():
            pl.semaphore_signal(barrier, inc=1, device_id=theirs, device_id_type=MESH)

    for turn in range(1, 3):
        pl.semaphore_signal(
            barrier, inc=1, device_id=(tok, place_of(lax.rem(mine + 32 - 2 * turn, 32), tok)), device_id_type=MESH
        )
    pl.semaphore_wait(barrier, 13 - jnp.where(at_home, 1, 0))

    own_cache.wait()
    own_slots.wait()
    for copy in (key_copy, query_copy):
        if copy is query_copy:
            for line_copy in line_copies():
                line_copy.start()
        for turn in range(4):
            source, place, send_sem, recv_sem, device = copy(turn)
            load(turn, copy is key_copy).wait()
            if turn == 0:

                @pl.when(at_home)
                def _():
                    pltpu.make_async_copy(source, place, recv_sem).start()

                @pl.when(jnp.logical_not(at_home))
                def _():
                    remote(source, place, send_sem, recv_sem, device).start()
            else:
                remote(source, place, send_sem, recv_sem, device).start()
    own = window_ref.at[pl.ds(reach * span, span)]
    pltpu.make_async_copy(own, own, key_recv).wait()
    for turn in range(1, 3):
        remote(*pass_copy(turn)).start()
    settle(3 * piece, line_recv)
    for plane_copy in plane_copies():
        plane_copy.start()
    settle(12 * piece, plane_recv)
    for pair_copy in pair_copies():
        pair_copy.start()
    for turn in range(1, 3):
        remote(*pass_copy(turn)).wait()
    for turn in range(1, 3):
        remote(*cross_copy(turn)).start()
    for turn in range(1, 3):
        remote(*cross_copy(turn)).wait()
    pltpu.make_async_copy(query_ref, query_ref, query_recv).wait()
    for copy in (key_copy, query_copy):
        for turn in range(4):
            if turn == 0:

                @pl.when(jnp.logical_not(at_home))
                def _():
                    remote(*copy(turn)).wait_send()
            else:
                remote(*copy(turn)).wait_send()
    settle(16 * piece, pair_recv)
    settle(3 * piece, line_send)
    settle(12 * piece, plane_send)
    settle(16 * piece, pair_send)


def exchange(qkv, cached, slots):
    tok_dev = qkv.shape[0]
    reach = SEG_MOST // (4 * tok_dev)
    kept = pl.BlockSpec(memory_space=pl.ANY)
    return pl.pallas_call(
        exchange_kernel,
        out_shape=(
            jax.ShapeDtypeStruct((4, tok_dev, QPG * HEAD), jnp.bfloat16),
            jax.ShapeDtypeStruct(((reach + 1) * 4 * tok_dev, 2 * HEAD), jnp.bfloat16),
            jax.ShapeDtypeStruct((32 * (cached.shape[0] + slots.shape[0]), 2 * HEAD), jnp.bfloat16),
        ),
        in_specs=[kept] * 3,
        out_specs=(kept,) * 3,
        scratch_shapes=[
            pltpu.VMEM((4, tok_dev, QPG * HEAD), jnp.bfloat16),
            pltpu.VMEM((4, tok_dev, 2 * HEAD), jnp.bfloat16),
            pltpu.SemaphoreType.DMA((8,)),
            pltpu.SemaphoreType.DMA((4,)),
            pltpu.SemaphoreType.DMA,
            pltpu.SemaphoreType.DMA((4,)),
            pltpu.SemaphoreType.DMA,
            pltpu.SemaphoreType.DMA((4,)),
            pltpu.SemaphoreType.DMA((4,)),
            pltpu.SemaphoreType.DMA((2,)),
        ]
        + [pltpu.SemaphoreType.DMA] * 6,
        compiler_params=pltpu.CompilerParams(collective_id=1, has_side_effects=True),
        cost_estimate=pl.CostEstimate(flops=0, bytes_accessed=80 << 20, transcendentals=0),
        name="exchange",
    )(qkv, cached, slots)


CAP = 16
SIDE = 4
PLANE = 32
CUTS = ((0, 768), (768, 640), (1408, 640))


def position():
    tok, ep = lax.axis_index("tok"), lax.axis_index("ep")
    return tok, lax.div(ep, 8), lax.rem(lax.div(ep, 2), 4), lax.rem(ep, 2)


def moved(offsets, way):
    at = [lax.rem(own + size + way * off, size) for own, off, size in zip(position(), offsets, (4, 4, 4, 2))]
    return at[0], (at[1] * 4 + at[2]) * 2 + at[3]


def plane_offsets(cut, index, div, rem):
    core, outer, inner = div(index, 16), rem(div(index, 4), 4), rem(index, 4)
    return ((0, inner, outer, core), (inner, 0, outer, core), (outer, inner, 0, core))[cut]


def line_offsets(cut, turn):
    return tuple(turn if axis == cut else 0 for axis in range(3)) + (0,)


def routed_kernel(
    attended_ref, weight_ref, resid_ref, gain_ref, table_ref, gate_up_hbm, down_hbm, out_ref,
    projected, heads, mixed_ref,
    line0, line1, line2, stage0, stage1, stage2, came0, came1, came2, back0, back1, back2,
    inbox0, inbox1, inbox2, sum0, sum1, sum2,
    gate_up, down, tables, rank, share, pick, rows_in,
    weight_sems, table_sems, line_send, line_recv, out_send, near_recv, far_recv, home_send, home_recv,
    part_send, part_recv, head_send, head_recv,
):
    lines, stages, cames, backs = (line0, line1, line2), (stage0, stage1, stage2), (came0, came1, came2), (back0, back1, back2)
    inboxes, sums = (inbox0, inbox1, inbox2), (sum0, sum1, sum2)
    tokens = resid_ref.shape[0]
    width = down.shape[0]
    devices = SIDE * PLANE
    message = SIDE * CAP
    load_gate_up = pltpu.make_async_copy(gate_up_hbm.at[0], gate_up, weight_sems.at[0])
    load_down = pltpu.make_async_copy(down_hbm.at[0], down, weight_sems.at[1])
    load_gate_up.start()
    load_down.start()
    barrier = pltpu.get_barrier_semaphore()

    def greet(step, ignored):
        offsets = (lax.div(step, 32), lax.rem(lax.div(step, 8), 4), lax.rem(lax.div(step, 2), 4), lax.rem(step, 2))
        pl.semaphore_signal(barrier, inc=1, device_id=moved(offsets, 1), device_id_type=MESH)
        return ignored

    lax.fori_loop(1, devices, greet, 0)
    for cut in range(3):
        tables[cut, 0] = table_ref[...]
    tok, ep = lax.axis_index("tok"), lax.axis_index("ep")
    mine = group_at(ep, tok)
    home = [owner_of(mine, turn) for turn in range(4)]
    is_own = [(place[0] == tok) & (place[1] == ep) for place in home]

    def project(turn):
        projected[turn] = jnp.dot(
            attended_ref[turn], weight_ref[...], preferred_element_type=jnp.float32
        ).astype(jnp.bfloat16)

    project(0)
    pl.semaphore_wait(barrier, devices - 1)

    def remote(source, place, send_sem, recv_sem, device):
        return pltpu.make_async_remote_copy(
            src_ref=source, dst_ref=place, send_sem=send_sem, recv_sem=recv_sem, device_id=device, device_id_type=MESH
        )

    def rows_of(ref, start, size):
        return ref.at[pl.ds(pl.multiple_of(start, CAP), size)]

    def settle(ref, size, sem):
        pltpu.make_async_copy(ref.at[pl.ds(0, size)], ref.at[pl.ds(0, size)], sem).wait()

    for cut in range(3):
        for turn in range(1, SIDE):
            remote(
                table_ref, tables.at[cut, turn], table_sems.at[0], table_sems.at[1], moved(line_offsets(cut, turn), 1)
            ).start()
    def head_copy(turn):
        return remote(projected.at[turn], heads.at[tok], head_send.at[turn], head_recv, home[turn])

    for turn in range(4):
        if turn:
            project(turn)

        @pl.when(is_own[turn])
        def _():
            pltpu.make_async_copy(projected.at[turn], heads.at[tok], head_recv).start()

        @pl.when(jnp.logical_not(is_own[turn]))
        def _():
            head_copy(turn).start()

    pltpu.make_async_copy(tables.at[:, pl.ds(0, 3)], tables.at[:, pl.ds(0, 3)], table_sems.at[1]).wait()
    before = (
        lax.broadcasted_iota(jnp.int32, (tokens, tokens), 0) < lax.broadcasted_iota(jnp.int32, (tokens, tokens), 1)
    ).astype(jnp.bfloat16)
    index = lax.broadcasted_iota(jnp.int32, (PLANE, tokens), 0)
    shift = {16: 4, 4: 2}
    top = table_ref.shape[0] // 2
    for cut in range(3):
        offsets = plane_offsets(cut, index, lambda v, d: v >> shift[d], lambda v, d: v & (d - 1))
        z, y, x, c = [(own + off) & (size - 1) for own, off, size in zip(position(), offsets, (4, 4, 4, 2))]
        expert = (z * 32 + y * 8 + x * 2 + c).astype(jnp.float32)
        for turn in range(SIDE):
            probs = tables[cut, turn, top:, :]
            shares = probs / jnp.sum(probs, axis=0, keepdims=True)
            named = jnp.zeros((PLANE, tokens), jnp.float32)
            owed = jnp.zeros((PLANE, tokens), jnp.float32)
            for k in range(top):
                match = expert == tables[cut, turn, k : k + 1, :]
                named = jnp.where(match, 1.0, named)
                owed = jnp.where(match, shares[k : k + 1, :], owed)
            earlier = jnp.dot(named.astype(jnp.bfloat16), before, preferred_element_type=jnp.float32)
            at = (cut * SIDE + turn) * PLANE
            rank[at : at + PLANE, :] = jnp.where(named > 0.0, earlier, -1.0)
            share[at : at + PLANE, :] = owed

    pltpu.make_async_copy(heads, heads, head_recv).wait()
    added = resid_ref[...].astype(jnp.float32)
    for head in range(4):
        added = added + heads[head].astype(jnp.float32)
    mixed_ref[...] = added.astype(jnp.bfloat16)
    wide = mixed_ref[...].astype(jnp.float32)
    level = lax.rsqrt(jnp.mean(wide * wide, axis=-1, keepdims=True) + NORM_EPS)
    for cut, (start, size) in enumerate(CUTS):
        part = mixed_ref[:, start : start + size].astype(jnp.float32)
        lines[cut][:tokens] = (part * level * gain_ref[:, start : start + size]).astype(jnp.bfloat16)
        for turn in range(1, SIDE):
            remote(
                rows_of(lines[cut], 0, tokens), rows_of(lines[cut], turn * tokens, tokens),
                line_send.at[cut], line_recv.at[cut], moved(line_offsets(cut, turn), 1),
            ).start()

    slot = lax.broadcasted_iota(jnp.int32, (CAP, tokens), 0).astype(jnp.float32)

    def choose(cut, core, turn, weighted):
        for j in range(16):
            at = (cut * SIDE + turn) * PLANE + core * 16 + j
            chosen = share[pl.ds(at, 1), :] if weighted else 1.0
            pick[j * CAP : (j + 1) * CAP, :] = jnp.where(rank[pl.ds(at, 1), :] == slot, chosen, 0.0).astype(jnp.bfloat16)

    def send(cut, i, recv_sem):
        source, place = rows_of(stages[cut], i * message, message), rows_of(cames[cut], i * message, message)
        offsets = plane_offsets(cut, i, lax.div, lax.rem)

        @pl.when(i == 0)
        def _():
            pltpu.make_async_copy(source, place, recv_sem).start()

        @pl.when(i > 0)
        def _():
            remote(source, place, out_send.at[cut], recv_sem, moved(offsets, 1)).start()

    def fill(cut, core):
        def one_shard(turn, ignored):
            choose(cut, core, turn, False)
            found = jnp.dot(
                pick[...], rows_of(lines[cut], turn * tokens, tokens)[...], preferred_element_type=jnp.float32
            ).astype(jnp.bfloat16)
            for j in range(16):
                rows_of(stages[cut], (core * 16 + j) * message + turn * CAP, CAP)[...] = found[j * CAP : (j + 1) * CAP]
            return ignored

        lax.fori_loop(0, SIDE, one_shard, 0)

    def dispatch(core, ignored):
        fill(2, core)

        def send_far(j, inner):
            send(2, core * 16 + j, far_recv.at[core])
            return inner

        lax.fori_loop(0, 16, send_far, 0)
        fill(0, core)
        fill(1, core)

        def send_near(j, inner):
            chunk = core * 4 + lax.div(j, 4)
            send(0, core * 16 + j, near_recv.at[0, chunk])
            send(1, core * 16 + j, near_recv.at[1, chunk])
            return inner

        return lax.fori_loop(0, 16, send_near, ignored)

    for cut in range(3):
        settle(lines[cut], 3 * tokens, line_recv.at[cut])
        settle(lines[cut], 3 * tokens, line_send.at[cut])
    lax.fori_loop(0, 2, dispatch, 0)
    load_gate_up.wait()
    load_down.wait()
    block = SIDE * message

    def slab1(chunk, j):
        return rows_of(came1, chunk * block + (j % 4) * message + (j // 4) * CAP, CAP)

    def slab2(chunk, j):
        core, wide = lax.div(chunk, 4), lax.rem(chunk, 4)
        return rows_of(came2, (core * 16 + (j % 4) * 4 + j // 4) * message + wide * CAP, CAP)

    def give(cut, i):
        source, place = rows_of(cames[cut], i * message, message), rows_of(backs[cut], i * message, message)
        offsets = plane_offsets(cut, i, lax.div, lax.rem)
        recv_sem = home_recv.at[cut, lax.div(i, 16)]

        @pl.when(i == 0)
        def _():
            pltpu.make_async_copy(source, place, recv_sem).start()

        @pl.when(i > 0)
        def _():
            remote(source, place, home_send.at[cut], recv_sem, moved(offsets, -1)).start()

    def work(chunk, ignored):
        @pl.when(lax.rem(chunk, 4) == 0)
        def _():
            settle(came2, 16 * message, far_recv.at[lax.div(chunk, 4)])

        settle(came0, block, near_recv.at[0, chunk])
        settle(came1, block, near_recv.at[1, chunk])
        rows_in[:, 0:768] = rows_of(came0, chunk * block, block)[...]
        for j in range(16):
            rows_in[j * CAP : (j + 1) * CAP, 768:1408] = slab1(chunk, j)[...]
            rows_in[j * CAP : (j + 1) * CAP, 1408:2048] = slab2(chunk, j)[...]
        gate = jnp.dot(rows_in[...], gate_up[:, :width], preferred_element_type=jnp.float32)
        up = jnp.dot(rows_in[...], gate_up[:, width:], preferred_element_type=jnp.float32)
        hidden = (gate * jax.nn.sigmoid(gate) * up).astype(jnp.bfloat16)
        made = jnp.dot(hidden, down[...], preferred_element_type=jnp.float32).astype(jnp.bfloat16)
        rows_of(came0, chunk * block, block)[...] = made[:, 0:768]
        for j in range(16):
            slab1(chunk, j)[...] = made[j * CAP : (j + 1) * CAP, 768:1408]
            slab2(chunk, j)[...] = made[j * CAP : (j + 1) * CAP, 1408:2048]

        def give_near(j, inner):
            give(0, chunk * 4 + j)
            give(1, chunk * 4 + j)
            return inner

        lax.fori_loop(0, 4, give_near, 0)

        @pl.when(lax.rem(chunk, 4) == 3)
        def _():
            def give_far(j, inner):
                give(2, lax.div(chunk, 4) * 16 + j)
                return inner

            lax.fori_loop(0, 16, give_far, 0)

        return ignored

    lax.fori_loop(0, 8, work, 0)

    for cut in range(3):
        sums[cut][...] = jnp.zeros_like(sums[cut])

    def combine(core, ignored):
        for cut in range(3):
            settle(backs[cut], 16 * message, home_recv.at[cut, core])

            def one_shard(turn, inner):
                choose(cut, core, turn, True)
                found = jnp.concatenate(
                    [rows_of(backs[cut], (core * 16 + j) * message + turn * CAP, CAP)[...] for j in range(16)], axis=0
                )
                total = rows_of(sums[cut], turn * tokens, tokens)
                total[...] += lax.dot_general(
                    pick[...], found, (((0,), (0,)), ((), ())), preferred_element_type=jnp.float32
                )
                return inner

            lax.fori_loop(0, SIDE, one_shard, 0)

            @pl.when(core == 1)
            def _():
                lines[cut][...] = sums[cut][...].astype(jnp.bfloat16)
                for turn in range(1, SIDE):
                    remote(
                        rows_of(lines[cut], turn * tokens, tokens), rows_of(inboxes[cut], turn * tokens, tokens),
                        part_send.at[cut], part_recv.at[cut], moved(line_offsets(cut, turn), -1),
                    ).start()

        return ignored

    lax.fori_loop(0, 2, combine, 0)
    for cut, (start, size) in enumerate(CUTS):
        settle(inboxes[cut], 3 * tokens, part_recv.at[cut])
        total = mixed_ref[:, start : start + size].astype(jnp.float32) + sums[cut][:tokens]
        for turn in range(1, SIDE):
            total = total + inboxes[cut][turn * tokens : (turn + 1) * tokens].astype(jnp.float32)
        out_ref[:, start : start + size] = total.astype(jnp.bfloat16)
    pltpu.make_async_copy(tables.at[:, pl.ds(0, 3)], tables.at[:, pl.ds(0, 3)], table_sems.at[0]).wait()
    for cut in range(3):
        settle(stages[cut], (PLANE - 1) * message, out_send.at[cut])
        settle(stages[cut], (PLANE - 1) * message, home_send.at[cut])
        settle(lines[cut], 3 * tokens, part_send.at[cut])
    for turn in range(4):

        @pl.when(jnp.logical_not(is_own[turn]))
        def _():
            head_copy(turn).wait_send()


def routed_experts(attended, weight, resid, gain, routes, probs, gate_up, down):
    tokens, width = resid.shape
    vmem = pl.BlockSpec(memory_space=pltpu.VMEM)
    kept = pl.BlockSpec(memory_space=pl.ANY)
    slots = SIDE * PLANE * CAP
    flops = 2 * slots * width * (down.shape[1] * 3 + 2 * tokens)
    table = jnp.concatenate([routes.T.astype(jnp.float32), probs.T], axis=0)

    def each(rows, kind):
        return [pltpu.VMEM((rows, size), kind) for start, size in CUTS]

    return pl.pallas_call(
        routed_kernel,
        out_shape=jax.ShapeDtypeStruct(resid.shape, jnp.bfloat16),
        in_specs=[vmem] * 5 + [kept] * 2,
        out_specs=vmem,
        scratch_shapes=[
            pltpu.VMEM((4, tokens, width), jnp.bfloat16),
            pltpu.VMEM((4, tokens, width), jnp.bfloat16),
            pltpu.VMEM((tokens, width), jnp.bfloat16),
        ]
        + each(SIDE * tokens, jnp.bfloat16)
        + each(slots, jnp.bfloat16)
        + each(slots, jnp.bfloat16)
        + each(slots, jnp.bfloat16)
        + each(SIDE * tokens, jnp.bfloat16)
        + each(SIDE * tokens, jnp.float32)
        + [
            pltpu.VMEM(gate_up.shape[1:], jnp.bfloat16),
            pltpu.VMEM(down.shape[1:], jnp.bfloat16),
            pltpu.VMEM((3, SIDE, 2 * routes.shape[1], tokens), jnp.float32),
            pltpu.VMEM((3 * SIDE * PLANE, tokens), jnp.float32),
            pltpu.VMEM((3 * SIDE * PLANE, tokens), jnp.float32),
            pltpu.VMEM((16 * CAP, tokens), jnp.bfloat16),
            pltpu.VMEM((16 * CAP, width), jnp.bfloat16),
            pltpu.SemaphoreType.DMA((2,)),
            pltpu.SemaphoreType.DMA((2,)),
            pltpu.SemaphoreType.DMA((3,)),
            pltpu.SemaphoreType.DMA((3,)),
            pltpu.SemaphoreType.DMA((3,)),
            pltpu.SemaphoreType.DMA((2, 8)),
            pltpu.SemaphoreType.DMA((2,)),
            pltpu.SemaphoreType.DMA((3,)),
            pltpu.SemaphoreType.DMA((3, 2)),
            pltpu.SemaphoreType.DMA((3,)),
            pltpu.SemaphoreType.DMA((3,)),
            pltpu.SemaphoreType.DMA((4,)),
            pltpu.SemaphoreType.DMA,
        ],
        compiler_params=pltpu.CompilerParams(collective_id=0, has_side_effects=True, vmem_limit_bytes=62 << 20),
        cost_estimate=pl.CostEstimate(flops=flops, bytes_accessed=6 * slots * width * 2, transcendentals=0),
        name="routed_experts",
    )(attended, weight, resid, gain[None, :], table, gate_up, down)


def on_device(
    resid,
    qkv,
    cache_kv,
    page_slot,
    seg_lengths,
    cache_age,
    w_out,
    norm_gain,
    routes,
    route_probs,
    w_gate_up,
    w_down,
):
    ep_count = lax.axis_size("ep")
    tok_dev = resid.shape[0]
    seg_count = seg_lengths.shape[0]
    page_count = cache_kv.shape[0]
    slots = jnp.broadcast_to(
        jnp.pad(page_slot, (0, 2 * HEAD - page_count))[None, :], (META_ROWS, 2 * HEAD)
    ).astype(jnp.bfloat16)
    bank_rows = page_count * PAGE + META_ROWS
    queries, window, bank = exchange(qkv, cache_kv.reshape(page_count * PAGE, 2 * HEAD), slots)
    held = bank.reshape(ep_count, bank_rows, 2 * HEAD)[:, bank_rows - 1, :page_count].astype(jnp.int32)
    slot_row = (
        jnp.arange(ep_count, dtype=jnp.int32)[:, None] * bank_rows
        + jnp.arange(page_count, dtype=jnp.int32)[None, :] * PAGE
    )
    page_match = held.reshape(-1)[None, :] == jnp.arange(seg_count * SEG_PAGES, dtype=jnp.int32)[:, None]
    row_table = jnp.sum(jnp.where(page_match, slot_row.reshape(-1)[None, :], 0), axis=1).astype(jnp.int32)
    seg_ends = jnp.cumsum(seg_lengths)
    blocks = queries.shape[0]
    first_tokens = (group_at(lax.axis_index("ep"), lax.axis_index("tok")) * blocks + jnp.arange(blocks, dtype=jnp.int32)) * tok_dev
    seg_table = jnp.concatenate([seg_ends - seg_lengths, seg_ends, cache_age, first_tokens]).astype(jnp.int32)
    attended = attention(seg_table, row_table, queries, window, bank, seg_count, SEG_MOST)
    return routed_experts(attended, w_out, resid, norm_gain, routes, route_probs, w_gate_up, w_down)


def solution(mesh):
    placed = (
        P(("tok", "ep"), None),
        P(("tok", "ep"), None),
        P("ep", "tok", None, None),
        P("ep"),
        P(),
        P(),
        P("tok", None),
        P(),
        P(("tok", "ep"), None),
        P(("tok", "ep"), None),
        P(("tok", "ep"), None, None),
        P(("tok", "ep"), None, None),
    )
    return jax.shard_map(
        on_device, mesh=mesh, in_specs=placed, out_specs=P(("tok", "ep"), None), check_vma=False
    )
```

```python
import functools
import math

import jax
import jax.numpy as jnp
from jax import lax
from jax.experimental import pallas as pl
from jax.experimental.pallas import tpu as pltpu
from jax.sharding import PartitionSpec as P

D = 2048
FF = 768
HEAD = 128
QPG = 8
TOP = 8
PAGE = 64
SEG_PAGES = 8
SEG_MOST = 2048
STEP = 512
META_ROWS = 16


NEG_FILL = -1e30
NORM_EPS = 1e-06


def attention_kernel(tok_dev, segs, lengths_ref, age_ref, row_ref, q_hbm, window_hbm, bank_hbm, out_ref, q_ref, window_ref, bank_ref, load_sems, seg_ref, score_ref, low_ref, top_ref, den_ref, acc_ref):
    load_q = pltpu.make_async_copy(q_hbm, q_ref, load_sems.at[0])
    load_window = pltpu.make_async_copy(window_hbm, window_ref, load_sems.at[1])
    load_bank = pltpu.make_async_copy(bank_hbm, bank_ref, load_sems.at[2])
    load_q.start()
    load_window.start()
    load_bank.start()
    begins = jnp.int32(0)
    for s in range(segs):
        seg_ref[s] = begins
        begins = begins + lengths_ref[s]
        seg_ref[segs + s] = begins
        seg_ref[2 * segs + s] = age_ref[s]
    seg_ref[3 * segs] = group_at(lax.axis_index("ep"), lax.axis_index("tok")) * q_ref.shape[0] * tok_dev
    rows = tok_dev * QPG
    held_chunks = window_ref.shape[0] // tok_dev
    opening_chunk = seg_ref[3 * segs] // tok_dev - (held_chunks - q_ref.shape[0])
    rate = math.log2(math.e) / math.sqrt(HEAD)

    def tiled(mask):
        return jnp.concatenate([mask] * QPG, axis=0)

    def one_block(block, carry):
        first = seg_ref[3 * segs] + block * tok_dev
        last = first + tok_dev - 1
        token = first + lax.broadcasted_iota(jnp.int32, (tok_dev, STEP), 0)
        column = lax.broadcasted_iota(jnp.int32, (tok_dev, STEP), 1)
        narrow = token[:, :HEAD]
        low = jnp.zeros((tok_dev, HEAD), jnp.int32)
        begin = jnp.int32(0)
        for s in range(segs):
            start = seg_ref[s]
            low = jnp.where(narrow >= start, start, low)
            begin = jnp.where(first >= start, start, begin)
        low_ref[...] = jnp.concatenate([low] * (STEP // HEAD), axis=1)
        query = jnp.concatenate([q_ref[block, :, h * HEAD:(h + 1) * HEAD] for h in range(QPG)], axis=0)
        den_ref[...] = jnp.zeros_like(den_ref)
        acc_ref[...] = jnp.zeros_like(acc_ref)

        def region(bank, steps, bank_of, mask_of, opening):
            if opening:
                held = jnp.full((rows, HEAD), NEG_FILL, jnp.float32)
            else:
                held = top_ref[...]

            def score(step, running):
                keys = jnp.concatenate([bank[pl.ds(at, size), :HEAD] for at, size in bank_of(step)], axis=0)
                scores = lax.dot_general(query, keys, (((1,), (1,)), ((), ())), preferred_element_type=jnp.float32) * rate
                scores = jnp.where(tiled(mask_of(step)), scores, NEG_FILL)
                score_ref[step] = scores
                for part in range(STEP // HEAD):
                    running = jnp.maximum(running, scores[:, part * HEAD : (part + 1) * HEAD])
                return running

            newest = lax.fori_loop(0, steps, score, held)
            newest = jnp.broadcast_to(jnp.max(newest, axis=1, keepdims=True), (rows, HEAD))
            if not opening:
                factor = jnp.exp2(held - newest)
                den_ref[...] = den_ref[...] * factor
                acc_ref[...] = acc_ref[...] * factor
            top_ref[...] = newest

            def weigh(step, ignored):
                top = top_ref[...]
                weights = jnp.exp2(score_ref[step] - jnp.concatenate([top] * (STEP // HEAD), axis=1))
                den_ref[...] += sum([weights[:, part * HEAD : (part + 1) * HEAD] for part in range(STEP // HEAD)])
                values = jnp.concatenate([bank[pl.ds(at, size), HEAD:] for at, size in bank_of(step)], axis=0)
                acc_ref[...] += jnp.dot(weights.astype(jnp.bfloat16), values, preferred_element_type=jnp.float32)
                return ignored

            lax.fori_loop(0, steps, weigh, 0)

        chunk_last = first // tok_dev
        chunk_first = begin // tok_dev
        per = STEP // tok_dev
        steps = (chunk_last - chunk_first + per) // per

        def new_chunk(step, half):
            return chunk_last - per * (step + 1) + 1 + half

        def new_bank(step):
            return [
                (pl.multiple_of(jnp.clip(new_chunk(step, half) - opening_chunk, 0, held_chunks - 1) * tok_dev, tok_dev), tok_dev)
                for half in range(per)
            ]

        def new_mask(step):
            key = new_chunk(step, 0) * tok_dev + column
            return (key >= low_ref[...]) & (key <= token)

        region(window_ref, steps, new_bank, new_mask, True)

        def cached(s, ignored):
            start, end, age = seg_ref[s], seg_ref[segs + s], seg_ref[2 * segs + s]

            @pl.when((start <= last) & (end > first) & (age > 0))
            def _():
                def page_bank(step):
                    return [(pl.multiple_of(row_ref[s * SEG_PAGES + step * (STEP // PAGE) + part], 16), PAGE) for part in range(STEP // PAGE)]

                def page_mask(step):
                    return (token >= start) & (token < end) & (step * STEP + column < age)

                region(bank_ref, (age + STEP - 1) // STEP, page_bank, page_mask, False)
            return ignored

        @pl.when(block == 0)
        def _():
            load_bank.wait()

        lax.fori_loop(0, segs, cached, 0)
        total = jnp.sum(den_ref[...], axis=1, keepdims=True)
        result = (acc_ref[...] / total).astype(jnp.bfloat16)
        for h in range(QPG):
            out_ref[block, :, h * HEAD:(h + 1) * HEAD] = result[h * tok_dev:(h + 1) * tok_dev]
        return carry

    load_q.wait()
    load_window.wait()
    lax.fori_loop(0, q_ref.shape[0], one_block, 0)


def attention(seg_lengths, cache_age, row_table, queries, window, bank, segs, seg_most):
    blocks, tok_dev, width = queries.shape
    most_steps = max(((seg_most + tok_dev) // tok_dev + STEP // tok_dev - 1) // (STEP // tok_dev), 1)
    rows = tok_dev * QPG
    return pl.pallas_call(
        functools.partial(attention_kernel, tok_dev, segs),
        out_shape=jax.ShapeDtypeStruct(queries.shape, jnp.bfloat16),
        in_specs=[pl.BlockSpec(memory_space=pltpu.SMEM)] * 3 + [pl.BlockSpec(memory_space=pl.ANY)] * 3,
        out_specs=pl.BlockSpec(memory_space=pltpu.VMEM),
        scratch_shapes=[
            pltpu.VMEM(queries.shape, jnp.bfloat16),
            pltpu.VMEM(window.shape, jnp.bfloat16),
            pltpu.VMEM(bank.shape, jnp.bfloat16),
            pltpu.SemaphoreType.DMA((3,)),
            pltpu.SMEM((3 * segs + 1,), jnp.int32),
            pltpu.VMEM((most_steps, rows, STEP), jnp.float32),
            pltpu.VMEM((tok_dev, STEP), jnp.int32),
            pltpu.VMEM((rows, HEAD), jnp.float32),
            pltpu.VMEM((rows, HEAD), jnp.float32),
            pltpu.VMEM((rows, HEAD), jnp.float32),
        ],
        compiler_params=pltpu.CompilerParams(vmem_limit_bytes=62 << 20),
        name="attend",
    )(seg_lengths, cache_age, row_table, queries, window, bank)


MESH = pl.DeviceIdType.MESH


def place_of(group, head):
    tok, tall, core = lax.div(group, 8), lax.rem(lax.div(group, 2), 4), lax.rem(group, 2)
    return (tall * 4 + lax.rem(tok + head, 4)) * 2 + core


def group_at(ep, head):
    tall, wide, core = lax.div(ep, 8), lax.rem(lax.div(ep, 2), 4), lax.rem(ep, 2)
    return lax.rem(wide + 4 - head, 4) * 8 + 2 * tall + core


def owner_of(group, block):
    tok = lax.div(group, 8)
    return tok, lax.rem(group, 8) * 4 + block


def exchange_kernel(
    qkv_ref, cache_ref, slots_ref, query_ref, window_ref, bank_ref,
    stage_q, stage_kv, stage_slots, load_sems, key_send, key_recv, query_send, query_recv, pass_send, pass_recv, own_sem, line_send, line_recv,
    plane_send, plane_recv, pair_send, pair_recv,
):
    tok, ep = lax.axis_index("tok"), lax.axis_index("ep")
    tok_dev = qkv_ref.shape[0]
    q_width = QPG * HEAD
    number = tok * 32 + ep
    group, block = lax.div(number, 4), lax.rem(number, 4)
    mine = group_at(ep, tok)
    reach = SEG_MOST // (4 * tok_dev)
    span = 4 * tok_dev

    def column(head):
        return head * (q_width + 2 * HEAD)

    def remote(source, place, send_sem, recv_sem, device):
        return pltpu.make_async_remote_copy(
            src_ref=source, dst_ref=place, send_sem=send_sem, recv_sem=recv_sem, device_id=device, device_id_type=MESH
        )

    def load(turn, keys):
        head = lax.rem(tok + turn, 4)
        if keys:
            source = qkv_ref.at[:, pl.ds(pl.multiple_of(column(head) + q_width, HEAD), 2 * HEAD)]
            return pltpu.make_async_copy(source, stage_kv.at[turn], load_sems.at[turn])
        source = qkv_ref.at[:, pl.ds(pl.multiple_of(column(head), HEAD), q_width)]
        return pltpu.make_async_copy(source, stage_q.at[turn], load_sems.at[4 + turn])

    for keys in (True, False):
        for turn in range(4):
            load(turn, keys).start()

    def key_copy(turn):
        head = lax.rem(tok + turn, 4)
        place = window_ref.at[pl.ds(pl.multiple_of(reach * span + block * tok_dev, tok_dev), tok_dev)]
        return stage_kv.at[turn], place, key_send.at[turn], key_recv, (head, place_of(group, head))

    def query_copy(turn):
        head = lax.rem(tok + turn, 4)
        return stage_q.at[turn], query_ref.at[block], query_send.at[turn], query_recv, (head, place_of(group, head))

    def spans(index):
        return window_ref.at[pl.ds(pl.multiple_of(index * span, span), span)]

    def pass_copy(turn):
        device = (tok, place_of(lax.rem(mine + 2 * turn, 32), tok))
        return spans(reach), spans(reach - 2 * turn), pass_send.at[turn - 1], pass_recv.at[turn - 1], device

    def cross_copy(turn):
        device = (tok, at(tall, wide, 1 - core))
        return spans(6 - 2 * turn - 2 * core), spans(5 - 2 * turn), pass_send.at[turn + 1], pass_recv.at[turn + 1], device

    held, told = cache_ref.shape[0], stage_slots.shape[0]
    piece = held + told
    cut = piece // 32 * 16
    tall, wide, core = lax.div(ep, 8), lax.rem(lax.div(ep, 2), 4), lax.rem(ep, 2)

    def at(y, x, c):
        return (lax.rem(y, 4) * 4 + lax.rem(x, 4)) * 2 + c

    def part(y, x, c, start, size):
        return bank_ref.at[pl.ds(pl.multiple_of(at(y, x, c) * piece + start, 16), size)]

    lane = lax.broadcasted_iota(jnp.int32, stage_slots.shape, 1)
    listed = jnp.zeros(stage_slots.shape, jnp.float32)
    for page in range(slots_ref.shape[0]):
        listed = jnp.where(lane == page, slots_ref[page].astype(jnp.float32), listed)
    stage_slots[...] = listed.astype(jnp.bfloat16)
    own_cache = pltpu.make_async_copy(cache_ref, part(tall, wide, core, 0, held), own_sem.at[0])
    own_slots = pltpu.make_async_copy(stage_slots, part(tall, wide, core, held, told), own_sem.at[1])
    own_cache.start()
    own_slots.start()

    def line_copies():
        for turn in range(1, 4):
            first = part(tall, wide, core, 0, cut)
            yield remote(first, first, line_send, line_recv, (tok, at(tall, wide + turn, core)))
            rest = part(tall, wide, core, cut, piece - cut)
            yield remote(rest, rest, line_send, line_recv, (tok, at(tall + turn, wide, core)))

    def plane_copies():
        for turn in range(1, 4):
            for along in range(4):
                first = part(tall, wide + along, core, 0, cut)
                yield remote(first, first, plane_send, plane_recv, (tok, at(tall + turn, wide, core)))
                rest = part(tall + along, wide, core, cut, piece - cut)
                yield remote(rest, rest, plane_send, plane_recv, (tok, at(tall, wide + turn, core)))

    def pair_copies():
        for y in range(4):
            for x in range(4):
                whole = part(y, x, core, 0, piece)
                yield remote(whole, whole, pair_send, pair_recv, (tok, at(tall, wide, 1 - core)))

    def settle(rows, sem):
        pltpu.make_async_copy(bank_ref.at[pl.ds(0, rows)], bank_ref.at[pl.ds(0, rows)], sem).wait()

    barrier = pltpu.get_barrier_semaphore()
    at_home = place_of(group, tok) == ep
    for turn in range(1, 4):
        for partner in (at(tall, wide + turn, core), at(tall + turn, wide, core)):
            pl.semaphore_signal(barrier, inc=1, device_id=(tok, partner), device_id_type=MESH)
    pl.semaphore_signal(barrier, inc=1, device_id=(tok, at(tall, wide, 1 - core)), device_id_type=MESH)
    for turn in range(4):
        theirs = owner_of(mine, turn)

        @pl.when(jnp.logical_not((theirs[0] == tok) & (theirs[1] == ep)))
        def _():
            pl.semaphore_signal(barrier, inc=1, device_id=theirs, device_id_type=MESH)

    for turn in range(1, 3):
        pl.semaphore_signal(
            barrier, inc=1, device_id=(tok, place_of(lax.rem(mine + 32 - 2 * turn, 32), tok)), device_id_type=MESH
        )
    pl.semaphore_wait(barrier, 13 - jnp.where(at_home, 1, 0))

    def send_each(copy, turns=range(4)):
        for turn in turns:
            source, place, send_sem, recv_sem, device = copy(turn)
            load(turn, copy is key_copy).wait()
            if turn == 0:

                @pl.when(at_home)
                def _():
                    pltpu.make_async_copy(source, place, recv_sem).start()

                @pl.when(jnp.logical_not(at_home))
                def _():
                    remote(source, place, send_sem, recv_sem, device).start()
            else:
                remote(source, place, send_sem, recv_sem, device).start()

    own = window_ref.at[pl.ds(reach * span, span)]
    send_each(key_copy)
    own_cache.wait()
    own_slots.wait()
    for line_copy in line_copies():
        line_copy.start()
    pltpu.make_async_copy(own, own, key_recv).wait()
    for turn in range(1, 3):
        remote(*pass_copy(turn)).start()
    settle(3 * piece, line_recv)
    for plane_copy in plane_copies():
        plane_copy.start()
    send_each(query_copy)
    settle(12 * piece, plane_recv)
    for pair_copy in pair_copies():
        pair_copy.start()
    for turn in range(1, 3):
        remote(*pass_copy(turn)).wait()
    for turn in range(1, 3):
        remote(*cross_copy(turn)).start()
    for turn in range(1, 3):
        remote(*cross_copy(turn)).wait()
    pltpu.make_async_copy(query_ref, query_ref, query_recv).wait()
    for copy in (key_copy, query_copy):
        for turn in range(4):
            if turn == 0:

                @pl.when(jnp.logical_not(at_home))
                def _():
                    remote(*copy(turn)).wait_send()
            else:
                remote(*copy(turn)).wait_send()
    settle(16 * piece, pair_recv)
    settle(3 * piece, line_send)
    settle(12 * piece, plane_send)
    settle(16 * piece, pair_send)


def exchange(qkv, cached, slots):
    tok_dev = qkv.shape[0]
    reach = SEG_MOST // (4 * tok_dev)
    kept = pl.BlockSpec(memory_space=pl.ANY)
    return pl.pallas_call(
        exchange_kernel,
        out_shape=(
            jax.ShapeDtypeStruct((4, tok_dev, QPG * HEAD), jnp.bfloat16),
            jax.ShapeDtypeStruct(((reach + 1) * 4 * tok_dev, 2 * HEAD), jnp.bfloat16),
            jax.ShapeDtypeStruct((32 * (cached.shape[0] + META_ROWS), 2 * HEAD), jnp.bfloat16),
        ),
        in_specs=[kept] * 2 + [pl.BlockSpec(memory_space=pltpu.SMEM)],
        out_specs=(kept,) * 3,
        scratch_shapes=[
            pltpu.VMEM((4, tok_dev, QPG * HEAD), jnp.bfloat16),
            pltpu.VMEM((4, tok_dev, 2 * HEAD), jnp.bfloat16),
            pltpu.VMEM((META_ROWS, 2 * HEAD), jnp.bfloat16),
            pltpu.SemaphoreType.DMA((8,)),
            pltpu.SemaphoreType.DMA((4,)),
            pltpu.SemaphoreType.DMA,
            pltpu.SemaphoreType.DMA((4,)),
            pltpu.SemaphoreType.DMA,
            pltpu.SemaphoreType.DMA((4,)),
            pltpu.SemaphoreType.DMA((4,)),
            pltpu.SemaphoreType.DMA((2,)),
        ]
        + [pltpu.SemaphoreType.DMA] * 6,
        compiler_params=pltpu.CompilerParams(collective_id=1, has_side_effects=True),
        cost_estimate=pl.CostEstimate(flops=0, bytes_accessed=80 << 20, transcendentals=0),
        name="exchange",
    )(qkv, cached, slots)


CAP = 16
SIDE = 4
PLANE = 32
CUTS = ((0, 768), (768, 640), (1408, 640))


def position():
    tok, ep = lax.axis_index("tok"), lax.axis_index("ep")
    return tok, lax.div(ep, 8), lax.rem(lax.div(ep, 2), 4), lax.rem(ep, 2)


def moved(offsets, way):
    at = [lax.rem(own + size + way * off, size) for own, off, size in zip(position(), offsets, (4, 4, 4, 2))]
    return at[0], (at[1] * 4 + at[2]) * 2 + at[3]


def plane_offsets(cut, index, div, rem):
    core, outer, inner = div(index, 16), rem(div(index, 4), 4), rem(index, 4)
    return ((0, inner, outer, core), (inner, 0, outer, core), (outer, inner, 0, core))[cut]


def line_offsets(cut, turn):
    return tuple(turn if axis == cut else 0 for axis in range(3)) + (0,)


def routed_kernel(
    attended_hbm, weight_hbm, resid_ref, gain_ref, table_ref, gate_up_hbm, down_hbm, out_ref,
    attended_ref, weight_ref, projected, heads, mixed_ref,
    line0, line1, line2, stage0, stage1, stage2, came0, came1, came2, back0, back1, back2,
    inbox0, inbox1, inbox2, sum0, sum1, sum2,
    gate_up, down, tables, rank, share, pick, rows_in,
    weight_sems, table_sems, line_send, line_recv, out_send, near_recv, far_recv, home_send, home_recv,
    part_send, part_recv, head_send, head_recv,
):
    lines, stages, cames, backs = (line0, line1, line2), (stage0, stage1, stage2), (came0, came1, came2), (back0, back1, back2)
    inboxes, sums = (inbox0, inbox1, inbox2), (sum0, sum1, sum2)
    tokens = resid_ref.shape[0]
    width = down.shape[0]
    devices = SIDE * PLANE
    message = SIDE * CAP
    load_attended = pltpu.make_async_copy(attended_hbm, attended_ref, weight_sems.at[2])
    load_weight = pltpu.make_async_copy(weight_hbm, weight_ref, weight_sems.at[3])
    load_attended.start()
    load_weight.start()
    load_gate_up = pltpu.make_async_copy(gate_up_hbm.at[0], gate_up, weight_sems.at[0])
    load_down = pltpu.make_async_copy(down_hbm.at[0], down, weight_sems.at[1])
    barrier = pltpu.get_barrier_semaphore()

    def greet(step, ignored):
        offsets = (lax.div(step, 32), lax.rem(lax.div(step, 8), 4), lax.rem(lax.div(step, 2), 4), lax.rem(step, 2))
        pl.semaphore_signal(barrier, inc=1, device_id=moved(offsets, 1), device_id_type=MESH)
        return ignored

    lax.fori_loop(1, devices, greet, 0)
    for cut in range(3):
        tables[cut, 0] = table_ref[...]
    tok, ep = lax.axis_index("tok"), lax.axis_index("ep")
    mine = group_at(ep, tok)
    home = [owner_of(mine, turn) for turn in range(4)]
    is_own = [(place[0] == tok) & (place[1] == ep) for place in home]

    def project(turn):
        projected[turn] = jnp.dot(
            attended_ref[turn], weight_ref[...], preferred_element_type=jnp.float32
        ).astype(jnp.bfloat16)

    load_attended.wait()
    load_weight.wait()
    load_gate_up.start()
    load_down.start()
    project(0)
    pl.semaphore_wait(barrier, devices - 1)

    def remote(source, place, send_sem, recv_sem, device):
        return pltpu.make_async_remote_copy(
            src_ref=source, dst_ref=place, send_sem=send_sem, recv_sem=recv_sem, device_id=device, device_id_type=MESH
        )

    def rows_of(ref, start, size):
        return ref.at[pl.ds(pl.multiple_of(start, CAP), size)]

    def settle(ref, size, sem):
        pltpu.make_async_copy(ref.at[pl.ds(0, size)], ref.at[pl.ds(0, size)], sem).wait()

    for cut in range(3):
        for turn in range(1, SIDE):
            remote(
                table_ref, tables.at[cut, turn], table_sems.at[0], table_sems.at[1], moved(line_offsets(cut, turn), 1)
            ).start()
    def head_copy(turn):
        return remote(projected.at[turn], heads.at[tok], head_send.at[turn], head_recv, home[turn])

    for turn in range(4):
        if turn:
            project(turn)

        @pl.when(is_own[turn])
        def _():
            pltpu.make_async_copy(projected.at[turn], heads.at[tok], head_recv).start()

        @pl.when(jnp.logical_not(is_own[turn]))
        def _():
            head_copy(turn).start()

    pltpu.make_async_copy(tables.at[:, pl.ds(0, 3)], tables.at[:, pl.ds(0, 3)], table_sems.at[1]).wait()
    before = (
        lax.broadcasted_iota(jnp.int32, (tokens, tokens), 0) < lax.broadcasted_iota(jnp.int32, (tokens, tokens), 1)
    ).astype(jnp.bfloat16)
    index = lax.broadcasted_iota(jnp.int32, (PLANE, tokens), 0)
    shift = {16: 4, 4: 2}
    top = table_ref.shape[0] // 2
    for cut in range(3):
        offsets = plane_offsets(cut, index, lambda v, d: v >> shift[d], lambda v, d: v & (d - 1))
        z, y, x, c = [(own + off) & (size - 1) for own, off, size in zip(position(), offsets, (4, 4, 4, 2))]
        expert = (z * 32 + y * 8 + x * 2 + c).astype(jnp.float32)
        for turn in range(SIDE):
            probs = tables[cut, turn, top:, :]
            shares = probs / jnp.sum(probs, axis=0, keepdims=True)
            named = jnp.zeros((PLANE, tokens), jnp.float32)
            owed = jnp.zeros((PLANE, tokens), jnp.float32)
            for k in range(top):
                match = expert == tables[cut, turn, k : k + 1, :]
                named = jnp.where(match, 1.0, named)
                owed = jnp.where(match, shares[k : k + 1, :], owed)
            earlier = jnp.dot(named.astype(jnp.bfloat16), before, preferred_element_type=jnp.float32)
            at = (cut * SIDE + turn) * PLANE
            rank[at : at + PLANE, :] = jnp.where(named > 0.0, earlier, -1.0)
            share[at : at + PLANE, :] = owed

    pltpu.make_async_copy(heads, heads, head_recv).wait()
    added = resid_ref[...].astype(jnp.float32)
    for head in range(4):
        added = added + heads[head].astype(jnp.float32)
    mixed_ref[...] = added.astype(jnp.bfloat16)
    wide = mixed_ref[...].astype(jnp.float32)
    level = lax.rsqrt(jnp.mean(wide * wide, axis=-1, keepdims=True) + NORM_EPS)
    for cut, (start, size) in enumerate(CUTS):
        part = mixed_ref[:, start : start + size].astype(jnp.float32)
        lines[cut][:tokens] = (part * level * gain_ref[:, start : start + size]).astype(jnp.bfloat16)
    for turn in range(1, SIDE):
        for cut in range(3):
            remote(
                rows_of(lines[cut], 0, tokens), rows_of(lines[cut], turn * tokens, tokens),
                line_send.at[cut], line_recv.at[cut], moved(line_offsets(cut, turn), 1),
            ).start()

    slot = lax.broadcasted_iota(jnp.int32, (CAP, tokens), 0).astype(jnp.float32)

    def choose(cut, core, turn, weighted):
        for j in range(16):
            at = (cut * SIDE + turn) * PLANE + core * 16 + j
            chosen = share[pl.ds(at, 1), :] if weighted else 1.0
            pick[j * CAP : (j + 1) * CAP, :] = jnp.where(rank[pl.ds(at, 1), :] == slot, chosen, 0.0).astype(jnp.bfloat16)

    def send(cut, i, recv_sem):
        source, place = rows_of(stages[cut], i * message, message), rows_of(cames[cut], i * message, message)
        offsets = plane_offsets(cut, i, lax.div, lax.rem)

        @pl.when(i == 0)
        def _():
            pltpu.make_async_copy(source, place, recv_sem).start()

        @pl.when(i > 0)
        def _():
            remote(source, place, out_send.at[cut], recv_sem, moved(offsets, 1)).start()

    def fill(cut, core):
        def one_shard(turn, ignored):
            choose(cut, core, turn, False)
            found = jnp.dot(
                pick[...], rows_of(lines[cut], turn * tokens, tokens)[...], preferred_element_type=jnp.float32
            ).astype(jnp.bfloat16)
            for j in range(16):
                rows_of(stages[cut], (core * 16 + j) * message + turn * CAP, CAP)[...] = found[j * CAP : (j + 1) * CAP]
            return ignored

        lax.fori_loop(0, SIDE, one_shard, 0)

    def dispatch(core, ignored):
        for cut in range(3):
            fill(cut, core)

        def send_all(j, inner):
            chunk = core * 4 + lax.div(j, 4)
            send(2, core * 16 + j, far_recv.at[core])
            send(0, core * 16 + j, near_recv.at[0, chunk])
            send(1, core * 16 + j, near_recv.at[1, chunk])
            return inner

        return lax.fori_loop(0, 16, send_all, ignored)

    for cut in range(3):
        settle(lines[cut], 3 * tokens, line_recv.at[cut])
        settle(lines[cut], 3 * tokens, line_send.at[cut])
    lax.fori_loop(0, 2, dispatch, 0)
    load_gate_up.wait()
    load_down.wait()
    block = SIDE * message

    def slab1(chunk, j):
        return rows_of(came1, chunk * block + (j % 4) * message + (j // 4) * CAP, CAP)

    def slab2(chunk, j):
        core, wide = lax.div(chunk, 4), lax.rem(chunk, 4)
        return rows_of(came2, (core * 16 + (j % 4) * 4 + j // 4) * message + wide * CAP, CAP)

    def give(cut, i):
        source, place = rows_of(cames[cut], i * message, message), rows_of(backs[cut], i * message, message)
        offsets = plane_offsets(cut, i, lax.div, lax.rem)
        recv_sem = home_recv.at[cut, lax.div(i, 16)]

        @pl.when(i == 0)
        def _():
            pltpu.make_async_copy(source, place, recv_sem).start()

        @pl.when(i > 0)
        def _():
            remote(source, place, home_send.at[cut], recv_sem, moved(offsets, -1)).start()

    def work(chunk, ignored):
        @pl.when(lax.rem(chunk, 4) == 0)
        def _():
            settle(came2, 16 * message, far_recv.at[lax.div(chunk, 4)])

        settle(came0, block, near_recv.at[0, chunk])
        settle(came1, block, near_recv.at[1, chunk])
        rows_in[:, 0:768] = rows_of(came0, chunk * block, block)[...]
        for j in range(16):
            rows_in[j * CAP : (j + 1) * CAP, 768:1408] = slab1(chunk, j)[...]
            rows_in[j * CAP : (j + 1) * CAP, 1408:2048] = slab2(chunk, j)[...]
        gate = jnp.dot(rows_in[...], gate_up[:, :width], preferred_element_type=jnp.float32)
        up = jnp.dot(rows_in[...], gate_up[:, width:], preferred_element_type=jnp.float32)
        hidden = (gate * jax.nn.sigmoid(gate) * up).astype(jnp.bfloat16)
        made = jnp.dot(hidden, down[...], preferred_element_type=jnp.float32).astype(jnp.bfloat16)
        rows_of(came0, chunk * block, block)[...] = made[:, 0:768]
        for j in range(16):
            slab1(chunk, j)[...] = made[j * CAP : (j + 1) * CAP, 768:1408]
            slab2(chunk, j)[...] = made[j * CAP : (j + 1) * CAP, 1408:2048]

        @pl.when(lax.rem(chunk, 4) == 3)
        def _():
            def give_all(j, inner):
                for cut in (2, 0, 1):
                    give(cut, lax.div(chunk, 4) * 16 + j)
                return inner

            lax.fori_loop(0, 16, give_all, 0)

        return ignored

    lax.fori_loop(0, 8, work, 0)

    for cut in range(3):
        sums[cut][...] = jnp.zeros_like(sums[cut])

    def combine(core, ignored):
        for cut in range(3):
            settle(backs[cut], 16 * message, home_recv.at[cut, core])

            def one_shard(turn, inner):
                choose(cut, core, turn, True)
                found = jnp.concatenate(
                    [rows_of(backs[cut], (core * 16 + j) * message + turn * CAP, CAP)[...] for j in range(16)], axis=0
                )
                total = rows_of(sums[cut], turn * tokens, tokens)
                total[...] += lax.dot_general(
                    pick[...], found, (((0,), (0,)), ((), ())), preferred_element_type=jnp.float32
                )
                return inner

            lax.fori_loop(0, SIDE, one_shard, 0)

            @pl.when(core == 1)
            def _():
                lines[cut][...] = sums[cut][...].astype(jnp.bfloat16)
                for turn in range(1, SIDE):
                    remote(
                        rows_of(lines[cut], turn * tokens, tokens), rows_of(inboxes[cut], turn * tokens, tokens),
                        part_send.at[cut], part_recv.at[cut], moved(line_offsets(cut, turn), -1),
                    ).start()

        return ignored

    lax.fori_loop(0, 2, combine, 0)
    for cut, (start, size) in enumerate(CUTS):
        settle(inboxes[cut], 3 * tokens, part_recv.at[cut])
        total = mixed_ref[:, start : start + size].astype(jnp.float32) + sums[cut][:tokens]
        for turn in range(1, SIDE):
            total = total + inboxes[cut][turn * tokens : (turn + 1) * tokens].astype(jnp.float32)
        out_ref[:, start : start + size] = total.astype(jnp.bfloat16)
    pltpu.make_async_copy(tables.at[:, pl.ds(0, 3)], tables.at[:, pl.ds(0, 3)], table_sems.at[0]).wait()
    for cut in range(3):
        settle(stages[cut], (PLANE - 1) * message, out_send.at[cut])
        settle(stages[cut], (PLANE - 1) * message, home_send.at[cut])
        settle(lines[cut], 3 * tokens, part_send.at[cut])
    for turn in range(4):

        @pl.when(jnp.logical_not(is_own[turn]))
        def _():
            head_copy(turn).wait_send()


def routed_experts(attended, weight, resid, gain, routes, probs, gate_up, down):
    tokens, width = resid.shape
    vmem = pl.BlockSpec(memory_space=pltpu.VMEM)
    kept = pl.BlockSpec(memory_space=pl.ANY)
    slots = SIDE * PLANE * CAP
    flops = 2 * slots * width * (down.shape[1] * 3 + 2 * tokens)
    table = jnp.concatenate([routes.T.astype(jnp.float32), probs.T], axis=0)

    def each(rows, kind):
        return [pltpu.VMEM((rows, size), kind) for start, size in CUTS]

    return pl.pallas_call(
        routed_kernel,
        out_shape=jax.ShapeDtypeStruct(resid.shape, jnp.bfloat16),
        in_specs=[kept] * 2 + [vmem] * 3 + [kept] * 2,
        out_specs=vmem,
        scratch_shapes=[
            pltpu.VMEM(attended.shape, jnp.bfloat16),
            pltpu.VMEM(weight.shape, jnp.bfloat16),
            pltpu.VMEM((4, tokens, width), jnp.bfloat16),
            pltpu.VMEM((4, tokens, width), jnp.bfloat16),
            pltpu.VMEM((tokens, width), jnp.bfloat16),
        ]
        + each(SIDE * tokens, jnp.bfloat16)
        + each(slots, jnp.bfloat16)
        + each(slots, jnp.bfloat16)
        + each(slots, jnp.bfloat16)
        + each(SIDE * tokens, jnp.bfloat16)
        + each(SIDE * tokens, jnp.float32)
        + [
            pltpu.VMEM(gate_up.shape[1:], jnp.bfloat16),
            pltpu.VMEM(down.shape[1:], jnp.bfloat16),
            pltpu.VMEM((3, SIDE, 2 * routes.shape[1], tokens), jnp.float32),
            pltpu.VMEM((3 * SIDE * PLANE, tokens), jnp.float32),
            pltpu.VMEM((3 * SIDE * PLANE, tokens), jnp.float32),
            pltpu.VMEM((16 * CAP, tokens), jnp.bfloat16),
            pltpu.VMEM((16 * CAP, width), jnp.bfloat16),
            pltpu.SemaphoreType.DMA((4,)),
            pltpu.SemaphoreType.DMA((2,)),
            pltpu.SemaphoreType.DMA((3,)),
            pltpu.SemaphoreType.DMA((3,)),
            pltpu.SemaphoreType.DMA((3,)),
            pltpu.SemaphoreType.DMA((2, 8)),
            pltpu.SemaphoreType.DMA((2,)),
            pltpu.SemaphoreType.DMA((3,)),
            pltpu.SemaphoreType.DMA((3, 2)),
            pltpu.SemaphoreType.DMA((3,)),
            pltpu.SemaphoreType.DMA((3,)),
            pltpu.SemaphoreType.DMA((4,)),
            pltpu.SemaphoreType.DMA,
        ],
        compiler_params=pltpu.CompilerParams(collective_id=0, has_side_effects=True, vmem_limit_bytes=62 << 20),
        cost_estimate=pl.CostEstimate(flops=flops, bytes_accessed=6 * slots * width * 2, transcendentals=0),
        name="routed_experts",
    )(attended, weight, resid, gain[None, :], table, gate_up, down)


def on_device(
    resid,
    qkv,
    cache_kv,
    page_slot,
    seg_lengths,
    cache_age,
    w_out,
    norm_gain,
    routes,
    route_probs,
    w_gate_up,
    w_down,
):
    ep_count = lax.axis_size("ep")
    tok_dev = resid.shape[0]
    seg_count = seg_lengths.shape[0]
    page_count = cache_kv.shape[0]
    bank_rows = page_count * PAGE + META_ROWS
    queries, window, bank = exchange(qkv, cache_kv.reshape(page_count * PAGE, 2 * HEAD), page_slot)
    held = bank.reshape(ep_count, bank_rows, 2 * HEAD)[:, bank_rows - 1, :page_count].astype(jnp.int32)
    slot_row = (
        jnp.arange(ep_count, dtype=jnp.int32)[:, None] * bank_rows
        + jnp.arange(page_count, dtype=jnp.int32)[None, :] * PAGE
    )
    page_match = held.reshape(-1)[None, :] == jnp.arange(seg_count * SEG_PAGES, dtype=jnp.int32)[:, None]
    row_table = jnp.sum(jnp.where(page_match, slot_row.reshape(-1)[None, :], 0), axis=1).astype(jnp.int32)
    attended = attention(seg_lengths, cache_age, row_table, queries, window, bank, seg_count, SEG_MOST)
    return routed_experts(attended, w_out, resid, norm_gain, routes, route_probs, w_gate_up, w_down)


def solution(mesh):
    placed = (
        P(("tok", "ep"), None),
        P(("tok", "ep"), None),
        P("ep", "tok", None, None),
        P("ep"),
        P(),
        P(),
        P("tok", None),
        P(),
        P(("tok", "ep"), None),
        P(("tok", "ep"), None),
        P(("tok", "ep"), None, None),
        P(("tok", "ep"), None, None),
    )
    return jax.shard_map(
        on_device, mesh=mesh, in_specs=placed, out_specs=P(("tok", "ep"), None), check_vma=False
    )
```

```python
import functools
import math

import jax
import jax.numpy as jnp
from jax import lax
from jax.experimental import pallas as pl
from jax.experimental.pallas import tpu as pltpu
from jax.sharding import PartitionSpec as P

D = 2048
FF = 768
HEAD = 128
QPG = 8
TOP = 8
PAGE = 64
SEG_PAGES = 8
SEG_MOST = 2048
STEP = 512
META_ROWS = 16


NEG_FILL = -1e30
NORM_EPS = 1e-06


def attention_kernel(tok_dev, segs, lengths_ref, age_ref, row_ref, q_hbm, window_hbm, bank_hbm, out_ref, q_ref, window_ref, bank_ref, load_sems, seg_ref, score_ref, low_ref, top_ref, den_ref, acc_ref):
    load_q = pltpu.make_async_copy(q_hbm, q_ref, load_sems.at[0])
    load_window = pltpu.make_async_copy(window_hbm, window_ref, load_sems.at[1])
    load_bank = pltpu.make_async_copy(bank_hbm, bank_ref, load_sems.at[2])
    load_q.start()
    load_window.start()
    load_bank.start()
    begins = jnp.int32(0)
    for s in range(segs):
        seg_ref[s] = begins
        begins = begins + lengths_ref[s]
        seg_ref[segs + s] = begins
        seg_ref[2 * segs + s] = age_ref[s]
    seg_ref[3 * segs] = group_at(lax.axis_index("ep"), lax.axis_index("tok")) * q_ref.shape[0] * tok_dev
    rows = tok_dev * QPG
    held_chunks = window_ref.shape[0] // tok_dev
    opening_chunk = seg_ref[3 * segs] // tok_dev - (held_chunks - q_ref.shape[0])
    rate = math.log2(math.e) / math.sqrt(HEAD)

    def tiled(mask):
        return jnp.concatenate([mask] * QPG, axis=0)

    def one_block(block, carry):
        first = seg_ref[3 * segs] + block * tok_dev
        last = first + tok_dev - 1
        token = first + lax.broadcasted_iota(jnp.int32, (tok_dev, STEP), 0)
        column = lax.broadcasted_iota(jnp.int32, (tok_dev, STEP), 1)
        narrow = token[:, :HEAD]
        low = jnp.zeros((tok_dev, HEAD), jnp.int32)
        begin = jnp.int32(0)
        for s in range(segs):
            start = seg_ref[s]
            low = jnp.where(narrow >= start, start, low)
            begin = jnp.where(first >= start, start, begin)
        low_ref[...] = jnp.concatenate([low] * (STEP // HEAD), axis=1)
        query = jnp.concatenate([q_ref[block, :, h * HEAD:(h + 1) * HEAD] for h in range(QPG)], axis=0)
        den_ref[...] = jnp.zeros_like(den_ref)
        acc_ref[...] = jnp.zeros_like(acc_ref)

        def region(bank, steps, bank_of, mask_of, opening):
            if opening:
                held = jnp.full((rows, HEAD), NEG_FILL, jnp.float32)
            else:
                held = top_ref[...]

            def score(step, running):
                keys = jnp.concatenate([bank[pl.ds(at, size), :HEAD] for at, size in bank_of(step)], axis=0)
                scores = lax.dot_general(query, keys, (((1,), (1,)), ((), ())), preferred_element_type=jnp.float32) * rate
                scores = jnp.where(tiled(mask_of(step)), scores, NEG_FILL)
                score_ref[step] = scores
                for part in range(STEP // HEAD):
                    running = jnp.maximum(running, scores[:, part * HEAD : (part + 1) * HEAD])
                return running

            newest = lax.fori_loop(0, steps, score, held)
            newest = jnp.broadcast_to(jnp.max(newest, axis=1, keepdims=True), (rows, HEAD))
            if not opening:
                factor = jnp.exp2(held - newest)
                den_ref[...] = den_ref[...] * factor
                acc_ref[...] = acc_ref[...] * factor
            top_ref[...] = newest

            def weigh(step, ignored):
                top = top_ref[...]
                weights = jnp.exp2(score_ref[step] - jnp.concatenate([top] * (STEP // HEAD), axis=1))
                den_ref[...] += sum([weights[:, part * HEAD : (part + 1) * HEAD] for part in range(STEP // HEAD)])
                values = jnp.concatenate([bank[pl.ds(at, size), HEAD:] for at, size in bank_of(step)], axis=0)
                acc_ref[...] += jnp.dot(weights.astype(jnp.bfloat16), values, preferred_element_type=jnp.float32)
                return ignored

            lax.fori_loop(0, steps, weigh, 0)

        chunk_last = first // tok_dev
        chunk_first = begin // tok_dev
        per = STEP // tok_dev
        steps = (chunk_last - chunk_first + per) // per

        def new_chunk(step, half):
            return chunk_last - per * (step + 1) + 1 + half

        def new_bank(step):
            return [
                (pl.multiple_of(jnp.clip(new_chunk(step, half) - opening_chunk, 0, held_chunks - 1) * tok_dev, tok_dev), tok_dev)
                for half in range(per)
            ]

        def new_mask(step):
            key = new_chunk(step, 0) * tok_dev + column
            return (key >= low_ref[...]) & (key <= token)

        region(window_ref, steps, new_bank, new_mask, True)

        def cached(s, ignored):
            start, end, age = seg_ref[s], seg_ref[segs + s], seg_ref[2 * segs + s]

            @pl.when((start <= last) & (end > first) & (age > 0))
            def _():
                def page_bank(step):
                    return [(pl.multiple_of(row_ref[s * SEG_PAGES + step * (STEP // PAGE) + part], 16), PAGE) for part in range(STEP // PAGE)]

                def page_mask(step):
                    return (token >= start) & (token < end) & (step * STEP + column < age)

                region(bank_ref, (age + STEP - 1) // STEP, page_bank, page_mask, False)
            return ignored

        @pl.when(block == 0)
        def _():
            load_bank.wait()

        lax.fori_loop(0, segs, cached, 0)
        total = jnp.sum(den_ref[...], axis=1, keepdims=True)
        result = (acc_ref[...] / total).astype(jnp.bfloat16)
        for h in range(QPG):
            out_ref[block, :, h * HEAD:(h + 1) * HEAD] = result[h * tok_dev:(h + 1) * tok_dev]
        return carry

    load_q.wait()
    load_window.wait()
    lax.fori_loop(0, q_ref.shape[0], one_block, 0)


def attention(seg_lengths, cache_age, row_table, queries, window, bank, segs, seg_most):
    blocks, tok_dev, width = queries.shape
    most_steps = max(((seg_most + tok_dev) // tok_dev + STEP // tok_dev - 1) // (STEP // tok_dev), 1)
    rows = tok_dev * QPG
    return pl.pallas_call(
        functools.partial(attention_kernel, tok_dev, segs),
        out_shape=jax.ShapeDtypeStruct(queries.shape, jnp.bfloat16),
        in_specs=[pl.BlockSpec(memory_space=pltpu.SMEM)] * 3 + [pl.BlockSpec(memory_space=pl.ANY)] * 3,
        out_specs=pl.BlockSpec(memory_space=pltpu.VMEM),
        scratch_shapes=[
            pltpu.VMEM(queries.shape, jnp.bfloat16),
            pltpu.VMEM(window.shape, jnp.bfloat16),
            pltpu.VMEM(bank.shape, jnp.bfloat16),
            pltpu.SemaphoreType.DMA((3,)),
            pltpu.SMEM((3 * segs + 1,), jnp.int32),
            pltpu.VMEM((most_steps, rows, STEP), jnp.float32),
            pltpu.VMEM((tok_dev, STEP), jnp.int32),
            pltpu.VMEM((rows, HEAD), jnp.float32),
            pltpu.VMEM((rows, HEAD), jnp.float32),
            pltpu.VMEM((rows, HEAD), jnp.float32),
        ],
        compiler_params=pltpu.CompilerParams(vmem_limit_bytes=62 << 20),
        name="attend",
    )(seg_lengths, cache_age, row_table, queries, window, bank)


MESH = pl.DeviceIdType.MESH


def place_of(group, head):
    tok, tall, core = lax.div(group, 8), lax.rem(lax.div(group, 2), 4), lax.rem(group, 2)
    return (tall * 4 + lax.rem(tok + head, 4)) * 2 + core


def group_at(ep, head):
    tall, wide, core = lax.div(ep, 8), lax.rem(lax.div(ep, 2), 4), lax.rem(ep, 2)
    return lax.rem(wide + 4 - head, 4) * 8 + 2 * tall + core


def owner_of(group, block):
    tok = lax.div(group, 8)
    return tok, lax.rem(group, 8) * 4 + block


def exchange_kernel(
    qkv_ref, cache_ref, slots_ref, query_ref, window_ref, bank_ref,
    stage_q, stage_kv, stage_slots, load_sems, key_send, key_recv, query_send, query_recv, pass_send, pass_recv, own_sem, line_send, line_recv,
    plane_send, plane_recv, pair_send, pair_recv,
):
    tok, ep = lax.axis_index("tok"), lax.axis_index("ep")
    tok_dev = qkv_ref.shape[0]
    q_width = QPG * HEAD
    number = tok * 32 + ep
    group, block = lax.div(number, 4), lax.rem(number, 4)
    mine = group_at(ep, tok)
    reach = SEG_MOST // (4 * tok_dev)
    span = 4 * tok_dev

    def column(head):
        return head * (q_width + 2 * HEAD)

    def remote(source, place, send_sem, recv_sem, device):
        return pltpu.make_async_remote_copy(
            src_ref=source, dst_ref=place, send_sem=send_sem, recv_sem=recv_sem, device_id=device, device_id_type=MESH
        )

    def load(turn, keys):
        head = lax.rem(tok + turn, 4)
        if keys:
            source = qkv_ref.at[:, pl.ds(pl.multiple_of(column(head) + q_width, HEAD), 2 * HEAD)]
            return pltpu.make_async_copy(source, stage_kv.at[turn], load_sems.at[turn])
        source = qkv_ref.at[:, pl.ds(pl.multiple_of(column(head), HEAD), q_width)]
        return pltpu.make_async_copy(source, stage_q.at[turn], load_sems.at[4 + turn])

    for keys in (True, False):
        for turn in range(4):
            load(turn, keys).start()

    def key_copy(turn):
        head = lax.rem(tok + turn, 4)
        place = window_ref.at[pl.ds(pl.multiple_of(reach * span + block * tok_dev, tok_dev), tok_dev)]
        return stage_kv.at[turn], place, key_send.at[turn], key_recv, (head, place_of(group, head))

    def query_copy(turn):
        head = lax.rem(tok + turn, 4)
        return stage_q.at[turn], query_ref.at[block], query_send.at[turn], query_recv, (head, place_of(group, head))

    def spans(index):
        return window_ref.at[pl.ds(pl.multiple_of(index * span, span), span)]

    def pass_copy(turn):
        device = (tok, place_of(lax.rem(mine + 2 * turn, 32), tok))
        return spans(reach), spans(reach - 2 * turn), pass_send.at[turn - 1], pass_recv.at[turn - 1], device

    def cross_copy(turn):
        device = (tok, at(tall, wide, 1 - core))
        return spans(6 - 2 * turn - 2 * core), spans(5 - 2 * turn), pass_send.at[turn + 1], pass_recv.at[turn + 1], device

    held, told = cache_ref.shape[0], stage_slots.shape[0]
    piece = held + told
    cut = piece // 32 * 16
    tall, wide, core = lax.div(ep, 8), lax.rem(lax.div(ep, 2), 4), lax.rem(ep, 2)

    def at(y, x, c):
        return (lax.rem(y, 4) * 4 + lax.rem(x, 4)) * 2 + c

    def part(y, x, c, start, size):
        return bank_ref.at[pl.ds(pl.multiple_of(at(y, x, c) * piece + start, 16), size)]

    lane = lax.broadcasted_iota(jnp.int32, stage_slots.shape, 1)
    listed = jnp.zeros(stage_slots.shape, jnp.float32)
    for page in range(slots_ref.shape[0]):
        listed = jnp.where(lane == page, slots_ref[page].astype(jnp.float32), listed)
    stage_slots[...] = listed.astype(jnp.bfloat16)
    own_cache = pltpu.make_async_copy(cache_ref, part(tall, wide, core, 0, held), own_sem.at[0])
    own_slots = pltpu.make_async_copy(stage_slots, part(tall, wide, core, held, told), own_sem.at[1])
    own_cache.start()
    own_slots.start()

    def line_copies():
        for turn in range(1, 4):
            first = part(tall, wide, core, 0, cut)
            yield remote(first, first, line_send, line_recv, (tok, at(tall, wide + turn, core)))
            rest = part(tall, wide, core, cut, piece - cut)
            yield remote(rest, rest, line_send, line_recv, (tok, at(tall + turn, wide, core)))

    def plane_copies():
        for turn in range(1, 4):
            for along in range(4):
                first = part(tall, wide + along, core, 0, cut)
                yield remote(first, first, plane_send, plane_recv, (tok, at(tall + turn, wide, core)))
                rest = part(tall + along, wide, core, cut, piece - cut)
                yield remote(rest, rest, plane_send, plane_recv, (tok, at(tall, wide + turn, core)))

    def pair_copies():
        for y in range(4):
            for x in range(4):
                whole = part(y, x, core, 0, piece)
                yield remote(whole, whole, pair_send, pair_recv, (tok, at(tall, wide, 1 - core)))

    def settle(rows, sem):
        pltpu.make_async_copy(bank_ref.at[pl.ds(0, rows)], bank_ref.at[pl.ds(0, rows)], sem).wait()

    barrier = pltpu.get_barrier_semaphore()
    at_home = place_of(group, tok) == ep
    for turn in range(1, 4):
        for partner in (at(tall, wide + turn, core), at(tall + turn, wide, core)):
            pl.semaphore_signal(barrier, inc=1, device_id=(tok, partner), device_id_type=MESH)
    pl.semaphore_signal(barrier, inc=1, device_id=(tok, at(tall, wide, 1 - core)), device_id_type=MESH)
    for turn in range(4):
        theirs = owner_of(mine, turn)

        @pl.when(jnp.logical_not((theirs[0] == tok) & (theirs[1] == ep)))
        def _():
            pl.semaphore_signal(barrier, inc=1, device_id=theirs, device_id_type=MESH)

    for turn in range(1, 3):
        pl.semaphore_signal(
            barrier, inc=1, device_id=(tok, place_of(lax.rem(mine + 32 - 2 * turn, 32), tok)), device_id_type=MESH
        )
    pl.semaphore_wait(barrier, 13 - jnp.where(at_home, 1, 0))

    def send_each(copy, turns=range(4)):
        for turn in turns:
            source, place, send_sem, recv_sem, device = copy(turn)
            load(turn, copy is key_copy).wait()
            if turn == 0:

                @pl.when(at_home)
                def _():
                    pltpu.make_async_copy(source, place, recv_sem).start()

                @pl.when(jnp.logical_not(at_home))
                def _():
                    remote(source, place, send_sem, recv_sem, device).start()
            else:
                remote(source, place, send_sem, recv_sem, device).start()

    own = window_ref.at[pl.ds(reach * span, span)]
    send_each(key_copy)
    own_cache.wait()
    own_slots.wait()
    for line_copy in line_copies():
        line_copy.start()
    pltpu.make_async_copy(own, own, key_recv).wait()
    for turn in range(1, 3):
        remote(*pass_copy(turn)).start()
    settle(3 * piece, line_recv)
    for plane_copy in plane_copies():
        plane_copy.start()
    send_each(query_copy)
    settle(12 * piece, plane_recv)
    for pair_copy in pair_copies():
        pair_copy.start()
    for turn in range(1, 3):
        remote(*pass_copy(turn)).wait()
    for turn in range(1, 3):
        remote(*cross_copy(turn)).start()
    for turn in range(1, 3):
        remote(*cross_copy(turn)).wait()
    pltpu.make_async_copy(query_ref, query_ref, query_recv).wait()
    for copy in (key_copy, query_copy):
        for turn in range(4):
            if turn == 0:

                @pl.when(jnp.logical_not(at_home))
                def _():
                    remote(*copy(turn)).wait_send()
            else:
                remote(*copy(turn)).wait_send()
    settle(16 * piece, pair_recv)
    settle(3 * piece, line_send)
    settle(12 * piece, plane_send)
    settle(16 * piece, pair_send)


def exchange(qkv, cached, slots):
    tok_dev = qkv.shape[0]
    reach = SEG_MOST // (4 * tok_dev)
    kept = pl.BlockSpec(memory_space=pl.ANY)
    return pl.pallas_call(
        exchange_kernel,
        out_shape=(
            jax.ShapeDtypeStruct((4, tok_dev, QPG * HEAD), jnp.bfloat16),
            jax.ShapeDtypeStruct(((reach + 1) * 4 * tok_dev, 2 * HEAD), jnp.bfloat16),
            jax.ShapeDtypeStruct((32 * (cached.shape[0] + META_ROWS), 2 * HEAD), jnp.bfloat16),
        ),
        in_specs=[kept] * 2 + [pl.BlockSpec(memory_space=pltpu.SMEM)],
        out_specs=(kept,) * 3,
        scratch_shapes=[
            pltpu.VMEM((4, tok_dev, QPG * HEAD), jnp.bfloat16),
            pltpu.VMEM((4, tok_dev, 2 * HEAD), jnp.bfloat16),
            pltpu.VMEM((META_ROWS, 2 * HEAD), jnp.bfloat16),
            pltpu.SemaphoreType.DMA((8,)),
            pltpu.SemaphoreType.DMA((4,)),
            pltpu.SemaphoreType.DMA,
            pltpu.SemaphoreType.DMA((4,)),
            pltpu.SemaphoreType.DMA,
            pltpu.SemaphoreType.DMA((4,)),
            pltpu.SemaphoreType.DMA((4,)),
            pltpu.SemaphoreType.DMA((2,)),
        ]
        + [pltpu.SemaphoreType.DMA] * 6,
        compiler_params=pltpu.CompilerParams(collective_id=1, has_side_effects=True),
        cost_estimate=pl.CostEstimate(flops=0, bytes_accessed=80 << 20, transcendentals=0),
        name="exchange",
    )(qkv, cached, slots)


CAP = 16
SIDE = 4
PLANE = 32
CUTS = ((0, 768), (768, 640), (1408, 640))


def position():
    tok, ep = lax.axis_index("tok"), lax.axis_index("ep")
    return tok, lax.div(ep, 8), lax.rem(lax.div(ep, 2), 4), lax.rem(ep, 2)


def moved(offsets, way):
    at = [lax.rem(own + size + way * off, size) for own, off, size in zip(position(), offsets, (4, 4, 4, 2))]
    return at[0], (at[1] * 4 + at[2]) * 2 + at[3]


def plane_offsets(cut, index, div, rem):
    core, outer, inner = div(index, 16), rem(div(index, 4), 4), rem(index, 4)
    return ((0, inner, outer, core), (inner, 0, outer, core), (outer, inner, 0, core))[cut]


def mixed_order(j):
    return lax.rem(j, 4) * 4 + lax.rem(lax.div(j, 4) + j, 4)


def line_offsets(cut, turn):
    return tuple(turn if axis == cut else 0 for axis in range(3)) + (0,)


def routed_kernel(
    attended_hbm, weight_hbm, resid_ref, gain_ref, table_ref, gate_up_hbm, down_hbm, out_ref,
    attended_ref, weight_ref, projected, heads, mixed_ref,
    line0, line1, line2, stage0, stage1, stage2, came0, came1, came2, back0, back1, back2,
    inbox0, inbox1, inbox2, sum0, sum1, sum2,
    gate_up, down, tables, rank, share, pick, rows_in,
    weight_sems, table_sems, line_send, line_recv, out_send, near_recv, far_recv, home_send, home_recv,
    part_send, part_recv, head_send, head_recv,
):
    lines, stages, cames, backs = (line0, line1, line2), (stage0, stage1, stage2), (came0, came1, came2), (back0, back1, back2)
    inboxes, sums = (inbox0, inbox1, inbox2), (sum0, sum1, sum2)
    tokens = resid_ref.shape[0]
    width = down.shape[0]
    devices = SIDE * PLANE
    message = SIDE * CAP
    load_attended = pltpu.make_async_copy(attended_hbm, attended_ref, weight_sems.at[2])
    load_weight = pltpu.make_async_copy(weight_hbm, weight_ref, weight_sems.at[3])
    load_attended.start()
    load_weight.start()
    load_gate_up = pltpu.make_async_copy(gate_up_hbm.at[0], gate_up, weight_sems.at[0])
    load_down = pltpu.make_async_copy(down_hbm.at[0], down, weight_sems.at[1])
    barrier = pltpu.get_barrier_semaphore()

    def greet(step, ignored):
        offsets = (lax.div(step, 32), lax.rem(lax.div(step, 8), 4), lax.rem(lax.div(step, 2), 4), lax.rem(step, 2))
        pl.semaphore_signal(barrier, inc=1, device_id=moved(offsets, 1), device_id_type=MESH)
        return ignored

    lax.fori_loop(1, devices, greet, 0)
    for cut in range(3):
        tables[cut, 0] = table_ref[...]
    tok, ep = lax.axis_index("tok"), lax.axis_index("ep")
    mine = group_at(ep, tok)
    home = [owner_of(mine, turn) for turn in range(4)]
    is_own = [(place[0] == tok) & (place[1] == ep) for place in home]

    def project(turn):
        projected[turn] = jnp.dot(
            attended_ref[turn], weight_ref[...], preferred_element_type=jnp.float32
        ).astype(jnp.bfloat16)

    load_attended.wait()
    load_weight.wait()
    load_gate_up.start()
    load_down.start()
    project(0)
    pl.semaphore_wait(barrier, devices - 1)

    def remote(source, place, send_sem, recv_sem, device):
        return pltpu.make_async_remote_copy(
            src_ref=source, dst_ref=place, send_sem=send_sem, recv_sem=recv_sem, device_id=device, device_id_type=MESH
        )

    def rows_of(ref, start, size):
        return ref.at[pl.ds(pl.multiple_of(start, CAP), size)]

    def settle(ref, size, sem):
        pltpu.make_async_copy(ref.at[pl.ds(0, size)], ref.at[pl.ds(0, size)], sem).wait()

    for cut in range(3):
        for turn in range(1, SIDE):
            remote(
                table_ref, tables.at[cut, turn], table_sems.at[0], table_sems.at[1], moved(line_offsets(cut, turn), 1)
            ).start()
    def head_copy(turn):
        return remote(projected.at[turn], heads.at[tok], head_send.at[turn], head_recv, home[turn])

    for turn in range(4):
        if turn:
            project(turn)

        @pl.when(is_own[turn])
        def _():
            pltpu.make_async_copy(projected.at[turn], heads.at[tok], head_recv).start()

        @pl.when(jnp.logical_not(is_own[turn]))
        def _():
            head_copy(turn).start()

    pltpu.make_async_copy(tables.at[:, pl.ds(0, 3)], tables.at[:, pl.ds(0, 3)], table_sems.at[1]).wait()
    before = (
        lax.broadcasted_iota(jnp.int32, (tokens, tokens), 0) < lax.broadcasted_iota(jnp.int32, (tokens, tokens), 1)
    ).astype(jnp.bfloat16)
    index = lax.broadcasted_iota(jnp.int32, (PLANE, tokens), 0)
    shift = {16: 4, 4: 2}
    top = table_ref.shape[0] // 2
    for cut in range(3):
        offsets = plane_offsets(cut, index, lambda v, d: v >> shift[d], lambda v, d: v & (d - 1))
        z, y, x, c = [(own + off) & (size - 1) for own, off, size in zip(position(), offsets, (4, 4, 4, 2))]
        expert = (z * 32 + y * 8 + x * 2 + c).astype(jnp.float32)
        for turn in range(SIDE):
            probs = tables[cut, turn, top:, :]
            shares = probs / jnp.sum(probs, axis=0, keepdims=True)
            named = jnp.zeros((PLANE, tokens), jnp.float32)
            owed = jnp.zeros((PLANE, tokens), jnp.float32)
            for k in range(top):
                match = expert == tables[cut, turn, k : k + 1, :]
                named = jnp.where(match, 1.0, named)
                owed = jnp.where(match, shares[k : k + 1, :], owed)
            earlier = jnp.dot(named.astype(jnp.bfloat16), before, preferred_element_type=jnp.float32)
            at = (cut * SIDE + turn) * PLANE
            rank[at : at + PLANE, :] = jnp.where(named > 0.0, earlier, -1.0)
            share[at : at + PLANE, :] = owed

    pltpu.make_async_copy(heads, heads, head_recv).wait()
    added = resid_ref[...].astype(jnp.float32)
    for head in range(4):
        added = added + heads[head].astype(jnp.float32)
    mixed_ref[...] = added.astype(jnp.bfloat16)
    wide = mixed_ref[...].astype(jnp.float32)
    level = lax.rsqrt(jnp.mean(wide * wide, axis=-1, keepdims=True) + NORM_EPS)
    for cut, (start, size) in enumerate(CUTS):
        part = mixed_ref[:, start : start + size].astype(jnp.float32)
        lines[cut][:tokens] = (part * level * gain_ref[:, start : start + size]).astype(jnp.bfloat16)
    for turn in (1, 3, 2):
        for cut in range(3):
            remote(
                rows_of(lines[cut], 0, tokens), rows_of(lines[cut], turn * tokens, tokens),
                line_send.at[cut], line_recv.at[cut], moved(line_offsets(cut, turn), 1),
            ).start()

    slot = lax.broadcasted_iota(jnp.int32, (CAP, tokens), 0).astype(jnp.float32)

    def choose(cut, core, turn, weighted):
        for j in range(16):
            at = (cut * SIDE + turn) * PLANE + core * 16 + j
            chosen = share[pl.ds(at, 1), :] if weighted else 1.0
            pick[j * CAP : (j + 1) * CAP, :] = jnp.where(rank[pl.ds(at, 1), :] == slot, chosen, 0.0).astype(jnp.bfloat16)

    def send(cut, i, recv_sem):
        source, place = rows_of(stages[cut], i * message, message), rows_of(cames[cut], i * message, message)
        offsets = plane_offsets(cut, i, lax.div, lax.rem)

        @pl.when(i == 0)
        def _():
            pltpu.make_async_copy(source, place, recv_sem).start()

        @pl.when(i > 0)
        def _():
            remote(source, place, out_send.at[cut], recv_sem, moved(offsets, 1)).start()

    def fill(cut, core):
        def one_shard(turn, ignored):
            choose(cut, core, turn, False)
            found = jnp.dot(
                pick[...], rows_of(lines[cut], turn * tokens, tokens)[...], preferred_element_type=jnp.float32
            ).astype(jnp.bfloat16)
            for j in range(16):
                rows_of(stages[cut], (core * 16 + j) * message + turn * CAP, CAP)[...] = found[j * CAP : (j + 1) * CAP]
            return ignored

        lax.fori_loop(0, SIDE, one_shard, 0)

    def dispatch(core, ignored):
        for cut in range(3):
            fill(cut, core)

        def send_all(order, inner):
            j = mixed_order(order)
            chunk = core * 4 + lax.div(j, 4)
            send(2, core * 16 + j, far_recv.at[core])
            send(0, core * 16 + j, near_recv.at[0, chunk])
            send(1, core * 16 + j, near_recv.at[1, chunk])
            return inner

        return lax.fori_loop(0, 16, send_all, ignored)

    for cut in range(3):
        settle(lines[cut], 3 * tokens, line_recv.at[cut])
        settle(lines[cut], 3 * tokens, line_send.at[cut])
    lax.fori_loop(0, 2, dispatch, 0)
    load_gate_up.wait()
    load_down.wait()
    block = SIDE * message

    def slab1(chunk, j):
        return rows_of(came1, chunk * block + (j % 4) * message + (j // 4) * CAP, CAP)

    def slab2(chunk, j):
        core, wide = lax.div(chunk, 4), lax.rem(chunk, 4)
        return rows_of(came2, (core * 16 + (j % 4) * 4 + j // 4) * message + wide * CAP, CAP)

    def give(cut, i):
        source, place = rows_of(cames[cut], i * message, message), rows_of(backs[cut], i * message, message)
        offsets = plane_offsets(cut, i, lax.div, lax.rem)
        recv_sem = home_recv.at[cut, lax.div(i, 16)]

        @pl.when(i == 0)
        def _():
            pltpu.make_async_copy(source, place, recv_sem).start()

        @pl.when(i > 0)
        def _():
            remote(source, place, home_send.at[cut], recv_sem, moved(offsets, -1)).start()

    def work(chunk, ignored):
        @pl.when(lax.rem(chunk, 4) == 0)
        def _():
            settle(came2, 16 * message, far_recv.at[lax.div(chunk, 4)])

        settle(came0, block, near_recv.at[0, chunk])
        settle(came1, block, near_recv.at[1, chunk])
        rows_in[:, 0:768] = rows_of(came0, chunk * block, block)[...]
        for j in range(16):
            rows_in[j * CAP : (j + 1) * CAP, 768:1408] = slab1(chunk, j)[...]
            rows_in[j * CAP : (j + 1) * CAP, 1408:2048] = slab2(chunk, j)[...]
        gate = jnp.dot(rows_in[...], gate_up[:, :width], preferred_element_type=jnp.float32)
        up = jnp.dot(rows_in[...], gate_up[:, width:], preferred_element_type=jnp.float32)
        hidden = (gate * jax.nn.sigmoid(gate) * up).astype(jnp.bfloat16)
        made = jnp.dot(hidden, down[...], preferred_element_type=jnp.float32).astype(jnp.bfloat16)
        rows_of(came0, chunk * block, block)[...] = made[:, 0:768]
        for j in range(16):
            slab1(chunk, j)[...] = made[j * CAP : (j + 1) * CAP, 768:1408]
            slab2(chunk, j)[...] = made[j * CAP : (j + 1) * CAP, 1408:2048]

        @pl.when(lax.rem(chunk, 4) == 3)
        def _():
            def give_all(order, inner):
                for cut in (2, 0, 1):
                    give(cut, lax.div(chunk, 4) * 16 + mixed_order(order))
                return inner

            lax.fori_loop(0, 16, give_all, 0)

        return ignored

    lax.fori_loop(0, 8, work, 0)

    for cut in range(3):
        sums[cut][...] = jnp.zeros_like(sums[cut])

    def combine(core, ignored):
        for cut in range(3):
            settle(backs[cut], 16 * message, home_recv.at[cut, core])

            def one_shard(turn, inner):
                choose(cut, core, turn, True)
                found = jnp.concatenate(
                    [rows_of(backs[cut], (core * 16 + j) * message + turn * CAP, CAP)[...] for j in range(16)], axis=0
                )
                total = rows_of(sums[cut], turn * tokens, tokens)
                total[...] += lax.dot_general(
                    pick[...], found, (((0,), (0,)), ((), ())), preferred_element_type=jnp.float32
                )
                return inner

            lax.fori_loop(0, SIDE, one_shard, 0)

            @pl.when(core == 1)
            def _():
                lines[cut][...] = sums[cut][...].astype(jnp.bfloat16)
                for turn in range(1, SIDE):
                    remote(
                        rows_of(lines[cut], turn * tokens, tokens), rows_of(inboxes[cut], turn * tokens, tokens),
                        part_send.at[cut], part_recv.at[cut], moved(line_offsets(cut, turn), -1),
                    ).start()

        return ignored

    lax.fori_loop(0, 2, combine, 0)
    for cut, (start, size) in enumerate(CUTS):
        settle(inboxes[cut], 3 * tokens, part_recv.at[cut])
        total = mixed_ref[:, start : start + size].astype(jnp.float32) + sums[cut][:tokens]
        for turn in range(1, SIDE):
            total = total + inboxes[cut][turn * tokens : (turn + 1) * tokens].astype(jnp.float32)
        out_ref[:, start : start + size] = total.astype(jnp.bfloat16)
    pltpu.make_async_copy(tables.at[:, pl.ds(0, 3)], tables.at[:, pl.ds(0, 3)], table_sems.at[0]).wait()
    for cut in range(3):
        settle(stages[cut], (PLANE - 1) * message, out_send.at[cut])
        settle(stages[cut], (PLANE - 1) * message, home_send.at[cut])
        settle(lines[cut], 3 * tokens, part_send.at[cut])
    for turn in range(4):

        @pl.when(jnp.logical_not(is_own[turn]))
        def _():
            head_copy(turn).wait_send()


def routed_experts(attended, weight, resid, gain, routes, probs, gate_up, down):
    tokens, width = resid.shape
    vmem = pl.BlockSpec(memory_space=pltpu.VMEM)
    kept = pl.BlockSpec(memory_space=pl.ANY)
    slots = SIDE * PLANE * CAP
    flops = 2 * slots * width * (down.shape[1] * 3 + 2 * tokens)
    table = jnp.concatenate([routes.T.astype(jnp.float32), probs.T], axis=0)

    def each(rows, kind):
        return [pltpu.VMEM((rows, size), kind) for start, size in CUTS]

    return pl.pallas_call(
        routed_kernel,
        out_shape=jax.ShapeDtypeStruct(resid.shape, jnp.bfloat16),
        in_specs=[kept] * 2 + [vmem] * 3 + [kept] * 2,
        out_specs=vmem,
        scratch_shapes=[
            pltpu.VMEM(attended.shape, jnp.bfloat16),
            pltpu.VMEM(weight.shape, jnp.bfloat16),
            pltpu.VMEM((4, tokens, width), jnp.bfloat16),
            pltpu.VMEM((4, tokens, width), jnp.bfloat16),
            pltpu.VMEM((tokens, width), jnp.bfloat16),
        ]
        + each(SIDE * tokens, jnp.bfloat16)
        + each(slots, jnp.bfloat16)
        + each(slots, jnp.bfloat16)
        + each(slots, jnp.bfloat16)
        + each(SIDE * tokens, jnp.bfloat16)
        + each(SIDE * tokens, jnp.float32)
        + [
            pltpu.VMEM(gate_up.shape[1:], jnp.bfloat16),
            pltpu.VMEM(down.shape[1:], jnp.bfloat16),
            pltpu.VMEM((3, SIDE, 2 * routes.shape[1], tokens), jnp.float32),
            pltpu.VMEM((3 * SIDE * PLANE, tokens), jnp.float32),
            pltpu.VMEM((3 * SIDE * PLANE, tokens), jnp.float32),
            pltpu.VMEM((16 * CAP, tokens), jnp.bfloat16),
            pltpu.VMEM((16 * CAP, width), jnp.bfloat16),
            pltpu.SemaphoreType.DMA((4,)),
            pltpu.SemaphoreType.DMA((2,)),
            pltpu.SemaphoreType.DMA((3,)),
            pltpu.SemaphoreType.DMA((3,)),
            pltpu.SemaphoreType.DMA((3,)),
            pltpu.SemaphoreType.DMA((2, 8)),
            pltpu.SemaphoreType.DMA((2,)),
            pltpu.SemaphoreType.DMA((3,)),
            pltpu.SemaphoreType.DMA((3, 2)),
            pltpu.SemaphoreType.DMA((3,)),
            pltpu.SemaphoreType.DMA((3,)),
            pltpu.SemaphoreType.DMA((4,)),
            pltpu.SemaphoreType.DMA,
        ],
        compiler_params=pltpu.CompilerParams(collective_id=0, has_side_effects=True, vmem_limit_bytes=62 << 20),
        cost_estimate=pl.CostEstimate(flops=flops, bytes_accessed=6 * slots * width * 2, transcendentals=0),
        name="routed_experts",
    )(attended, weight, resid, gain[None, :], table, gate_up, down)


def on_device(
    resid,
    qkv,
    cache_kv,
    page_slot,
    seg_lengths,
    cache_age,
    w_out,
    norm_gain,
    routes,
    route_probs,
    w_gate_up,
    w_down,
):
    ep_count = lax.axis_size("ep")
    tok_dev = resid.shape[0]
    seg_count = seg_lengths.shape[0]
    page_count = cache_kv.shape[0]
    bank_rows = page_count * PAGE + META_ROWS
    queries, window, bank = exchange(qkv, cache_kv.reshape(page_count * PAGE, 2 * HEAD), page_slot)
    held = bank.reshape(ep_count, bank_rows, 2 * HEAD)[:, bank_rows - 1, :page_count].astype(jnp.int32)
    slot_row = (
        jnp.arange(ep_count, dtype=jnp.int32)[:, None] * bank_rows
        + jnp.arange(page_count, dtype=jnp.int32)[None, :] * PAGE
    )
    page_match = held.reshape(-1)[None, :] == jnp.arange(seg_count * SEG_PAGES, dtype=jnp.int32)[:, None]
    row_table = jnp.sum(jnp.where(page_match, slot_row.reshape(-1)[None, :], 0), axis=1).astype(jnp.int32)
    attended = attention(seg_lengths, cache_age, row_table, queries, window, bank, seg_count, SEG_MOST)
    return routed_experts(attended, w_out, resid, norm_gain, routes, route_probs, w_gate_up, w_down)


def solution(mesh):
    placed = (
        P(("tok", "ep"), None),
        P(("tok", "ep"), None),
        P("ep", "tok", None, None),
        P("ep"),
        P(),
        P(),
        P("tok", None),
        P(),
        P(("tok", "ep"), None),
        P(("tok", "ep"), None),
        P(("tok", "ep"), None, None),
        P(("tok", "ep"), None, None),
    )
    return jax.shard_map(
        on_device, mesh=mesh, in_specs=placed, out_specs=P(("tok", "ep"), None), check_vma=False
    )
```

```python
import functools
import math

import jax
import jax.numpy as jnp
from jax import lax
from jax.experimental import pallas as pl
from jax.experimental.pallas import tpu as pltpu
from jax.sharding import PartitionSpec as P

D = 2048
FF = 768
HEAD = 128
QPG = 8
TOP = 8
PAGE = 64
SEG_PAGES = 8
SEG_MOST = 2048
STEP = 512
META_ROWS = 16


NEG_FILL = -1e30
NORM_EPS = 1e-06


def attention_kernel(tok_dev, segs, lengths_ref, age_ref, row_ref, q_hbm, window_hbm, bank_hbm, out_ref, q_ref, window_ref, bank_ref, load_sems, seg_ref, score_ref, low_ref, top_ref, den_ref, acc_ref):
    load_q = pltpu.make_async_copy(q_hbm, q_ref, load_sems.at[0])
    load_window = pltpu.make_async_copy(window_hbm, window_ref, load_sems.at[1])
    load_bank = pltpu.make_async_copy(bank_hbm, bank_ref, load_sems.at[2])
    load_q.start()
    load_window.start()
    load_bank.start()
    begins = jnp.int32(0)
    for s in range(segs):
        seg_ref[s] = begins
        begins = begins + lengths_ref[s]
        seg_ref[segs + s] = begins
        seg_ref[2 * segs + s] = age_ref[s]
    seg_ref[3 * segs] = group_at(lax.axis_index("ep"), lax.axis_index("tok")) * q_ref.shape[0] * tok_dev
    rows = tok_dev * QPG
    held_chunks = window_ref.shape[0] // tok_dev
    opening_chunk = seg_ref[3 * segs] // tok_dev - (held_chunks - q_ref.shape[0])
    rate = math.log2(math.e) / math.sqrt(HEAD)

    def tiled(mask):
        return jnp.concatenate([mask] * QPG, axis=0)

    def one_block(block, carry):
        first = seg_ref[3 * segs] + block * tok_dev
        last = first + tok_dev - 1
        token = first + lax.broadcasted_iota(jnp.int32, (tok_dev, STEP), 0)
        column = lax.broadcasted_iota(jnp.int32, (tok_dev, STEP), 1)
        narrow = token[:, :HEAD]
        low = jnp.zeros((tok_dev, HEAD), jnp.int32)
        begin = jnp.int32(0)
        for s in range(segs):
            start = seg_ref[s]
            low = jnp.where(narrow >= start, start, low)
            begin = jnp.where(first >= start, start, begin)
        low_ref[...] = jnp.concatenate([low] * (STEP // HEAD), axis=1)
        query = jnp.concatenate([q_ref[block, :, h * HEAD:(h + 1) * HEAD] for h in range(QPG)], axis=0)
        den_ref[...] = jnp.zeros_like(den_ref)
        acc_ref[...] = jnp.zeros_like(acc_ref)

        def region(bank, steps, bank_of, mask_of, opening):
            if opening:
                held = jnp.full((rows, HEAD), NEG_FILL, jnp.float32)
            else:
                held = top_ref[...]

            def score(step, running):
                keys = jnp.concatenate([bank[pl.ds(at, size), :HEAD] for at, size in bank_of(step)], axis=0)
                scores = lax.dot_general(query, keys, (((1,), (1,)), ((), ())), preferred_element_type=jnp.float32) * rate
                scores = jnp.where(tiled(mask_of(step)), scores, NEG_FILL)
                score_ref[step] = scores
                for part in range(STEP // HEAD):
                    running = jnp.maximum(running, scores[:, part * HEAD : (part + 1) * HEAD])
                return running

            newest = lax.fori_loop(0, steps, score, held)
            newest = jnp.broadcast_to(jnp.max(newest, axis=1, keepdims=True), (rows, HEAD))
            if not opening:
                factor = jnp.exp2(held - newest)
                den_ref[...] = den_ref[...] * factor
                acc_ref[...] = acc_ref[...] * factor
            top_ref[...] = newest

            def weigh(step, ignored):
                top = top_ref[...]
                weights = jnp.exp2(score_ref[step] - jnp.concatenate([top] * (STEP // HEAD), axis=1))
                den_ref[...] += sum([weights[:, part * HEAD : (part + 1) * HEAD] for part in range(STEP // HEAD)])
                values = jnp.concatenate([bank[pl.ds(at, size), HEAD:] for at, size in bank_of(step)], axis=0)
                acc_ref[...] += jnp.dot(weights.astype(jnp.bfloat16), values, preferred_element_type=jnp.float32)
                return ignored

            lax.fori_loop(0, steps, weigh, 0)

        chunk_last = first // tok_dev
        chunk_first = begin // tok_dev
        per = STEP // tok_dev
        steps = (chunk_last - chunk_first + per) // per

        def new_chunk(step, half):
            return chunk_last - per * (step + 1) + 1 + half

        def new_bank(step):
            return [
                (pl.multiple_of(jnp.clip(new_chunk(step, half) - opening_chunk, 0, held_chunks - 1) * tok_dev, tok_dev), tok_dev)
                for half in range(per)
            ]

        def new_mask(step):
            key = new_chunk(step, 0) * tok_dev + column
            return (key >= low_ref[...]) & (key <= token)

        region(window_ref, steps, new_bank, new_mask, True)

        def cached(s, ignored):
            start, end, age = seg_ref[s], seg_ref[segs + s], seg_ref[2 * segs + s]

            @pl.when((start <= last) & (end > first) & (age > 0))
            def _():
                def page_bank(step):
                    return [(pl.multiple_of(row_ref[s * SEG_PAGES + step * (STEP // PAGE) + part], 16), PAGE) for part in range(STEP // PAGE)]

                def page_mask(step):
                    return (token >= start) & (token < end) & (step * STEP + column < age)

                region(bank_ref, (age + STEP - 1) // STEP, page_bank, page_mask, False)
            return ignored

        @pl.when(block == 0)
        def _():
            load_bank.wait()

        lax.fori_loop(0, segs, cached, 0)
        total = jnp.sum(den_ref[...], axis=1, keepdims=True)
        result = (acc_ref[...] / total).astype(jnp.bfloat16)
        for h in range(QPG):
            out_ref[block, :, h * HEAD:(h + 1) * HEAD] = result[h * tok_dev:(h + 1) * tok_dev]
        return carry

    load_q.wait()
    load_window.wait()
    lax.fori_loop(0, q_ref.shape[0], one_block, 0)


def attention(seg_lengths, cache_age, row_table, queries, window, bank, segs, seg_most):
    blocks, tok_dev, width = queries.shape
    most_steps = max(((seg_most + tok_dev) // tok_dev + STEP // tok_dev - 1) // (STEP // tok_dev), 1)
    rows = tok_dev * QPG
    return pl.pallas_call(
        functools.partial(attention_kernel, tok_dev, segs),
        out_shape=jax.ShapeDtypeStruct(queries.shape, jnp.bfloat16),
        in_specs=[pl.BlockSpec(memory_space=pltpu.SMEM)] * 3 + [pl.BlockSpec(memory_space=pl.ANY)] * 3,
        out_specs=pl.BlockSpec(memory_space=pltpu.VMEM),
        scratch_shapes=[
            pltpu.VMEM(queries.shape, jnp.bfloat16),
            pltpu.VMEM(window.shape, jnp.bfloat16),
            pltpu.VMEM(bank.shape, jnp.bfloat16),
            pltpu.SemaphoreType.DMA((3,)),
            pltpu.SMEM((3 * segs + 1,), jnp.int32),
            pltpu.VMEM((most_steps, rows, STEP), jnp.float32),
            pltpu.VMEM((tok_dev, STEP), jnp.int32),
            pltpu.VMEM((rows, HEAD), jnp.float32),
            pltpu.VMEM((rows, HEAD), jnp.float32),
            pltpu.VMEM((rows, HEAD), jnp.float32),
        ],
        compiler_params=pltpu.CompilerParams(vmem_limit_bytes=62 << 20),
        name="attend",
    )(seg_lengths, cache_age, row_table, queries, window, bank)


MESH = pl.DeviceIdType.MESH


def place_of(group, head):
    tok, tall, core = lax.div(group, 8), lax.rem(lax.div(group, 2), 4), lax.rem(group, 2)
    return (tall * 4 + lax.rem(tok + head, 4)) * 2 + core


def group_at(ep, head):
    tall, wide, core = lax.div(ep, 8), lax.rem(lax.div(ep, 2), 4), lax.rem(ep, 2)
    return lax.rem(wide + 4 - head, 4) * 8 + 2 * tall + core


def owner_of(group, block):
    tok = lax.div(group, 8)
    return tok, lax.rem(group, 8) * 4 + block


def exchange_kernel(
    qkv_ref, cache_ref, slots_ref, query_ref, window_ref, bank_ref,
    stage_q, stage_kv, stage_slots, load_sems, key_send, key_recv, query_send, query_recv, pass_send, pass_recv, own_sem, line_send, line_recv,
    plane_send, plane_recv, pair_send, pair_recv,
):
    tok, ep = lax.axis_index("tok"), lax.axis_index("ep")
    tok_dev = qkv_ref.shape[0]
    q_width = QPG * HEAD
    number = tok * 32 + ep
    group, block = lax.div(number, 4), lax.rem(number, 4)
    mine = group_at(ep, tok)
    reach = SEG_MOST // (4 * tok_dev)
    span = 4 * tok_dev

    def column(head):
        return head * (q_width + 2 * HEAD)

    def remote(source, place, send_sem, recv_sem, device):
        return pltpu.make_async_remote_copy(
            src_ref=source, dst_ref=place, send_sem=send_sem, recv_sem=recv_sem, device_id=device, device_id_type=MESH
        )

    def load(turn, keys):
        head = lax.rem(tok + turn, 4)
        if keys:
            source = qkv_ref.at[:, pl.ds(pl.multiple_of(column(head) + q_width, HEAD), 2 * HEAD)]
            return pltpu.make_async_copy(source, stage_kv.at[turn], load_sems.at[turn])
        source = qkv_ref.at[:, pl.ds(pl.multiple_of(column(head), HEAD), q_width)]
        return pltpu.make_async_copy(source, stage_q.at[turn], load_sems.at[4 + turn])

    for keys in (True, False):
        for turn in range(4):
            load(turn, keys).start()

    def key_copy(turn):
        head = lax.rem(tok + turn, 4)
        place = window_ref.at[pl.ds(pl.multiple_of(reach * span + block * tok_dev, tok_dev), tok_dev)]
        return stage_kv.at[turn], place, key_send.at[turn], key_recv, (head, place_of(group, head))

    def query_copy(turn):
        head = lax.rem(tok + turn, 4)
        return stage_q.at[turn], query_ref.at[block], query_send.at[turn], query_recv, (head, place_of(group, head))

    def spans(index):
        return window_ref.at[pl.ds(pl.multiple_of(index * span, span), span)]

    def pass_copy(turn):
        device = (tok, place_of(lax.rem(mine + 2 * turn, 32), tok))
        return spans(reach), spans(reach - 2 * turn), pass_send.at[turn - 1], pass_recv.at[turn - 1], device

    def cross_copy(turn):
        device = (tok, at(tall, wide, 1 - core))
        return spans(6 - 2 * turn - 2 * core), spans(5 - 2 * turn), pass_send.at[turn + 1], pass_recv.at[turn + 1], device

    held, told = cache_ref.shape[0], stage_slots.shape[0]
    piece = held + told
    cut = piece // 32 * 16
    tall, wide, core = lax.div(ep, 8), lax.rem(lax.div(ep, 2), 4), lax.rem(ep, 2)

    def at(y, x, c):
        return (lax.rem(y, 4) * 4 + lax.rem(x, 4)) * 2 + c

    def part(y, x, c, start, size):
        return bank_ref.at[pl.ds(pl.multiple_of(at(y, x, c) * piece + start, 16), size)]

    lane = lax.broadcasted_iota(jnp.int32, stage_slots.shape, 1)
    listed = jnp.zeros(stage_slots.shape, jnp.float32)
    for page in range(slots_ref.shape[0]):
        listed = jnp.where(lane == page, slots_ref[page].astype(jnp.float32), listed)
    stage_slots[...] = listed.astype(jnp.bfloat16)
    own_cache = pltpu.make_async_copy(cache_ref, part(tall, wide, core, 0, held), own_sem.at[0])
    own_slots = pltpu.make_async_copy(stage_slots, part(tall, wide, core, held, told), own_sem.at[1])
    own_cache.start()
    own_slots.start()

    def line_copies():
        for turn in range(1, 4):
            first = part(tall, wide, core, 0, cut)
            yield remote(first, first, line_send, line_recv, (tok, at(tall, wide + turn, core)))
            rest = part(tall, wide, core, cut, piece - cut)
            yield remote(rest, rest, line_send, line_recv, (tok, at(tall + turn, wide, core)))

    def plane_copies():
        for turn in range(1, 4):
            for along in range(4):
                first = part(tall, wide + along, core, 0, cut)
                yield remote(first, first, plane_send, plane_recv, (tok, at(tall + turn, wide, core)))
                rest = part(tall + along, wide, core, cut, piece - cut)
                yield remote(rest, rest, plane_send, plane_recv, (tok, at(tall, wide + turn, core)))

    def pair_copies():
        for y in range(4):
            for x in range(4):
                whole = part(y, x, core, 0, piece)
                yield remote(whole, whole, pair_send, pair_recv, (tok, at(tall, wide, 1 - core)))

    def settle(rows, sem):
        pltpu.make_async_copy(bank_ref.at[pl.ds(0, rows)], bank_ref.at[pl.ds(0, rows)], sem).wait()

    barrier = pltpu.get_barrier_semaphore()
    at_home = place_of(group, tok) == ep
    for turn in range(1, 4):
        for partner in (at(tall, wide + turn, core), at(tall + turn, wide, core)):
            pl.semaphore_signal(barrier, inc=1, device_id=(tok, partner), device_id_type=MESH)
    pl.semaphore_signal(barrier, inc=1, device_id=(tok, at(tall, wide, 1 - core)), device_id_type=MESH)
    for turn in range(4):
        theirs = owner_of(mine, turn)

        @pl.when(jnp.logical_not((theirs[0] == tok) & (theirs[1] == ep)))
        def _():
            pl.semaphore_signal(barrier, inc=1, device_id=theirs, device_id_type=MESH)

    for turn in range(1, 3):
        pl.semaphore_signal(
            barrier, inc=1, device_id=(tok, place_of(lax.rem(mine + 32 - 2 * turn, 32), tok)), device_id_type=MESH
        )
    pl.semaphore_wait(barrier, 13 - jnp.where(at_home, 1, 0))

    def send_each(copy, turns=range(4)):
        for turn in turns:
            source, place, send_sem, recv_sem, device = copy(turn)
            load(turn, copy is key_copy).wait()
            if turn == 0:

                @pl.when(at_home)
                def _():
                    pltpu.make_async_copy(source, place, recv_sem).start()

                @pl.when(jnp.logical_not(at_home))
                def _():
                    remote(source, place, send_sem, recv_sem, device).start()
            else:
                remote(source, place, send_sem, recv_sem, device).start()

    own = window_ref.at[pl.ds(reach * span, span)]
    send_each(key_copy)
    own_cache.wait()
    own_slots.wait()
    for line_copy in line_copies():
        line_copy.start()
    pltpu.make_async_copy(own, own, key_recv).wait()
    for turn in range(1, 3):
        remote(*pass_copy(turn)).start()
    settle(3 * piece, line_recv)
    for plane_copy in plane_copies():
        plane_copy.start()
    send_each(query_copy)
    settle(12 * piece, plane_recv)
    for pair_copy in pair_copies():
        pair_copy.start()
    for turn in range(1, 3):
        remote(*pass_copy(turn)).wait()
    for turn in range(1, 3):
        remote(*cross_copy(turn)).start()
    for turn in range(1, 3):
        remote(*cross_copy(turn)).wait()
    pltpu.make_async_copy(query_ref, query_ref, query_recv).wait()
    for copy in (key_copy, query_copy):
        for turn in range(4):
            if turn == 0:

                @pl.when(jnp.logical_not(at_home))
                def _():
                    remote(*copy(turn)).wait_send()
            else:
                remote(*copy(turn)).wait_send()
    settle(16 * piece, pair_recv)
    settle(3 * piece, line_send)
    settle(12 * piece, plane_send)
    settle(16 * piece, pair_send)


def exchange(qkv, cached, slots):
    tok_dev = qkv.shape[0]
    reach = SEG_MOST // (4 * tok_dev)
    kept = pl.BlockSpec(memory_space=pl.ANY)
    return pl.pallas_call(
        exchange_kernel,
        out_shape=(
            jax.ShapeDtypeStruct((4, tok_dev, QPG * HEAD), jnp.bfloat16),
            jax.ShapeDtypeStruct(((reach + 1) * 4 * tok_dev, 2 * HEAD), jnp.bfloat16),
            jax.ShapeDtypeStruct((32 * (cached.shape[0] + META_ROWS), 2 * HEAD), jnp.bfloat16),
        ),
        in_specs=[kept] * 2 + [pl.BlockSpec(memory_space=pltpu.SMEM)],
        out_specs=(kept,) * 3,
        scratch_shapes=[
            pltpu.VMEM((4, tok_dev, QPG * HEAD), jnp.bfloat16),
            pltpu.VMEM((4, tok_dev, 2 * HEAD), jnp.bfloat16),
            pltpu.VMEM((META_ROWS, 2 * HEAD), jnp.bfloat16),
            pltpu.SemaphoreType.DMA((8,)),
            pltpu.SemaphoreType.DMA((4,)),
            pltpu.SemaphoreType.DMA,
            pltpu.SemaphoreType.DMA((4,)),
            pltpu.SemaphoreType.DMA,
            pltpu.SemaphoreType.DMA((4,)),
            pltpu.SemaphoreType.DMA((4,)),
            pltpu.SemaphoreType.DMA((2,)),
        ]
        + [pltpu.SemaphoreType.DMA] * 6,
        compiler_params=pltpu.CompilerParams(collective_id=1, has_side_effects=True),
        cost_estimate=pl.CostEstimate(flops=0, bytes_accessed=80 << 20, transcendentals=0),
        name="exchange",
    )(qkv, cached, slots)


CAP = 16
SIDE = 4
PLANE = 32
CUTS = ((0, 768), (768, 640), (1408, 640))


def position():
    tok, ep = lax.axis_index("tok"), lax.axis_index("ep")
    return tok, lax.div(ep, 8), lax.rem(lax.div(ep, 2), 4), lax.rem(ep, 2)


def moved(offsets, way):
    at = [lax.rem(own + size + way * off, size) for own, off, size in zip(position(), offsets, (4, 4, 4, 2))]
    return at[0], (at[1] * 4 + at[2]) * 2 + at[3]


def plane_offsets(cut, index, div, rem):
    core, outer, inner = div(index, 16), rem(div(index, 4), 4), rem(index, 4)
    return ((0, inner, outer, core), (inner, 0, outer, core), (outer, inner, 0, core))[cut]


def mixed_order(j):
    return lax.rem(j, 4) * 4 + lax.rem(lax.div(j, 4) + j, 4)


def line_offsets(cut, turn):
    return tuple(turn if axis == cut else 0 for axis in range(3)) + (0,)


def routed_kernel(
    attended_hbm, weight_hbm, resid_ref, gain_ref, table_ref, gate_up_hbm, down_hbm, out_ref,
    attended_ref, weight_ref, projected, heads, mixed_ref,
    line0, line1, line2, stage0, stage1, stage2, came0, came1, came2, back0, back1, back2,
    inbox0, inbox1, inbox2, sum0, sum1, sum2,
    gate_up, down, tables, rank, share, pick, rows_in,
    weight_sems, table_sems, line_send, line_recv, out_send, near_recv, far_recv, home_send, home_recv,
    part_send, part_recv, head_send, head_recv,
):
    lines, stages, cames, backs = (line0, line1, line2), (stage0, stage1, stage2), (came0, came1, came2), (back0, back1, back2)
    inboxes, sums = (inbox0, inbox1, inbox2), (sum0, sum1, sum2)
    tokens = resid_ref.shape[0]
    width = down.shape[0]
    devices = SIDE * PLANE
    message = SIDE * CAP
    load_attended = pltpu.make_async_copy(attended_hbm, attended_ref, weight_sems.at[2])
    load_weight = pltpu.make_async_copy(weight_hbm, weight_ref, weight_sems.at[3])
    load_attended.start()
    load_weight.start()
    load_gate_up = pltpu.make_async_copy(gate_up_hbm.at[0], gate_up, weight_sems.at[0])
    load_down = pltpu.make_async_copy(down_hbm.at[0], down, weight_sems.at[1])
    barrier = pltpu.get_barrier_semaphore()

    def greet(step, ignored):
        offsets = (lax.div(step, 32), lax.rem(lax.div(step, 8), 4), lax.rem(lax.div(step, 2), 4), lax.rem(step, 2))
        pl.semaphore_signal(barrier, inc=1, device_id=moved(offsets, 1), device_id_type=MESH)
        return ignored

    lax.fori_loop(1, devices, greet, 0)
    for cut in range(3):
        tables[cut, 0] = table_ref[...]
    tok, ep = lax.axis_index("tok"), lax.axis_index("ep")
    mine = group_at(ep, tok)
    home = [owner_of(mine, turn) for turn in range(4)]
    is_own = [(place[0] == tok) & (place[1] == ep) for place in home]

    def project(turn):
        projected[turn] = jnp.dot(
            attended_ref[turn], weight_ref[...], preferred_element_type=jnp.float32
        ).astype(jnp.bfloat16)

    load_attended.wait()
    load_weight.wait()
    load_gate_up.start()
    load_down.start()
    project(0)
    pl.semaphore_wait(barrier, devices - 1)

    def remote(source, place, send_sem, recv_sem, device):
        return pltpu.make_async_remote_copy(
            src_ref=source, dst_ref=place, send_sem=send_sem, recv_sem=recv_sem, device_id=device, device_id_type=MESH
        )

    def rows_of(ref, start, size):
        return ref.at[pl.ds(pl.multiple_of(start, CAP), size)]

    def settle(ref, size, sem):
        pltpu.make_async_copy(ref.at[pl.ds(0, size)], ref.at[pl.ds(0, size)], sem).wait()

    for cut in range(3):
        for turn in range(1, SIDE):
            remote(
                table_ref, tables.at[cut, turn], table_sems.at[0], table_sems.at[1], moved(line_offsets(cut, turn), 1)
            ).start()
    def head_copy(turn):
        return remote(projected.at[turn], heads.at[tok], head_send.at[turn], head_recv, home[turn])

    for turn in range(4):
        if turn:
            project(turn)

        @pl.when(is_own[turn])
        def _():
            pltpu.make_async_copy(projected.at[turn], heads.at[tok], head_recv).start()

        @pl.when(jnp.logical_not(is_own[turn]))
        def _():
            head_copy(turn).start()

    pltpu.make_async_copy(tables.at[:, pl.ds(0, 3)], tables.at[:, pl.ds(0, 3)], table_sems.at[1]).wait()
    before = (
        lax.broadcasted_iota(jnp.int32, (tokens, tokens), 0) < lax.broadcasted_iota(jnp.int32, (tokens, tokens), 1)
    ).astype(jnp.bfloat16)
    index = lax.broadcasted_iota(jnp.int32, (PLANE, tokens), 0)
    shift = {16: 4, 4: 2}
    top = table_ref.shape[0] // 2
    for cut in range(3):
        offsets = plane_offsets(cut, index, lambda v, d: v >> shift[d], lambda v, d: v & (d - 1))
        z, y, x, c = [(own + off) & (size - 1) for own, off, size in zip(position(), offsets, (4, 4, 4, 2))]
        expert = (z * 32 + y * 8 + x * 2 + c).astype(jnp.float32)
        for turn in range(SIDE):
            probs = tables[cut, turn, top:, :]
            shares = probs / jnp.sum(probs, axis=0, keepdims=True)
            named = jnp.zeros((PLANE, tokens), jnp.float32)
            owed = jnp.zeros((PLANE, tokens), jnp.float32)
            for k in range(top):
                match = expert == tables[cut, turn, k : k + 1, :]
                named = jnp.where(match, 1.0, named)
                owed = jnp.where(match, shares[k : k + 1, :], owed)
            earlier = jnp.dot(named.astype(jnp.bfloat16), before, preferred_element_type=jnp.float32)
            at = (cut * SIDE + turn) * PLANE
            rank[at : at + PLANE, :] = jnp.where(named > 0.0, earlier, -1.0)
            share[at : at + PLANE, :] = owed

    pltpu.make_async_copy(heads, heads, head_recv).wait()
    added = resid_ref[...].astype(jnp.float32)
    for head in range(4):
        added = added + heads[head].astype(jnp.float32)
    mixed_ref[...] = added.astype(jnp.bfloat16)
    wide = mixed_ref[...].astype(jnp.float32)
    level = lax.rsqrt(jnp.mean(wide * wide, axis=-1, keepdims=True) + NORM_EPS)
    for cut, (start, size) in enumerate(CUTS):
        part = mixed_ref[:, start : start + size].astype(jnp.float32)
        lines[cut][:tokens] = (part * level * gain_ref[:, start : start + size]).astype(jnp.bfloat16)
    for turn in (1, 3, 2):
        for cut in range(3):
            remote(
                rows_of(lines[cut], 0, tokens), rows_of(lines[cut], turn * tokens, tokens),
                line_send.at[cut], line_recv.at[cut], moved(line_offsets(cut, turn), 1),
            ).start()

    slot = lax.broadcasted_iota(jnp.int32, (CAP, tokens), 0).astype(jnp.float32)

    def choose(cut, core, turn, weighted):
        for j in range(16):
            at = (cut * SIDE + turn) * PLANE + core * 16 + j
            chosen = share[pl.ds(at, 1), :] if weighted else 1.0
            pick[j * CAP : (j + 1) * CAP, :] = jnp.where(rank[pl.ds(at, 1), :] == slot, chosen, 0.0).astype(jnp.bfloat16)

    def send(cut, i, recv_sem):
        source, place = rows_of(stages[cut], i * message, message), rows_of(cames[cut], i * message, message)
        offsets = plane_offsets(cut, i, lax.div, lax.rem)

        @pl.when(i == 0)
        def _():
            pltpu.make_async_copy(source, place, recv_sem).start()

        @pl.when(i > 0)
        def _():
            remote(source, place, out_send.at[cut], recv_sem, moved(offsets, 1)).start()

    def fill(cut, core):
        def one_shard(turn, ignored):
            choose(cut, core, turn, False)
            found = jnp.dot(
                pick[...], rows_of(lines[cut], turn * tokens, tokens)[...], preferred_element_type=jnp.float32
            ).astype(jnp.bfloat16)
            for j in range(16):
                rows_of(stages[cut], (core * 16 + j) * message + turn * CAP, CAP)[...] = found[j * CAP : (j + 1) * CAP]
            return ignored

        lax.fori_loop(0, SIDE, one_shard, 0)

    def dispatch(core, ignored):
        def send_one(cut, order):
            j = mixed_order(order)
            arrival = far_recv.at[core] if cut == 2 else near_recv.at[cut, core * 4 + lax.div(j, 4)]
            send(cut, core * 16 + j, arrival)

        for cut in (2, 0, 1):
            fill(cut, core)

            def send_first(order, inner, cut=cut):
                send_one(cut, order)
                return inner

            lax.fori_loop(0, 4, send_first, 0)

        def send_all(order, inner):
            for cut in (2, 0, 1):
                send_one(cut, order)
            return inner

        return lax.fori_loop(4, 16, send_all, ignored)

    for cut in range(3):
        settle(lines[cut], 3 * tokens, line_recv.at[cut])
        settle(lines[cut], 3 * tokens, line_send.at[cut])
    lax.fori_loop(0, 2, dispatch, 0)
    load_gate_up.wait()
    load_down.wait()
    block = SIDE * message

    def slab1(chunk, j):
        return rows_of(came1, chunk * block + (j % 4) * message + (j // 4) * CAP, CAP)

    def slab2(chunk, j):
        core, wide = lax.div(chunk, 4), lax.rem(chunk, 4)
        return rows_of(came2, (core * 16 + (j % 4) * 4 + j // 4) * message + wide * CAP, CAP)

    def give(cut, i):
        source, place = rows_of(cames[cut], i * message, message), rows_of(backs[cut], i * message, message)
        offsets = plane_offsets(cut, i, lax.div, lax.rem)
        recv_sem = home_recv.at[cut, lax.div(i, 16)]

        @pl.when(i == 0)
        def _():
            pltpu.make_async_copy(source, place, recv_sem).start()

        @pl.when(i > 0)
        def _():
            remote(source, place, home_send.at[cut], recv_sem, moved(offsets, -1)).start()

    def work(chunk, ignored):
        @pl.when(lax.rem(chunk, 4) == 0)
        def _():
            settle(came2, 16 * message, far_recv.at[lax.div(chunk, 4)])

        settle(came0, block, near_recv.at[0, chunk])
        settle(came1, block, near_recv.at[1, chunk])
        rows_in[:, 0:768] = rows_of(came0, chunk * block, block)[...]
        for j in range(16):
            rows_in[j * CAP : (j + 1) * CAP, 768:1408] = slab1(chunk, j)[...]
            rows_in[j * CAP : (j + 1) * CAP, 1408:2048] = slab2(chunk, j)[...]
        gate = jnp.dot(rows_in[...], gate_up[:, :width], preferred_element_type=jnp.float32)
        up = jnp.dot(rows_in[...], gate_up[:, width:], preferred_element_type=jnp.float32)
        hidden = (gate * jax.nn.sigmoid(gate) * up).astype(jnp.bfloat16)
        made = jnp.dot(hidden, down[...], preferred_element_type=jnp.float32).astype(jnp.bfloat16)
        rows_of(came0, chunk * block, block)[...] = made[:, 0:768]
        for j in range(16):
            slab1(chunk, j)[...] = made[j * CAP : (j + 1) * CAP, 768:1408]
            slab2(chunk, j)[...] = made[j * CAP : (j + 1) * CAP, 1408:2048]

        @pl.when(lax.rem(chunk, 4) == 3)
        def _():
            def give_all(order, inner):
                for cut in (2, 0, 1):
                    give(cut, lax.div(chunk, 4) * 16 + mixed_order(order))
                return inner

            lax.fori_loop(0, 16, give_all, 0)

        return ignored

    lax.fori_loop(0, 8, work, 0)

    for cut in range(3):
        sums[cut][...] = jnp.zeros_like(sums[cut])

    def combine(core, ignored):
        for cut in range(3):
            settle(backs[cut], 16 * message, home_recv.at[cut, core])

            def one_shard(turn, inner):
                choose(cut, core, turn, True)
                found = jnp.concatenate(
                    [rows_of(backs[cut], (core * 16 + j) * message + turn * CAP, CAP)[...] for j in range(16)], axis=0
                )
                total = rows_of(sums[cut], turn * tokens, tokens)
                total[...] += lax.dot_general(
                    pick[...], found, (((0,), (0,)), ((), ())), preferred_element_type=jnp.float32
                )
                return inner

            lax.fori_loop(0, SIDE, one_shard, 0)

            @pl.when(core == 1)
            def _():
                lines[cut][...] = sums[cut][...].astype(jnp.bfloat16)
                for turn in range(1, SIDE):
                    remote(
                        rows_of(lines[cut], turn * tokens, tokens), rows_of(inboxes[cut], turn * tokens, tokens),
                        part_send.at[cut], part_recv.at[cut], moved(line_offsets(cut, turn), -1),
                    ).start()

        return ignored

    lax.fori_loop(0, 2, combine, 0)
    for cut, (start, size) in enumerate(CUTS):
        settle(inboxes[cut], 3 * tokens, part_recv.at[cut])
        total = mixed_ref[:, start : start + size].astype(jnp.float32) + sums[cut][:tokens]
        for turn in range(1, SIDE):
            total = total + inboxes[cut][turn * tokens : (turn + 1) * tokens].astype(jnp.float32)
        out_ref[:, start : start + size] = total.astype(jnp.bfloat16)
    pltpu.make_async_copy(tables.at[:, pl.ds(0, 3)], tables.at[:, pl.ds(0, 3)], table_sems.at[0]).wait()
    for cut in range(3):
        settle(stages[cut], (PLANE - 1) * message, out_send.at[cut])
        settle(stages[cut], (PLANE - 1) * message, home_send.at[cut])
        settle(lines[cut], 3 * tokens, part_send.at[cut])
    for turn in range(4):

        @pl.when(jnp.logical_not(is_own[turn]))
        def _():
            head_copy(turn).wait_send()


def routed_experts(attended, weight, resid, gain, routes, probs, gate_up, down):
    tokens, width = resid.shape
    vmem = pl.BlockSpec(memory_space=pltpu.VMEM)
    kept = pl.BlockSpec(memory_space=pl.ANY)
    slots = SIDE * PLANE * CAP
    flops = 2 * slots * width * (down.shape[1] * 3 + 2 * tokens)
    table = jnp.concatenate([routes.T.astype(jnp.float32), probs.T], axis=0)

    def each(rows, kind):
        return [pltpu.VMEM((rows, size), kind) for start, size in CUTS]

    return pl.pallas_call(
        routed_kernel,
        out_shape=jax.ShapeDtypeStruct(resid.shape, jnp.bfloat16),
        in_specs=[kept] * 2 + [vmem] * 3 + [kept] * 2,
        out_specs=vmem,
        scratch_shapes=[
            pltpu.VMEM(attended.shape, jnp.bfloat16),
            pltpu.VMEM(weight.shape, jnp.bfloat16),
            pltpu.VMEM((4, tokens, width), jnp.bfloat16),
            pltpu.VMEM((4, tokens, width), jnp.bfloat16),
            pltpu.VMEM((tokens, width), jnp.bfloat16),
        ]
        + each(SIDE * tokens, jnp.bfloat16)
        + each(slots, jnp.bfloat16)
        + each(slots, jnp.bfloat16)
        + each(slots, jnp.bfloat16)
        + each(SIDE * tokens, jnp.bfloat16)
        + each(SIDE * tokens, jnp.float32)
        + [
            pltpu.VMEM(gate_up.shape[1:], jnp.bfloat16),
            pltpu.VMEM(down.shape[1:], jnp.bfloat16),
            pltpu.VMEM((3, SIDE, 2 * routes.shape[1], tokens), jnp.float32),
            pltpu.VMEM((3 * SIDE * PLANE, tokens), jnp.float32),
            pltpu.VMEM((3 * SIDE * PLANE, tokens), jnp.float32),
            pltpu.VMEM((16 * CAP, tokens), jnp.bfloat16),
            pltpu.VMEM((16 * CAP, width), jnp.bfloat16),
            pltpu.SemaphoreType.DMA((4,)),
            pltpu.SemaphoreType.DMA((2,)),
            pltpu.SemaphoreType.DMA((3,)),
            pltpu.SemaphoreType.DMA((3,)),
            pltpu.SemaphoreType.DMA((3,)),
            pltpu.SemaphoreType.DMA((2, 8)),
            pltpu.SemaphoreType.DMA((2,)),
            pltpu.SemaphoreType.DMA((3,)),
            pltpu.SemaphoreType.DMA((3, 2)),
            pltpu.SemaphoreType.DMA((3,)),
            pltpu.SemaphoreType.DMA((3,)),
            pltpu.SemaphoreType.DMA((4,)),
            pltpu.SemaphoreType.DMA,
        ],
        compiler_params=pltpu.CompilerParams(collective_id=0, has_side_effects=True, vmem_limit_bytes=62 << 20),
        cost_estimate=pl.CostEstimate(flops=flops, bytes_accessed=6 * slots * width * 2, transcendentals=0),
        name="routed_experts",
    )(attended, weight, resid, gain[None, :], table, gate_up, down)


def on_device(
    resid,
    qkv,
    cache_kv,
    page_slot,
    seg_lengths,
    cache_age,
    w_out,
    norm_gain,
    routes,
    route_probs,
    w_gate_up,
    w_down,
):
    ep_count = lax.axis_size("ep")
    tok_dev = resid.shape[0]
    seg_count = seg_lengths.shape[0]
    page_count = cache_kv.shape[0]
    bank_rows = page_count * PAGE + META_ROWS
    queries, window, bank = exchange(qkv, cache_kv.reshape(page_count * PAGE, 2 * HEAD), page_slot)
    held = bank.reshape(ep_count, bank_rows, 2 * HEAD)[:, bank_rows - 1, :page_count].astype(jnp.int32)
    slot_row = (
        jnp.arange(ep_count, dtype=jnp.int32)[:, None] * bank_rows
        + jnp.arange(page_count, dtype=jnp.int32)[None, :] * PAGE
    )
    page_match = held.reshape(-1)[None, :] == jnp.arange(seg_count * SEG_PAGES, dtype=jnp.int32)[:, None]
    row_table = jnp.sum(jnp.where(page_match, slot_row.reshape(-1)[None, :], 0), axis=1).astype(jnp.int32)
    attended = attention(seg_lengths, cache_age, row_table, queries, window, bank, seg_count, SEG_MOST)
    return routed_experts(attended, w_out, resid, norm_gain, routes, route_probs, w_gate_up, w_down)


def solution(mesh):
    placed = (
        P(("tok", "ep"), None),
        P(("tok", "ep"), None),
        P("ep", "tok", None, None),
        P("ep"),
        P(),
        P(),
        P("tok", None),
        P(),
        P(("tok", "ep"), None),
        P(("tok", "ep"), None),
        P(("tok", "ep"), None, None),
        P(("tok", "ep"), None, None),
    )
    return jax.shard_map(
        on_device, mesh=mesh, in_specs=placed, out_specs=P(("tok", "ep"), None), check_vma=False
    )
```

```python
import functools
import math

import jax
import jax.numpy as jnp
from jax import lax
from jax.experimental import pallas as pl
from jax.experimental.pallas import tpu as pltpu
from jax.sharding import PartitionSpec as P

D = 2048
FF = 768
HEAD = 128
QPG = 8
TOP = 8
PAGE = 64
SEG_PAGES = 8
SEG_MOST = 2048
STEP = 512
META_ROWS = 16


NEG_FILL = -1e30
NORM_EPS = 1e-06


def attention_kernel(tok_dev, segs, lengths_ref, age_ref, row_ref, q_hbm, window_hbm, bank_hbm, out_ref, q_ref, window_ref, bank_ref, load_sems, seg_ref, score_ref, low_ref, top_ref, den_ref, acc_ref):
    load_q = pltpu.make_async_copy(q_hbm, q_ref, load_sems.at[0])
    load_window = pltpu.make_async_copy(window_hbm, window_ref, load_sems.at[1])
    load_bank = pltpu.make_async_copy(bank_hbm, bank_ref, load_sems.at[2])
    load_q.start()
    load_window.start()
    load_bank.start()
    begins = jnp.int32(0)
    for s in range(segs):
        seg_ref[s] = begins
        begins = begins + lengths_ref[s]
        seg_ref[segs + s] = begins
        seg_ref[2 * segs + s] = age_ref[s]
    seg_ref[3 * segs] = group_at(lax.axis_index("ep"), lax.axis_index("tok")) * q_ref.shape[0] * tok_dev
    rows = tok_dev * QPG
    held_chunks = window_ref.shape[0] // tok_dev
    opening_chunk = seg_ref[3 * segs] // tok_dev - (held_chunks - q_ref.shape[0])
    rate = math.log2(math.e) / math.sqrt(HEAD)

    def tiled(mask):
        return jnp.concatenate([mask] * QPG, axis=0)

    def one_block(block, carry):
        first = seg_ref[3 * segs] + block * tok_dev
        last = first + tok_dev - 1
        token = first + lax.broadcasted_iota(jnp.int32, (tok_dev, STEP), 0)
        column = lax.broadcasted_iota(jnp.int32, (tok_dev, STEP), 1)
        narrow = token[:, :HEAD]
        low = jnp.zeros((tok_dev, HEAD), jnp.int32)
        begin = jnp.int32(0)
        for s in range(segs):
            start = seg_ref[s]
            low = jnp.where(narrow >= start, start, low)
            begin = jnp.where(first >= start, start, begin)
        low_ref[...] = jnp.concatenate([low] * (STEP // HEAD), axis=1)
        query = jnp.concatenate([q_ref[block, :, h * HEAD:(h + 1) * HEAD] for h in range(QPG)], axis=0)
        den_ref[...] = jnp.zeros_like(den_ref)
        acc_ref[...] = jnp.zeros_like(acc_ref)

        def region(bank, steps, bank_of, mask_of, opening):
            if opening:
                held = jnp.full((rows, HEAD), NEG_FILL, jnp.float32)
            else:
                held = top_ref[...]

            def score(step, running):
                keys = jnp.concatenate([bank[pl.ds(at, size), :HEAD] for at, size in bank_of(step)], axis=0)
                scores = lax.dot_general(query, keys, (((1,), (1,)), ((), ())), preferred_element_type=jnp.float32) * rate
                scores = jnp.where(tiled(mask_of(step)), scores, NEG_FILL)
                score_ref[step] = scores
                for part in range(STEP // HEAD):
                    running = jnp.maximum(running, scores[:, part * HEAD : (part + 1) * HEAD])
                return running

            newest = lax.fori_loop(0, steps, score, held)
            newest = jnp.broadcast_to(jnp.max(newest, axis=1, keepdims=True), (rows, HEAD))
            if not opening:
                factor = jnp.exp2(held - newest)
                den_ref[...] = den_ref[...] * factor
                acc_ref[...] = acc_ref[...] * factor
            top_ref[...] = newest

            def weigh(step, ignored):
                top = top_ref[...]
                weights = jnp.exp2(score_ref[step] - jnp.concatenate([top] * (STEP // HEAD), axis=1))
                den_ref[...] += sum([weights[:, part * HEAD : (part + 1) * HEAD] for part in range(STEP // HEAD)])
                values = jnp.concatenate([bank[pl.ds(at, size), HEAD:] for at, size in bank_of(step)], axis=0)
                acc_ref[...] += jnp.dot(weights.astype(jnp.bfloat16), values, preferred_element_type=jnp.float32)
                return ignored

            lax.fori_loop(0, steps, weigh, 0)

        chunk_last = first // tok_dev
        chunk_first = begin // tok_dev
        per = STEP // tok_dev
        steps = (chunk_last - chunk_first + per) // per

        def new_chunk(step, half):
            return chunk_last - per * (step + 1) + 1 + half

        def new_bank(step):
            return [
                (pl.multiple_of(jnp.clip(new_chunk(step, half) - opening_chunk, 0, held_chunks - 1) * tok_dev, tok_dev), tok_dev)
                for half in range(per)
            ]

        def new_mask(step):
            key = new_chunk(step, 0) * tok_dev + column
            return (key >= low_ref[...]) & (key <= token)

        region(window_ref, steps, new_bank, new_mask, True)

        def cached(s, ignored):
            start, end, age = seg_ref[s], seg_ref[segs + s], seg_ref[2 * segs + s]

            @pl.when((start <= last) & (end > first) & (age > 0))
            def _():
                def page_bank(step):
                    return [(pl.multiple_of(row_ref[s * SEG_PAGES + step * (STEP // PAGE) + part], 16), PAGE) for part in range(STEP // PAGE)]

                def page_mask(step):
                    return (token >= start) & (token < end) & (step * STEP + column < age)

                region(bank_ref, (age + STEP - 1) // STEP, page_bank, page_mask, False)
            return ignored

        @pl.when(block == 0)
        def _():
            load_bank.wait()

        lax.fori_loop(0, segs, cached, 0)
        total = jnp.sum(den_ref[...], axis=1, keepdims=True)
        result = (acc_ref[...] / total).astype(jnp.bfloat16)
        for h in range(QPG):
            out_ref[block, :, h * HEAD:(h + 1) * HEAD] = result[h * tok_dev:(h + 1) * tok_dev]
        return carry

    load_q.wait()
    load_window.wait()
    lax.fori_loop(0, q_ref.shape[0], one_block, 0)


def attention(seg_lengths, cache_age, row_table, queries, window, bank, segs, seg_most):
    blocks, tok_dev, width = queries.shape
    most_steps = max(((seg_most + tok_dev) // tok_dev + STEP // tok_dev - 1) // (STEP // tok_dev), 1)
    rows = tok_dev * QPG
    return pl.pallas_call(
        functools.partial(attention_kernel, tok_dev, segs),
        out_shape=jax.ShapeDtypeStruct(queries.shape, jnp.bfloat16),
        in_specs=[pl.BlockSpec(memory_space=pltpu.SMEM)] * 3 + [pl.BlockSpec(memory_space=pl.ANY)] * 3,
        out_specs=pl.BlockSpec(memory_space=pltpu.VMEM),
        scratch_shapes=[
            pltpu.VMEM(queries.shape, jnp.bfloat16),
            pltpu.VMEM(window.shape, jnp.bfloat16),
            pltpu.VMEM(bank.shape, jnp.bfloat16),
            pltpu.SemaphoreType.DMA((3,)),
            pltpu.SMEM((3 * segs + 1,), jnp.int32),
            pltpu.VMEM((most_steps, rows, STEP), jnp.float32),
            pltpu.VMEM((tok_dev, STEP), jnp.int32),
            pltpu.VMEM((rows, HEAD), jnp.float32),
            pltpu.VMEM((rows, HEAD), jnp.float32),
            pltpu.VMEM((rows, HEAD), jnp.float32),
        ],
        compiler_params=pltpu.CompilerParams(vmem_limit_bytes=62 << 20),
        name="attend",
    )(seg_lengths, cache_age, row_table, queries, window, bank)


MESH = pl.DeviceIdType.MESH


def place_of(group, head):
    tok, tall, core = lax.div(group, 8), lax.rem(lax.div(group, 2), 4), lax.rem(group, 2)
    return (tall * 4 + lax.rem(tok + head, 4)) * 2 + core


def group_at(ep, head):
    tall, wide, core = lax.div(ep, 8), lax.rem(lax.div(ep, 2), 4), lax.rem(ep, 2)
    return lax.rem(wide + 4 - head, 4) * 8 + 2 * tall + core


def owner_of(group, block):
    tok = lax.div(group, 8)
    return tok, lax.rem(group, 8) * 4 + block


def exchange_kernel(
    qkv_ref, cache_ref, slots_ref, query_ref, window_ref, bank_ref,
    stage_q, stage_kv, stage_slots, load_sems, key_send, key_recv, query_send, query_recv, pass_send, pass_recv, own_sem, line_send, line_recv,
    plane_send, plane_recv, pair_send, pair_recv,
):
    tok, ep = lax.axis_index("tok"), lax.axis_index("ep")
    tok_dev = qkv_ref.shape[0]
    q_width = QPG * HEAD
    number = tok * 32 + ep
    group, block = lax.div(number, 4), lax.rem(number, 4)
    mine = group_at(ep, tok)
    reach = SEG_MOST // (4 * tok_dev)
    span = 4 * tok_dev

    def column(head):
        return head * (q_width + 2 * HEAD)

    def remote(source, place, send_sem, recv_sem, device):
        return pltpu.make_async_remote_copy(
            src_ref=source, dst_ref=place, send_sem=send_sem, recv_sem=recv_sem, device_id=device, device_id_type=MESH
        )

    def load(turn, keys):
        head = lax.rem(tok + turn, 4)
        if keys:
            source = qkv_ref.at[:, pl.ds(pl.multiple_of(column(head) + q_width, HEAD), 2 * HEAD)]
            return pltpu.make_async_copy(source, stage_kv.at[turn], load_sems.at[turn])
        source = qkv_ref.at[:, pl.ds(pl.multiple_of(column(head), HEAD), q_width)]
        return pltpu.make_async_copy(source, stage_q.at[turn], load_sems.at[4 + turn])

    for keys in (True, False):
        for turn in range(4):
            load(turn, keys).start()

    def key_copy(turn):
        head = lax.rem(tok + turn, 4)
        place = window_ref.at[pl.ds(pl.multiple_of(reach * span + block * tok_dev, tok_dev), tok_dev)]
        return stage_kv.at[turn], place, key_send.at[turn], key_recv, (head, place_of(group, head))

    def query_copy(turn):
        head = lax.rem(tok + turn, 4)
        return stage_q.at[turn], query_ref.at[block], query_send.at[turn], query_recv, (head, place_of(group, head))

    def spans(index):
        return window_ref.at[pl.ds(pl.multiple_of(index * span, span), span)]

    def pass_copy(turn):
        device = (tok, place_of(lax.rem(mine + 2 * turn, 32), tok))
        return spans(reach), spans(reach - 2 * turn), pass_send.at[turn - 1], pass_recv.at[turn - 1], device

    def cross_copy(turn):
        device = (tok, at(tall, wide, 1 - core))
        return spans(6 - 2 * turn - 2 * core), spans(5 - 2 * turn), pass_send.at[turn + 1], pass_recv.at[turn + 1], device

    held, told = cache_ref.shape[0], stage_slots.shape[0]
    piece = held + told
    cut = piece // 32 * 16
    tall, wide, core = lax.div(ep, 8), lax.rem(lax.div(ep, 2), 4), lax.rem(ep, 2)

    def at(y, x, c):
        return (lax.rem(y, 4) * 4 + lax.rem(x, 4)) * 2 + c

    def part(y, x, c, start, size):
        return bank_ref.at[pl.ds(pl.multiple_of(at(y, x, c) * piece + start, 16), size)]

    lane = lax.broadcasted_iota(jnp.int32, stage_slots.shape, 1)
    listed = jnp.zeros(stage_slots.shape, jnp.float32)
    for page in range(slots_ref.shape[0]):
        listed = jnp.where(lane == page, slots_ref[page].astype(jnp.float32), listed)
    stage_slots[...] = listed.astype(jnp.bfloat16)
    own_cache = pltpu.make_async_copy(cache_ref, part(tall, wide, core, 0, held), own_sem.at[0])
    own_slots = pltpu.make_async_copy(stage_slots, part(tall, wide, core, held, told), own_sem.at[1])
    own_cache.start()
    own_slots.start()

    def line_copies():
        for turn in range(1, 4):
            first = part(tall, wide, core, 0, cut)
            yield remote(first, first, line_send, line_recv, (tok, at(tall, wide + turn, core)))
            rest = part(tall, wide, core, cut, piece - cut)
            yield remote(rest, rest, line_send, line_recv, (tok, at(tall + turn, wide, core)))

    def plane_copies():
        for turn in range(1, 4):
            for along in range(4):
                first = part(tall, wide + along, core, 0, cut)
                yield remote(first, first, plane_send, plane_recv, (tok, at(tall + turn, wide, core)))
                rest = part(tall + along, wide, core, cut, piece - cut)
                yield remote(rest, rest, plane_send, plane_recv, (tok, at(tall, wide + turn, core)))

    def pair_copies():
        for y in range(4):
            for x in range(4):
                whole = part(y, x, core, 0, piece)
                yield remote(whole, whole, pair_send, pair_recv, (tok, at(tall, wide, 1 - core)))

    def settle(rows, sem):
        pltpu.make_async_copy(bank_ref.at[pl.ds(0, rows)], bank_ref.at[pl.ds(0, rows)], sem).wait()

    barrier = pltpu.get_barrier_semaphore()
    at_home = place_of(group, tok) == ep
    for turn in range(1, 4):
        for partner in (at(tall, wide + turn, core), at(tall + turn, wide, core)):
            pl.semaphore_signal(barrier, inc=1, device_id=(tok, partner), device_id_type=MESH)
    pl.semaphore_signal(barrier, inc=1, device_id=(tok, at(tall, wide, 1 - core)), device_id_type=MESH)
    for turn in range(4):
        theirs = owner_of(mine, turn)

        @pl.when(jnp.logical_not((theirs[0] == tok) & (theirs[1] == ep)))
        def _():
            pl.semaphore_signal(barrier, inc=1, device_id=theirs, device_id_type=MESH)

    for turn in range(1, 3):
        pl.semaphore_signal(
            barrier, inc=1, device_id=(tok, place_of(lax.rem(mine + 32 - 2 * turn, 32), tok)), device_id_type=MESH
        )
    pl.semaphore_wait(barrier, 13 - jnp.where(at_home, 1, 0))

    def send_each(copy, turns=range(4)):
        for turn in turns:
            source, place, send_sem, recv_sem, device = copy(turn)
            load(turn, copy is key_copy).wait()
            if turn == 0:

                @pl.when(at_home)
                def _():
                    pltpu.make_async_copy(source, place, recv_sem).start()

                @pl.when(jnp.logical_not(at_home))
                def _():
                    remote(source, place, send_sem, recv_sem, device).start()
            else:
                remote(source, place, send_sem, recv_sem, device).start()

    own = window_ref.at[pl.ds(reach * span, span)]
    send_each(key_copy)
    own_cache.wait()
    own_slots.wait()
    for line_copy in line_copies():
        line_copy.start()
    pltpu.make_async_copy(own, own, key_recv).wait()
    for turn in range(1, 3):
        remote(*pass_copy(turn)).start()
    settle(3 * piece, line_recv)
    for plane_copy in plane_copies():
        plane_copy.start()
    send_each(query_copy)
    settle(12 * piece, plane_recv)
    for pair_copy in pair_copies():
        pair_copy.start()
    for turn in range(1, 3):
        remote(*pass_copy(turn)).wait()
    for turn in range(1, 3):
        remote(*cross_copy(turn)).start()
    for turn in range(1, 3):
        remote(*cross_copy(turn)).wait()
    pltpu.make_async_copy(query_ref, query_ref, query_recv).wait()
    for copy in (key_copy, query_copy):
        for turn in range(4):
            if turn == 0:

                @pl.when(jnp.logical_not(at_home))
                def _():
                    remote(*copy(turn)).wait_send()
            else:
                remote(*copy(turn)).wait_send()
    settle(16 * piece, pair_recv)
    settle(3 * piece, line_send)
    settle(12 * piece, plane_send)
    settle(16 * piece, pair_send)


def exchange(qkv, cached, slots):
    tok_dev = qkv.shape[0]
    reach = SEG_MOST // (4 * tok_dev)
    kept = pl.BlockSpec(memory_space=pl.ANY)
    return pl.pallas_call(
        exchange_kernel,
        out_shape=(
            jax.ShapeDtypeStruct((4, tok_dev, QPG * HEAD), jnp.bfloat16),
            jax.ShapeDtypeStruct(((reach + 1) * 4 * tok_dev, 2 * HEAD), jnp.bfloat16),
            jax.ShapeDtypeStruct((32 * (cached.shape[0] + META_ROWS), 2 * HEAD), jnp.bfloat16),
        ),
        in_specs=[kept] * 2 + [pl.BlockSpec(memory_space=pltpu.SMEM)],
        out_specs=(kept,) * 3,
        scratch_shapes=[
            pltpu.VMEM((4, tok_dev, QPG * HEAD), jnp.bfloat16),
            pltpu.VMEM((4, tok_dev, 2 * HEAD), jnp.bfloat16),
            pltpu.VMEM((META_ROWS, 2 * HEAD), jnp.bfloat16),
            pltpu.SemaphoreType.DMA((8,)),
            pltpu.SemaphoreType.DMA((4,)),
            pltpu.SemaphoreType.DMA,
            pltpu.SemaphoreType.DMA((4,)),
            pltpu.SemaphoreType.DMA,
            pltpu.SemaphoreType.DMA((4,)),
            pltpu.SemaphoreType.DMA((4,)),
            pltpu.SemaphoreType.DMA((2,)),
        ]
        + [pltpu.SemaphoreType.DMA] * 6,
        compiler_params=pltpu.CompilerParams(collective_id=1, has_side_effects=True),
        cost_estimate=pl.CostEstimate(flops=0, bytes_accessed=80 << 20, transcendentals=0),
        name="exchange",
    )(qkv, cached, slots)


CAP = 16
SIDE = 4
PLANE = 32
CUTS = ((0, 768), (768, 640), (1408, 640))


def position():
    tok, ep = lax.axis_index("tok"), lax.axis_index("ep")
    return tok, lax.div(ep, 8), lax.rem(lax.div(ep, 2), 4), lax.rem(ep, 2)


def moved(offsets, way):
    at = [lax.rem(own + size + way * off, size) for own, off, size in zip(position(), offsets, (4, 4, 4, 2))]
    return at[0], (at[1] * 4 + at[2]) * 2 + at[3]


def plane_offsets(cut, index, div, rem):
    core, outer, inner = div(index, 16), rem(div(index, 4), 4), rem(index, 4)
    return ((0, inner, outer, core), (inner, 0, outer, core), (outer, inner, 0, core))[cut]


def mixed_order(j):
    return lax.rem(j, 4) * 4 + lax.rem(lax.div(j, 4) + j, 4)


def line_offsets(cut, turn):
    return tuple(turn if axis == cut else 0 for axis in range(3)) + (0,)


def routed_kernel(
    attended_hbm, weight_hbm, resid_ref, gain_ref, table_ref, gate_up_hbm, down_hbm, out_ref,
    attended_ref, weight_ref, projected, heads, mixed_ref,
    line0, line1, line2, stage0, stage1, stage2, came0, came1, came2, back0, back1, back2,
    inbox0, inbox1, inbox2, sum0, sum1, sum2,
    gate_up, down, tables, rank, share, pick, rows_in,
    weight_sems, table_sems, line_send, line_recv, out_send, near_recv, far_recv, home_send, home_recv,
    part_send, part_recv, head_send, head_recv,
):
    lines, stages, cames, backs = (line0, line1, line2), (stage0, stage1, stage2), (came0, came1, came2), (back0, back1, back2)
    inboxes, sums = (inbox0, inbox1, inbox2), (sum0, sum1, sum2)
    tokens = resid_ref.shape[0]
    width = down.shape[0]
    devices = SIDE * PLANE
    message = SIDE * CAP
    load_attended = pltpu.make_async_copy(attended_hbm, attended_ref, weight_sems.at[2])
    load_weight = pltpu.make_async_copy(weight_hbm, weight_ref, weight_sems.at[3])
    load_attended.start()
    load_weight.start()
    load_gate_up = pltpu.make_async_copy(gate_up_hbm.at[0], gate_up, weight_sems.at[0])
    load_down = pltpu.make_async_copy(down_hbm.at[0], down, weight_sems.at[1])
    barrier = pltpu.get_barrier_semaphore()

    def greet(step, ignored):
        offsets = (lax.div(step, 32), lax.rem(lax.div(step, 8), 4), lax.rem(lax.div(step, 2), 4), lax.rem(step, 2))
        pl.semaphore_signal(barrier, inc=1, device_id=moved(offsets, 1), device_id_type=MESH)
        return ignored

    lax.fori_loop(1, devices, greet, 0)
    for cut in range(3):
        tables[cut, 0] = table_ref[...]
    tok, ep = lax.axis_index("tok"), lax.axis_index("ep")
    mine = group_at(ep, tok)
    home = [owner_of(mine, turn) for turn in range(4)]
    is_own = [(place[0] == tok) & (place[1] == ep) for place in home]

    def project(turn):
        projected[turn] = jnp.dot(
            attended_ref[turn], weight_ref[...], preferred_element_type=jnp.float32
        ).astype(jnp.bfloat16)

    load_attended.wait()
    load_weight.wait()
    load_gate_up.start()
    load_down.start()
    project(0)
    pl.semaphore_wait(barrier, devices - 1)

    def remote(source, place, send_sem, recv_sem, device):
        return pltpu.make_async_remote_copy(
            src_ref=source, dst_ref=place, send_sem=send_sem, recv_sem=recv_sem, device_id=device, device_id_type=MESH
        )

    def rows_of(ref, start, size):
        return ref.at[pl.ds(pl.multiple_of(start, CAP), size)]

    def settle(ref, size, sem):
        pltpu.make_async_copy(ref.at[pl.ds(0, size)], ref.at[pl.ds(0, size)], sem).wait()

    for cut in range(3):
        for turn in range(1, SIDE):
            remote(
                table_ref, tables.at[cut, turn], table_sems.at[0], table_sems.at[1], moved(line_offsets(cut, turn), 1)
            ).start()
    def head_copy(turn):
        return remote(projected.at[turn], heads.at[tok], head_send.at[turn], head_recv, home[turn])

    for turn in (0, 2, 1, 3):
        if turn:
            project(turn)

        @pl.when(is_own[turn])
        def _():
            pltpu.make_async_copy(projected.at[turn], heads.at[tok], head_recv).start()

        @pl.when(jnp.logical_not(is_own[turn]))
        def _():
            head_copy(turn).start()

    pltpu.make_async_copy(tables.at[:, pl.ds(0, 3)], tables.at[:, pl.ds(0, 3)], table_sems.at[1]).wait()
    before = (
        lax.broadcasted_iota(jnp.int32, (tokens, tokens), 0) < lax.broadcasted_iota(jnp.int32, (tokens, tokens), 1)
    ).astype(jnp.bfloat16)
    index = lax.broadcasted_iota(jnp.int32, (PLANE, tokens), 0)
    shift = {16: 4, 4: 2}
    top = table_ref.shape[0] // 2
    for cut in range(3):
        offsets = plane_offsets(cut, index, lambda v, d: v >> shift[d], lambda v, d: v & (d - 1))
        z, y, x, c = [(own + off) & (size - 1) for own, off, size in zip(position(), offsets, (4, 4, 4, 2))]
        expert = (z * 32 + y * 8 + x * 2 + c).astype(jnp.float32)
        for turn in range(SIDE):
            probs = tables[cut, turn, top:, :]
            shares = probs / jnp.sum(probs, axis=0, keepdims=True)
            named = jnp.zeros((PLANE, tokens), jnp.float32)
            owed = jnp.zeros((PLANE, tokens), jnp.float32)
            for k in range(top):
                match = expert == tables[cut, turn, k : k + 1, :]
                named = jnp.where(match, 1.0, named)
                owed = jnp.where(match, shares[k : k + 1, :], owed)
            earlier = jnp.dot(named.astype(jnp.bfloat16), before, preferred_element_type=jnp.float32)
            at = (cut * SIDE + turn) * PLANE
            rank[at : at + PLANE, :] = jnp.where(named > 0.0, earlier, -1.0)
            share[at : at + PLANE, :] = owed

    pltpu.make_async_copy(heads, heads, head_recv).wait()
    added = resid_ref[...].astype(jnp.float32)
    for head in range(4):
        added = added + heads[head].astype(jnp.float32)
    mixed_ref[...] = added.astype(jnp.bfloat16)
    wide = mixed_ref[...].astype(jnp.float32)
    level = lax.rsqrt(jnp.mean(wide * wide, axis=-1, keepdims=True) + NORM_EPS)
    for cut, (start, size) in enumerate(CUTS):
        part = mixed_ref[:, start : start + size].astype(jnp.float32)
        lines[cut][:tokens] = (part * level * gain_ref[:, start : start + size]).astype(jnp.bfloat16)
    for turn in (1, 3, 2):
        for cut in range(3):
            remote(
                rows_of(lines[cut], 0, tokens), rows_of(lines[cut], turn * tokens, tokens),
                line_send.at[cut], line_recv.at[cut], moved(line_offsets(cut, turn), 1),
            ).start()

    slot = lax.broadcasted_iota(jnp.int32, (CAP, tokens), 0).astype(jnp.float32)

    def choose(cut, core, turn, weighted):
        for j in range(16):
            at = (cut * SIDE + turn) * PLANE + core * 16 + j
            chosen = share[pl.ds(at, 1), :] if weighted else 1.0
            pick[j * CAP : (j + 1) * CAP, :] = jnp.where(rank[pl.ds(at, 1), :] == slot, chosen, 0.0).astype(jnp.bfloat16)

    def send(cut, i, recv_sem):
        source, place = rows_of(stages[cut], i * message, message), rows_of(cames[cut], i * message, message)
        offsets = plane_offsets(cut, i, lax.div, lax.rem)

        @pl.when(i == 0)
        def _():
            pltpu.make_async_copy(source, place, recv_sem).start()

        @pl.when(i > 0)
        def _():
            remote(source, place, out_send.at[cut], recv_sem, moved(offsets, 1)).start()

    def fill(cut, core):
        def one_shard(turn, ignored):
            choose(cut, core, turn, False)
            found = jnp.dot(
                pick[...], rows_of(lines[cut], turn * tokens, tokens)[...], preferred_element_type=jnp.float32
            ).astype(jnp.bfloat16)
            for j in range(16):
                rows_of(stages[cut], (core * 16 + j) * message + turn * CAP, CAP)[...] = found[j * CAP : (j + 1) * CAP]
            return ignored

        lax.fori_loop(0, SIDE, one_shard, 0)

    def dispatch(core, ignored):
        for cut in range(3):
            fill(cut, core)

        def send_all(order, inner):
            j = mixed_order(order)
            chunk = core * 4 + lax.div(j, 4)
            send(2, core * 16 + j, far_recv.at[core])
            send(0, core * 16 + j, near_recv.at[0, chunk])
            send(1, core * 16 + j, near_recv.at[1, chunk])
            return inner

        return lax.fori_loop(0, 16, send_all, ignored)

    for cut in range(3):
        settle(lines[cut], 3 * tokens, line_recv.at[cut])
        settle(lines[cut], 3 * tokens, line_send.at[cut])
    lax.fori_loop(0, 2, dispatch, 0)
    load_gate_up.wait()
    load_down.wait()
    block = SIDE * message

    def slab1(chunk, j):
        return rows_of(came1, chunk * block + (j % 4) * message + (j // 4) * CAP, CAP)

    def slab2(chunk, j):
        core, wide = lax.div(chunk, 4), lax.rem(chunk, 4)
        return rows_of(came2, (core * 16 + (j % 4) * 4 + j // 4) * message + wide * CAP, CAP)

    def give(cut, i):
        source, place = rows_of(cames[cut], i * message, message), rows_of(backs[cut], i * message, message)
        offsets = plane_offsets(cut, i, lax.div, lax.rem)
        recv_sem = home_recv.at[cut, lax.div(i, 16)]

        @pl.when(i == 0)
        def _():
            pltpu.make_async_copy(source, place, recv_sem).start()

        @pl.when(i > 0)
        def _():
            remote(source, place, home_send.at[cut], recv_sem, moved(offsets, -1)).start()

    def work(chunk, ignored):
        @pl.when(lax.rem(chunk, 4) == 0)
        def _():
            settle(came2, 16 * message, far_recv.at[lax.div(chunk, 4)])

        settle(came0, block, near_recv.at[0, chunk])
        settle(came1, block, near_recv.at[1, chunk])
        rows_in[:, 0:768] = rows_of(came0, chunk * block, block)[...]
        for j in range(16):
            rows_in[j * CAP : (j + 1) * CAP, 768:1408] = slab1(chunk, j)[...]
            rows_in[j * CAP : (j + 1) * CAP, 1408:2048] = slab2(chunk, j)[...]
        gate = jnp.dot(rows_in[...], gate_up[:, :width], preferred_element_type=jnp.float32)
        up = jnp.dot(rows_in[...], gate_up[:, width:], preferred_element_type=jnp.float32)
        hidden = (gate * jax.nn.sigmoid(gate) * up).astype(jnp.bfloat16)
        made = jnp.dot(hidden, down[...], preferred_element_type=jnp.float32).astype(jnp.bfloat16)
        rows_of(came0, chunk * block, block)[...] = made[:, 0:768]
        for j in range(16):
            slab1(chunk, j)[...] = made[j * CAP : (j + 1) * CAP, 768:1408]
            slab2(chunk, j)[...] = made[j * CAP : (j + 1) * CAP, 1408:2048]

        @pl.when(lax.rem(chunk, 4) == 3)
        def _():
            def give_all(order, inner):
                for cut in (2, 0, 1):
                    give(cut, lax.div(chunk, 4) * 16 + mixed_order(order))
                return inner

            lax.fori_loop(0, 16, give_all, 0)

        return ignored

    lax.fori_loop(0, 8, work, 0)

    for cut in range(3):
        sums[cut][...] = jnp.zeros_like(sums[cut])

    def combine(core, ignored):
        for cut in range(3):
            settle(backs[cut], 16 * message, home_recv.at[cut, core])

            def one_shard(turn, inner):
                choose(cut, core, turn, True)
                found = jnp.concatenate(
                    [rows_of(backs[cut], (core * 16 + j) * message + turn * CAP, CAP)[...] for j in range(16)], axis=0
                )
                total = rows_of(sums[cut], turn * tokens, tokens)
                total[...] += lax.dot_general(
                    pick[...], found, (((0,), (0,)), ((), ())), preferred_element_type=jnp.float32
                )
                return inner

            lax.fori_loop(0, SIDE, one_shard, 0)

            @pl.when(core == 1)
            def _():
                lines[cut][...] = sums[cut][...].astype(jnp.bfloat16)
                for turn in range(1, SIDE):
                    remote(
                        rows_of(lines[cut], turn * tokens, tokens), rows_of(inboxes[cut], turn * tokens, tokens),
                        part_send.at[cut], part_recv.at[cut], moved(line_offsets(cut, turn), -1),
                    ).start()

        return ignored

    lax.fori_loop(0, 2, combine, 0)
    for cut, (start, size) in enumerate(CUTS):
        settle(inboxes[cut], 3 * tokens, part_recv.at[cut])
        total = mixed_ref[:, start : start + size].astype(jnp.float32) + sums[cut][:tokens]
        for turn in range(1, SIDE):
            total = total + inboxes[cut][turn * tokens : (turn + 1) * tokens].astype(jnp.float32)
        out_ref[:, start : start + size] = total.astype(jnp.bfloat16)
    pltpu.make_async_copy(tables.at[:, pl.ds(0, 3)], tables.at[:, pl.ds(0, 3)], table_sems.at[0]).wait()
    for cut in range(3):
        settle(stages[cut], (PLANE - 1) * message, out_send.at[cut])
        settle(stages[cut], (PLANE - 1) * message, home_send.at[cut])
        settle(lines[cut], 3 * tokens, part_send.at[cut])
    for turn in range(4):

        @pl.when(jnp.logical_not(is_own[turn]))
        def _():
            head_copy(turn).wait_send()


def routed_experts(attended, weight, resid, gain, routes, probs, gate_up, down):
    tokens, width = resid.shape
    vmem = pl.BlockSpec(memory_space=pltpu.VMEM)
    kept = pl.BlockSpec(memory_space=pl.ANY)
    slots = SIDE * PLANE * CAP
    flops = 2 * slots * width * (down.shape[1] * 3 + 2 * tokens)
    table = jnp.concatenate([routes.T.astype(jnp.float32), probs.T], axis=0)

    def each(rows, kind):
        return [pltpu.VMEM((rows, size), kind) for start, size in CUTS]

    return pl.pallas_call(
        routed_kernel,
        out_shape=jax.ShapeDtypeStruct(resid.shape, jnp.bfloat16),
        in_specs=[kept] * 2 + [vmem] * 3 + [kept] * 2,
        out_specs=vmem,
        scratch_shapes=[
            pltpu.VMEM(attended.shape, jnp.bfloat16),
            pltpu.VMEM(weight.shape, jnp.bfloat16),
            pltpu.VMEM((4, tokens, width), jnp.bfloat16),
            pltpu.VMEM((4, tokens, width), jnp.bfloat16),
            pltpu.VMEM((tokens, width), jnp.bfloat16),
        ]
        + each(SIDE * tokens, jnp.bfloat16)
        + each(slots, jnp.bfloat16)
        + each(slots, jnp.bfloat16)
        + each(slots, jnp.bfloat16)
        + each(SIDE * tokens, jnp.bfloat16)
        + each(SIDE * tokens, jnp.float32)
        + [
            pltpu.VMEM(gate_up.shape[1:], jnp.bfloat16),
            pltpu.VMEM(down.shape[1:], jnp.bfloat16),
            pltpu.VMEM((3, SIDE, 2 * routes.shape[1], tokens), jnp.float32),
            pltpu.VMEM((3 * SIDE * PLANE, tokens), jnp.float32),
            pltpu.VMEM((3 * SIDE * PLANE, tokens), jnp.float32),
            pltpu.VMEM((16 * CAP, tokens), jnp.bfloat16),
            pltpu.VMEM((16 * CAP, width), jnp.bfloat16),
            pltpu.SemaphoreType.DMA((4,)),
            pltpu.SemaphoreType.DMA((2,)),
            pltpu.SemaphoreType.DMA((3,)),
            pltpu.SemaphoreType.DMA((3,)),
            pltpu.SemaphoreType.DMA((3,)),
            pltpu.SemaphoreType.DMA((2, 8)),
            pltpu.SemaphoreType.DMA((2,)),
            pltpu.SemaphoreType.DMA((3,)),
            pltpu.SemaphoreType.DMA((3, 2)),
            pltpu.SemaphoreType.DMA((3,)),
            pltpu.SemaphoreType.DMA((3,)),
            pltpu.SemaphoreType.DMA((4,)),
            pltpu.SemaphoreType.DMA,
        ],
        compiler_params=pltpu.CompilerParams(collective_id=0, has_side_effects=True, vmem_limit_bytes=62 << 20),
        cost_estimate=pl.CostEstimate(flops=flops, bytes_accessed=6 * slots * width * 2, transcendentals=0),
        name="routed_experts",
    )(attended, weight, resid, gain[None, :], table, gate_up, down)


def on_device(
    resid,
    qkv,
    cache_kv,
    page_slot,
    seg_lengths,
    cache_age,
    w_out,
    norm_gain,
    routes,
    route_probs,
    w_gate_up,
    w_down,
):
    ep_count = lax.axis_size("ep")
    tok_dev = resid.shape[0]
    seg_count = seg_lengths.shape[0]
    page_count = cache_kv.shape[0]
    bank_rows = page_count * PAGE + META_ROWS
    queries, window, bank = exchange(qkv, cache_kv.reshape(page_count * PAGE, 2 * HEAD), page_slot)
    held = bank.reshape(ep_count, bank_rows, 2 * HEAD)[:, bank_rows - 1, :page_count].astype(jnp.int32)
    slot_row = (
        jnp.arange(ep_count, dtype=jnp.int32)[:, None] * bank_rows
        + jnp.arange(page_count, dtype=jnp.int32)[None, :] * PAGE
    )
    page_match = held.reshape(-1)[None, :] == jnp.arange(seg_count * SEG_PAGES, dtype=jnp.int32)[:, None]
    row_table = jnp.sum(jnp.where(page_match, slot_row.reshape(-1)[None, :], 0), axis=1).astype(jnp.int32)
    attended = attention(seg_lengths, cache_age, row_table, queries, window, bank, seg_count, SEG_MOST)
    return routed_experts(attended, w_out, resid, norm_gain, routes, route_probs, w_gate_up, w_down)


def solution(mesh):
    placed = (
        P(("tok", "ep"), None),
        P(("tok", "ep"), None),
        P("ep", "tok", None, None),
        P("ep"),
        P(),
        P(),
        P("tok", None),
        P(),
        P(("tok", "ep"), None),
        P(("tok", "ep"), None),
        P(("tok", "ep"), None, None),
        P(("tok", "ep"), None, None),
    )
    return jax.shard_map(
        on_device, mesh=mesh, in_specs=placed, out_specs=P(("tok", "ep"), None), check_vma=False
    )
```
